512 devices in a mesh: tile: 128 (over z_lo, y, x, core), layer: 4 (over z_hi).
Axes of the slice: x: 4, y: 8, z: 8 (z_hi: 4, z_lo: 2; z = z_hi * 2 + z_lo), core: 2. Of those that a mesh axis runs over, the one named last changes fastest.
Arguments:
- rand_vectors: bfloat16 [4, 16, 1572864], P(None, None, ('tile', 'layer')), may hold values from -4 to 4
- onsite: bfloat16 [12288, 128, 128], P(('tile', 'layer')), as said below
- down_hop: bfloat16 [12288, 128, 128], P(('tile', 'layer')), may hold values from -0.1875 to 0.1875
- right_hop: bfloat16 [12288, 128, 128], P(('tile', 'layer')), may hold values from -0.1875 to 0.1875
- pattern: int32 [12288, 2], P(('tile', 'layer')), may hold values 0 or 1
- pairing: float32 [1572864], P(('tile', 'layer')), may hold values from 0.1 to 1
- link_rows: int32 [65536, 8], P(('tile', 'layer')), may hold values from 0 to 3071
- link_target: int32 [65536, 8], P(('tile', 'layer')), may hold values from 0 to 3071
- link_weight: bfloat16 [65536, 8], P(('tile', 'layer')), may hold values from -3 to 3
- link_count: int32 [65536], P(('tile', 'layer')), may hold values from 0 to 8, as said below
Outputs:
- cheb_one: float32 [4, 16, 1572864], P(None, None, ('tile', 'layer'))
- cheb_two: float32 [4, 16, 1572864], P(None, None, ('tile', 'layer'))
- moments: float32 [3, 4, 1572864], P(None, None, ('tile', 'layer'))
The draws below stay inside these ranges and needn't reach their ends.
Inputs may be any that keep to these rules, and one draw needn't show every extreme that they name: `onsite`: every tile is symmetric. `link_rows`: a local site of the sending device. `link_target`: a local site of the receiving device. `link_count`: the number of used slots from one source tile row index to one receiving device; loads differ strongly between receiving tile row indices.
All inputs are finite; a program needn't handle non-finite values. No bound on the sum of `pattern` on one device may be relied on, other than what follows from the above.
Results may differ from the reference program's by a relative error of at most 0.0025.
Values may be sent and summed in bfloat16 or wider, within the bound.
No kernel may reach another device: no remote copies, remote signals or barrier semaphores. Data moves between devices by JAX's collectives and lax.ppermute only.
A program may use at most 64 MiB of HBM per device.

```python
import math
import jax
import jax.numpy as jnp
from jax import lax

COMP = 4
VECS = 16
TILE = 128
TR = 4
TC = 6
CAP = 8
SD = 3072
SITES = 1572864
TILES = 12288
LINKS = 65536
N_TILE = 128
N_LAYER = 4


def draw_onsite(key, part):
    base = jax.random.normal(key, (TILES, TILE, TILE), jnp.float32)
    base = base * (1.0 / math.sqrt(TILE))
    return ((base + jnp.swapaxes(base, 1, 2)) * 0.5).astype(jnp.bfloat16)


def draw_link_count(key, part):
    first_key, second_key, third_key = jax.random.split(key, 3)
    tile_total = math.isqrt(LINKS // 4)
    counts = jax.random.randint(first_key, (LINKS,), 0, CAP + 1, dtype=jnp.int32)
    keeper = jax.random.randint(second_key, (LINKS,), 0, 4, dtype=jnp.int32)
    counts = jnp.where(keeper > 0, counts, 0)
    hottest = jax.random.randint(third_key, (), 0, tile_total, dtype=jnp.int32)
    receiver_tile = jnp.arange(LINKS, dtype=jnp.int32) // (4 * tile_total)
    counts = jnp.where(receiver_tile == hottest, CAP, counts)
    return counts.astype(jnp.int32)


def with_ends(drawn, own_key, low, high):
    longest = drawn.shape.index(max(drawn.shape))
    spots = []
    for shift in (0, 1):
        where = [jax.random.randint(jax.random.fold_in(own_key, axis), (), 0, length) for axis, length in enumerate(drawn.shape)]
        where[longest] = (where[longest] + shift) % drawn.shape[longest]
        spots.append(tuple(where))
    return drawn.at[spots[0]].set(low).at[spots[1]].set(high)


def steps_of(rng, shape, shards, smallest, largest):
    level = 1.0
    for position, shards_of in shards:
        draws = jax.random.uniform(jax.random.fold_in(jax.random.fold_in(rng, 6), position), (shards_of,), jnp.float32, smallest / len(shards), largest / len(shards))
        level = level * jnp.repeat(jnp.exp(draws), shape[position] // shards_of).reshape((-1,) + (1,) * (len(shape) - 1 - position))
    return level


def gaussian(own_key, extent, deviation, limit, shards=(), held_as=jnp.bfloat16):
    result = deviation * jax.random.normal(own_key, extent, jnp.float32)
    if shards:
        result = result * steps_of(own_key, extent, shards, -0.22, 0.18)
    return jnp.clip(result, -limit, limit).astype(held_as)


def setup_inputs(seed: int = 0) -> dict:
    arg_keys = jax.random.split(jax.random.key(seed), 11)
    rand_vectors = gaussian(arg_keys[0], (COMP, VECS, SITES), 1.0, 4.0, ((2, 512),))
    onsite = draw_onsite(jax.random.fold_in(arg_keys[10], 71), 0)
    down_hop = gaussian(arg_keys[2], (TILES, TILE, TILE), (8 * TILE) ** -0.5, 0.1875, ((0, 512),))
    right_hop = gaussian(arg_keys[3], (TILES, TILE, TILE), (8 * TILE) ** -0.5, 0.1875, ((0, 512),))
    pattern = with_ends((jax.random.randint(arg_keys[4], (TILES, 2), 0, 4) < 3).astype(jnp.int32), jax.random.fold_in(arg_keys[4], 1), 0, 1)
    pairing = jnp.clip(jnp.exp(math.log(1.0) - 2.3025851 * jax.random.uniform(arg_keys[5], (SITES,), jnp.float32) ** steps_of(arg_keys[5], (SITES,), ((0, 512),), -0.2, 0.2)), 0.1, 1.0)
    link_rows = with_ends(jax.random.randint(arg_keys[6], (LINKS, CAP), 0, SD), jax.random.fold_in(arg_keys[6], 1), 0, SD - 1).astype(jnp.int32)
    link_target = with_ends(jax.random.randint(arg_keys[7], (LINKS, CAP), 0, SD), jax.random.fold_in(arg_keys[7], 1), 0, SD - 1).astype(jnp.int32)
    link_weight = gaussian(arg_keys[8], (LINKS, CAP), 0.5, 3.0, ((0, 512),))
    link_count = draw_link_count(jax.random.fold_in(arg_keys[10], 71), 0)
    return {"rand_vectors": rand_vectors, "onsite": onsite, "down_hop": down_hop, "right_hop": right_hop, "pattern": pattern, "pairing": pairing, "link_rows": link_rows, "link_target": link_target, "link_weight": link_weight, "link_count": link_count}


FORWARD_FORM = "kij,nkj->nki"
TRANSPOSED_FORM = "kji,nkj->nki"


def tile_rows(tiles, field_grid, einsum_form):
    def row_product(row_pair):
        block_tiles, field_row = row_pair
        return jnp.einsum(einsum_form, block_tiles.astype(jnp.float32), field_row.astype(jnp.float32))

    mapped = lax.map(row_product, (tiles, jnp.moveaxis(field_grid, 1, 0)))
    return jnp.moveaxis(mapped, 0, 1)


def layer_tiles(tiles, layer_index):
    sixfold = tiles.reshape(N_TILE, N_LAYER, TR, TC, TILE, TILE)[:, 2 * layer_index:2 * layer_index + 2]
    return sixfold.transpose(0, 2, 1, 3, 4, 5).reshape(N_TILE * TR, 2 * TC, TILE, TILE)


def layer_field(field, layer_index):
    field_rows = field.shape[0]
    sixfold = field.reshape(field_rows, N_TILE, N_LAYER, TR, TC, TILE)[:, :, 2 * layer_index:2 * layer_index + 2]
    return sixfold.transpose(0, 1, 3, 2, 4, 5).reshape(field_rows, N_TILE * TR, 2 * TC, TILE)


def intra_layer(field_b, self_tiles, down_mask, right_mask):
    field_rows = field_b.shape[0]
    pieces = []
    for layer_index in range(2):
        field_grid = layer_field(field_b, layer_index)
        onsite_grid = layer_tiles(self_tiles, layer_index)
        down_grid = layer_tiles(down_mask, layer_index)
        right_grid = layer_tiles(right_mask, layer_index)
        zero_row = jnp.zeros_like(field_grid[:, :1])
        zero_column = jnp.zeros_like(field_grid[:, :, :1])
        result_grid = tile_rows(onsite_grid, field_grid, FORWARD_FORM)
        result_grid = result_grid + tile_rows(down_grid, jnp.concatenate([field_grid[:, 1:], zero_row], axis=1), FORWARD_FORM)
        upward = tile_rows(down_grid, field_grid, TRANSPOSED_FORM)
        result_grid = result_grid + jnp.concatenate([jnp.zeros_like(upward[:, :1]), upward[:, :-1]], axis=1)
        result_grid = result_grid + tile_rows(right_grid, jnp.concatenate([field_grid[:, :, 1:], zero_column], axis=2), FORWARD_FORM)
        leftward = tile_rows(right_grid, field_grid, TRANSPOSED_FORM)
        result_grid = result_grid + jnp.concatenate([jnp.zeros_like(leftward[:, :, :1]), leftward[:, :, :-1]], axis=2)
        pieces.append(result_grid.reshape(field_rows, N_TILE, TR, 2, TC, TILE).transpose(0, 1, 3, 2, 4, 5))
    return jnp.concatenate(pieces, axis=2).reshape(field_rows, SITES)


def inter_layer(field_b, link_rows, link_target, link_weight, link_count):
    columns = field_b.T
    flipped = jnp.array([2, 3, 0, 1], dtype=jnp.int32)
    sent_rows = link_rows.reshape(N_TILE, N_LAYER, N_TILE, CAP)[:, flipped].transpose(2, 1, 0, 3)
    slot_live = jnp.arange(CAP, dtype=jnp.int32).reshape(1, 1, 1, CAP) < link_count.reshape(N_TILE, N_LAYER, N_TILE, 1)
    slot_weight = jnp.where(slot_live, link_weight.reshape(N_TILE, N_LAYER, N_TILE, CAP).astype(jnp.float32), 0.0).reshape(-1, 1)
    tile_index = jnp.arange(N_TILE, dtype=jnp.int32).reshape(N_TILE, 1, 1, 1)
    layer_index = jnp.arange(N_LAYER, dtype=jnp.int32).reshape(1, N_LAYER, 1, 1)
    source_tile = jnp.arange(N_TILE, dtype=jnp.int32).reshape(1, 1, N_TILE, 1)
    receiver = ((tile_index * N_LAYER + layer_index) * SD + link_target.reshape(N_TILE, N_LAYER, N_TILE, CAP)).astype(jnp.int32).reshape(-1)
    sender = ((source_tile * N_LAYER + (layer_index + 2) % N_LAYER) * SD + sent_rows).astype(jnp.int32).reshape(-1)
    forward = jnp.take(columns, sender, axis=0).astype(jnp.float32) * slot_weight
    backward = jnp.take(columns, receiver, axis=0).astype(jnp.float32) * slot_weight
    summed = jax.ops.segment_sum(forward, receiver, num_segments=SITES) + jax.ops.segment_sum(backward, sender, num_segments=SITES)
    return summed.T


def reference(rand_vectors, onsite, down_hop, right_hop, pattern, pairing, link_rows, link_target, link_weight, link_count):
    down_mask = down_hop * pattern[:, 0][:, None, None].astype(jnp.bfloat16)
    right_mask = right_hop * pattern[:, 1][:, None, None].astype(jnp.bfloat16)
    nambu_sign = jnp.array([1.0, 1.0, -1.0, -1.0], dtype=jnp.float32)[:, None, None]
    field_rows = COMP * VECS

    def apply_hop(field_b):
        flat_field = field_b.reshape(field_rows, SITES)
        summed = intra_layer(flat_field, onsite, down_mask, right_mask) + inter_layer(flat_field, link_rows, link_target, link_weight, link_count)
        return summed.reshape(COMP, VECS, SITES)

    initial = rand_vectors.astype(jnp.float32)
    cheb_one = nambu_sign * apply_hop(rand_vectors) + pairing * jnp.roll(initial, 2, axis=0)
    one_rounded = cheb_one.astype(jnp.bfloat16)
    cheb_two = 2.0 * (nambu_sign * apply_hop(one_rounded) + pairing * jnp.roll(cheb_one, 2, axis=0)) - initial
    moments = jnp.stack([jnp.mean(initial * initial, axis=1), jnp.mean(initial * cheb_one, axis=1), jnp.mean(initial * cheb_two, axis=1)])
    return cheb_one, cheb_two, moments
```

```python
import jax
import jax.numpy as jnp
from jax import lax
from jax.experimental import pallas as pl
from jax.experimental.pallas import tpu as pltpu
from jax.sharding import PartitionSpec as P

TILE = 128
TR = 4
TC = 6
ROWS = 64
SITES_DEV = TR * TC * TILE
PEERS = 128
CAP = 8
SLOTS = PEERS * CAP
SPAN = 256
HI = SITES_DEV // SPAN
F32 = jnp.float32
BF16 = jnp.bfloat16
NT = (((1,), (1,)), ((), ()))
NN = (((1,), (0,)), ((), ()))
VMEM_LIMIT = 56 * 1024 * 1024


def dot(a, b, dims=NN):
    return lax.dot_general(a, b, dims, preferred_element_type=F32)


def per_slot(table):
    spread = jnp.broadcast_to(table.astype(F32)[:, None, :], (PEERS, CAP, CAP)).reshape(SLOTS, CAP)
    own = lax.broadcasted_iota(jnp.int32, (SLOTS, CAP), 0) % CAP == lax.broadcasted_iota(
        jnp.int32, (SLOTS, CAP), 1
    )
    picked = jnp.where(own, spread, 0.0).astype(BF16)
    return dot(picked, jnp.ones((CAP, TILE), BF16))


def gather_into(x, hot_ref, high_ref, out_ref):
    chunk = 256
    lane = lax.broadcasted_iota(jnp.int32, (chunk, TILE), 1)
    half = (lane >= ROWS).astype(F32)
    pieces = []
    for q in range(HI // 2):
        pieces.append(
            jnp.concatenate(
                [x[:, 2 * q * SPAN : (2 * q + 1) * SPAN], x[:, (2 * q + 1) * SPAN : (2 * q + 2) * SPAN]],
                axis=0,
            )
        )
    for start in range(0, SLOTS, chunk):
        ends = []
        for end in range(2):
            hot = hot_ref[end * SLOTS + start : end * SLOTS + start + chunk, :]
            high = high_ref[end * SLOTS + start : end * SLOTS + start + chunk, :] - half
            total = jnp.zeros((chunk, TILE), F32)
            for q in range(HI // 2):
                total = jnp.where(high == 2.0 * q, dot(hot, pieces[q], NT), total)
            ends.append(total + pltpu.roll(total, ROWS, 1))
        out_ref[start : start + chunk, :] = jnp.where(lane < ROWS, ends[0], ends[1]).astype(BF16)


def prepare_kernel(x_ref, rows_ref, target_ref, weight_ref, count_ref, hot_ref, high_ref, out_ref):
    lane = lax.broadcasted_iota(jnp.int32, (SLOTS, SPAN), 1).astype(F32)
    live = lax.broadcasted_iota(jnp.int32, (PEERS, CAP), 1) < count_ref[...]
    weight = per_slot(jnp.where(live, weight_ref[...].astype(F32), 0.0))
    for end, table_ref in ((0, rows_ref), (1, target_ref)):
        table = table_ref[...]
        low = per_slot(table % SPAN)
        high_ref[end * SLOTS : (end + 1) * SLOTS, :] = per_slot(table // SPAN)
        low = jnp.concatenate([low, low], axis=1)
        value = 1.0 if end == 0 else jnp.concatenate([weight, weight], axis=1)
        hot_ref[end * SLOTS : (end + 1) * SLOTS, :] = jnp.where(lane == low, value, 0.0).astype(BF16)
    gather_into(x_ref[...], hot_ref, high_ref, out_ref)


def prepare(x, link_rows, link_target, link_weight, link_count):
    return pl.pallas_call(
        prepare_kernel,
        out_shape=(
            jax.ShapeDtypeStruct((2 * SLOTS, SPAN), BF16),
            jax.ShapeDtypeStruct((2 * SLOTS, TILE), F32),
            jax.ShapeDtypeStruct((SLOTS, 2 * ROWS), BF16),
        ),
        compiler_params=pltpu.CompilerParams(vmem_limit_bytes=VMEM_LIMIT),
        name="prepare",
    )(x, link_rows, link_target, link_weight, link_count.reshape(PEERS, 1))


def edges_kernel(pattern_ref, left_ref, x_ref, down_ref, right_ref, below_ref, side_ref):
    x = x_ref[...]
    for k in range(TC):
        tile = (TR - 1) * TC + k
        keep = pattern_ref[tile, 0].astype(F32)
        below_ref[:, k * TILE : (k + 1) * TILE] = keep * dot(
            x[:, tile * TILE : (tile + 1) * TILE], down_ref[k]
        )
    is_left = left_ref[0] == 1
    for r in range(TR):
        last = r * TC + TC - 1
        keep = pattern_ref[last, 1].astype(F32)
        product = keep * dot(x[:, last * TILE : (last + 1) * TILE], right_ref[r, 0])
        first = x[:, r * TC * TILE : (r * TC + 1) * TILE].astype(F32)
        side_ref[:, r * TILE : (r + 1) * TILE] = jnp.where(is_left, product, first)


def edges(pattern, left_flag, x, down_hop, right_hop):
    return pl.pallas_call(
        edges_kernel,
        grid=(1,),
        in_specs=[
            pl.BlockSpec(memory_space=pltpu.SMEM),
            pl.BlockSpec(memory_space=pltpu.SMEM),
            pl.BlockSpec((ROWS, SITES_DEV), lambda i: (0, 0)),
            pl.BlockSpec((TC, TILE, TILE), lambda i: (TR - 1, 0, 0)),
            pl.BlockSpec((TR, 1, TILE, TILE), lambda i: (0, TC - 1, 0, 0)),
        ],
        out_specs=(
            pl.BlockSpec((ROWS, TC * TILE), lambda i: (0, 0)),
            pl.BlockSpec((ROWS, TR * TILE), lambda i: (0, 0)),
        ),
        out_shape=(
            jax.ShapeDtypeStruct((ROWS, TC * TILE), F32),
            jax.ShapeDtypeStruct((ROWS, TR * TILE), F32),
        ),
        compiler_params=pltpu.CompilerParams(vmem_limit_bytes=VMEM_LIMIT),
        name="edges",
    )(pattern, left_flag, x, down_hop, right_hop.reshape(TR, TC, TILE, TILE))


def intra_kernel(
    pattern_ref, left_ref, x_ref, onsite_ref, down_ref, right_ref, above_ref, below_ref, side_ref, out_ref
):
    is_left = left_ref[0] == 1
    x = x_ref[...]

    def block(tile):
        return x[:, tile * TILE : (tile + 1) * TILE]

    def kept(tile, which, value):
        return jnp.where(pattern_ref[tile, which] == 1, value, jnp.zeros_like(value))

    for r in range(TR):
        for k in range(TC):
            tile = r * TC + k
            fields = [block(tile)]
            tiles = [onsite_ref[tile]]
            if r > 0:
                fields.append(kept(tile - TC, 0, block(tile - TC)))
                tiles.append(down_ref[tile - TC])
            if k > 0:
                fields.append(kept(tile - 1, 1, block(tile - 1)))
                tiles.append(right_ref[tile - 1])
            total = dot(jnp.concatenate(fields, axis=1), jnp.concatenate(tiles, axis=0))
            lower = block(tile + TC) if r < TR - 1 else below_ref[:, k * TILE : (k + 1) * TILE]
            if k < TC - 1:
                righter = block(tile + 1)
            else:
                edge = side_ref[:, r * TILE : (r + 1) * TILE]
                righter = jnp.where(is_left, edge, 0.0).astype(BF16)
            total = total + dot(
                jnp.concatenate([kept(tile, 0, lower), kept(tile, 1, righter)], axis=1),
                jnp.concatenate([down_ref[tile], right_ref[tile]], axis=1),
                NT,
            )
            if r == 0:
                total = total + above_ref[:, k * TILE : (k + 1) * TILE]
            if k == 0:
                edge = side_ref[:, r * TILE : (r + 1) * TILE]
                total = total + jnp.where(is_left, 0.0, edge)
            out_ref[:, tile * TILE : (tile + 1) * TILE] = total


def intra(pattern, left_flag, x, onsite, down_hop, right_hop, above, below, side):
    smem = pl.BlockSpec(memory_space=pltpu.SMEM)
    vmem = pl.BlockSpec(memory_space=pltpu.VMEM)
    return pl.pallas_call(
        intra_kernel,
        in_specs=[smem, smem] + [vmem] * 7,
        out_shape=jax.ShapeDtypeStruct((ROWS, SITES_DEV), F32),
        compiler_params=pltpu.CompilerParams(vmem_limit_bytes=VMEM_LIMIT),
        name="intra",
    )(pattern, left_flag, x, onsite, down_hop, right_hop, above, below, side)


def scatter_into(landed, hot_ref, high_ref, mask_ref, total_ref):
    turned = landed.astype(F32).T.astype(BF16)
    high_send = high_ref[0:SLOTS, :].T.astype(BF16)[:ROWS]
    high_recv = high_ref[SLOTS : 2 * SLOTS, :].T.astype(BF16)[:ROWS]
    zero = jnp.zeros((ROWS, SLOTS), BF16)
    for h in range(HI):
        mask_ref[h * ROWS : (h + 1) * ROWS, 0:SLOTS] = jnp.where(
            high_send == BF16(h), turned[ROWS:], zero
        )
        mask_ref[h * ROWS : (h + 1) * ROWS, SLOTS : 2 * SLOTS] = jnp.where(
            high_recv == BF16(h), turned[:ROWS], zero
        )
    group = 4
    for start in range(0, HI, group):
        total_ref[start * ROWS : (start + group) * ROWS, :] = dot(
            mask_ref[start * ROWS : (start + group) * ROWS, :], hot_ref[...]
        )


def signed(value):
    return jnp.where(lax.broadcasted_iota(jnp.int32, value.shape, 0) < ROWS // 2, value, -value)


def swapped(value):
    return jnp.concatenate([value[ROWS // 2 :], value[: ROWS // 2]], axis=0)


def vector_mean(value):
    comps = value.reshape(4, 16, value.shape[-1])
    return jnp.sum(comps, axis=1) * (1.0 / 16.0)


def first_kernel(
    v0_ref, landed_ref, hot_ref, high_ref, intra_ref, pairing_ref, one_ref, x_ref, mom_ref, out_ref, mask_ref, total_ref
):
    scatter_into(landed_ref[...], hot_ref, high_ref, mask_ref, total_ref)
    for h in range(HI):
        cols = slice(h * SPAN, (h + 1) * SPAN)
        hop = total_ref[h * ROWS : (h + 1) * ROWS, :] + intra_ref[:, cols]
        v0 = v0_ref[:, cols].astype(F32)
        one = signed(hop) + pairing_ref[:, cols] * swapped(v0)
        one_ref[:, cols] = one
        x_ref[:, cols] = one.astype(BF16)
        mom_ref[0:4, cols] = vector_mean(v0 * v0)
        mom_ref[4:8, cols] = vector_mean(v0 * one)
    gather_into(x_ref[...], hot_ref, high_ref, out_ref)


def first(v0, landed, hot, high, intra_part, pairing):
    return pl.pallas_call(
        first_kernel,
        out_shape=(
            jax.ShapeDtypeStruct((ROWS, SITES_DEV), F32),
            jax.ShapeDtypeStruct((ROWS, SITES_DEV), BF16),
            jax.ShapeDtypeStruct((8, SITES_DEV), F32),
            jax.ShapeDtypeStruct((SLOTS, 2 * ROWS), BF16),
        ),
        scratch_shapes=[pltpu.VMEM((HI * ROWS, 2 * SLOTS), BF16), pltpu.VMEM((HI * ROWS, SPAN), F32)],
        compiler_params=pltpu.CompilerParams(vmem_limit_bytes=VMEM_LIMIT),
        name="first",
    )(v0, landed, hot, high, intra_part, pairing)


def second_kernel(
    v0_ref, one_ref, landed_ref, hot_ref, high_ref, intra_ref, pairing_ref, mom_in_ref, two_ref, mom_ref, mask_ref, total_ref
):
    scatter_into(landed_ref[...], hot_ref, high_ref, mask_ref, total_ref)
    mom_ref[0:8, :] = mom_in_ref[...]
    for h in range(HI):
        cols = slice(h * SPAN, (h + 1) * SPAN)
        hop = total_ref[h * ROWS : (h + 1) * ROWS, :] + intra_ref[:, cols]
        v0 = v0_ref[:, cols].astype(F32)
        two = 2.0 * (signed(hop) + pairing_ref[:, cols] * swapped(one_ref[:, cols])) - v0
        two_ref[:, cols] = two
        mom_ref[8:12, cols] = vector_mean(v0 * two)


def second(v0, one, landed, hot, high, intra_part, pairing, mom):
    return pl.pallas_call(
        second_kernel,
        out_shape=(
            jax.ShapeDtypeStruct((ROWS, SITES_DEV), F32),
            jax.ShapeDtypeStruct((12, SITES_DEV), F32),
        ),
        scratch_shapes=[pltpu.VMEM((HI * ROWS, 2 * SLOTS), BF16), pltpu.VMEM((HI * ROWS, SPAN), F32)],
        compiler_params=pltpu.CompilerParams(vmem_limit_bytes=VMEM_LIMIT),
        name="second",
    )(v0, one, landed, hot, high, intra_part, pairing, mom)


def passed_along(value, axis, by):
    length = lax.axis_size(axis)
    pairs = [(i, i + by) for i in range(length) if 0 <= i + by < length]
    return lax.ppermute(value, axis, pairs)


def partner_2(value, axis, bit):
    return lax.ppermute(value, axis, [(i, i ^ 1 << bit) for i in range(lax.axis_size(axis))])


def exchange(payload):
    spread = lax.all_to_all(
        payload.reshape(PEERS, CAP, 2 * ROWS), "tile", split_axis=0, concat_axis=0, tiled=True
    )
    return partner_2(spread, "layer", 1).reshape(SLOTS, 2 * ROWS)


def shards(
    rand_vectors,
    onsite,
    down_hop,
    right_hop,
    pattern,
    pairing,
    link_rows,
    link_target,
    link_weight,
    link_count,
):
    v0 = rand_vectors.reshape(ROWS, SITES_DEV)
    pairing = pairing.reshape(1, SITES_DEV)
    left_flag = (1 - lax.axis_index("layer") % 2).astype(jnp.int32).reshape(1)

    def intra_of(x):
        below_part, side_part = edges(pattern, left_flag, x, down_hop, right_hop)
        above = passed_along(below_part, "tile", 1)
        below = passed_along(x[:, : TC * TILE], "tile", -1)
        side = partner_2(side_part, "layer", 0)
        return intra(pattern, left_flag, x, onsite, down_hop, right_hop, above, below, side)

    hot, high, payload = prepare(v0, link_rows, link_target, link_weight, link_count)
    landed = exchange(payload)
    one, x, mom, payload = first(v0, landed, hot, high, intra_of(v0), pairing)
    landed = exchange(payload)
    two, mom = second(v0, one, landed, hot, high, intra_of(x), pairing, mom)
    shape = rand_vectors.shape
    return one.reshape(shape), two.reshape(shape), mom.reshape(3, 4, SITES_DEV)


def solution(mesh):
    both = ("tile", "layer")
    in_specs = (
        P(None, None, both),
        P(both, None, None),
        P(both, None, None),
        P(both, None, None),
        P(both, None),
        P(both),
        P(both, None),
        P(both, None),
        P(both, None),
        P(both),
    )
    out_specs = (P(None, None, both), P(None, None, both), P(None, None, both))
    return jax.shard_map(shards, mesh=mesh, in_specs=in_specs, out_specs=out_specs, check_vma=False)
```

```python
import jax
import jax.numpy as jnp
from jax import lax
from jax.experimental import pallas as pl
from jax.experimental.pallas import tpu as pltpu
from jax.sharding import PartitionSpec as P

TILE = 128
TR = 4
TC = 6
ROWS = 64
SITES_DEV = TR * TC * TILE
PEERS = 128
CAP = 8
SLOTS = PEERS * CAP
SPAN = 256
HI = SITES_DEV // SPAN
F32 = jnp.float32
BF16 = jnp.bfloat16
NT = (((1,), (1,)), ((), ()))
NN = (((1,), (0,)), ((), ()))
VMEM_LIMIT = 56 * 1024 * 1024


def dot(a, b, dims=NN):
    return lax.dot_general(a, b, dims, preferred_element_type=F32)


COST = pl.CostEstimate(flops=1000000, bytes_accessed=100000, transcendentals=0)


def params():
    return pltpu.CompilerParams(vmem_limit_bytes=VMEM_LIMIT)


def per_slot(table):
    spread = jnp.broadcast_to(table[None], (PEERS, CAP, PEERS)).reshape(SLOTS, PEERS)
    own = lax.broadcasted_iota(jnp.int32, (SLOTS, PEERS), 0) // CAP == lax.broadcasted_iota(
        jnp.int32, (SLOTS, PEERS), 1
    )
    return dot(jnp.where(own, spread, 0.0).astype(BF16), jnp.ones((PEERS, TILE), BF16))


def build_tables(rows, target, weight, hot_ref, high_ref, weight_ref):
    lane = lax.broadcasted_iota(jnp.int32, (SLOTS, SPAN), 1).astype(F32)
    spread_weight = per_slot(weight)
    weight_ref[...] = spread_weight
    wide_weight = jnp.concatenate([spread_weight, spread_weight], axis=1)
    for end, table in ((0, rows), (1, target)):
        coarse = jnp.floor(table * (1.0 / SPAN))
        low = per_slot(table - coarse * SPAN)
        high_ref[end * SLOTS : (end + 1) * SLOTS, :] = per_slot(coarse)
        same = lane == jnp.concatenate([low, low], axis=1)
        hot_ref[2 * end * SLOTS : (2 * end + 1) * SLOTS, :] = jnp.where(same, 1.0, 0.0).astype(BF16)
        if end == 1:
            hot_ref[SLOTS : 2 * SLOTS, :] = jnp.where(same, wide_weight, 0.0).astype(BF16)


def gather_ends(terms, hot_ref, high_ref, start, chunk):
    lane = lax.broadcasted_iota(jnp.int32, (chunk, TILE), 1)
    half = (lane >= ROWS).astype(F32)
    ends = []
    for end in range(2):
        hot = hot_ref[2 * end * SLOTS + start : 2 * end * SLOTS + start + chunk, :]
        high = high_ref[end * SLOTS + start : end * SLOTS + start + chunk, :] - half
        total = jnp.zeros((chunk, TILE), F32)
        for q in range(HI // 2):
            found = sum(dot(hot, jnp.concatenate([t[2 * q], t[2 * q + 1]], axis=0), NT) for t in terms)
            total = jnp.where(high == 2.0 * q, found, total)
        ends.append(total + pltpu.roll(total, ROWS, 1))
    return jnp.where(lane < ROWS, ends[0], ends[1])


def as_payload(ends, weight):
    field = ends.astype(BF16)
    lane = lax.broadcasted_iota(jnp.int32, ends.shape, 1)
    return jnp.where(lane < ROWS, field.astype(F32), field.astype(F32) * weight).astype(BF16)


def split(value):
    high = value.astype(BF16)
    return high, (value - high.astype(F32)).astype(BF16)


CHUNK = 256


def prepare_kernel(x_ref, table_ref, hot_ref, high_ref, spread_ref, out_ref):
    build_tables(table_ref[0], table_ref[1], table_ref[2], hot_ref, high_ref, spread_ref)
    parts = [x_ref[:, h * SPAN : (h + 1) * SPAN] for h in range(HI)]
    for start in range(0, SLOTS, CHUNK):
        ends = gather_ends([parts], hot_ref, high_ref, start, CHUNK)
        out_ref[start : start + CHUNK, :] = as_payload(ends, spread_ref[start : start + CHUNK, :])


TABLE_SHAPES = (
    jax.ShapeDtypeStruct((3 * SLOTS, SPAN), BF16),
    jax.ShapeDtypeStruct((2 * SLOTS, TILE), F32),
    jax.ShapeDtypeStruct((SLOTS, TILE), F32),
)


def prepare(x, table):
    return pl.pallas_call(
        prepare_kernel,
        out_shape=TABLE_SHAPES + (jax.ShapeDtypeStruct((SLOTS, 2 * ROWS), BF16),),
        compiler_params=params(),
        cost_estimate=COST,
        name="prepare",
    )(x, table)


def tables_kernel(table_ref, hot_ref, high_ref, spread_ref):
    build_tables(table_ref[0], table_ref[1], table_ref[2], hot_ref, high_ref, spread_ref)


def tables_of(table):
    return pl.pallas_call(
        tables_kernel, out_shape=TABLE_SHAPES, compiler_params=params(),
        cost_estimate=COST, name="other_tables"
    )(table)


def write_edges(pattern_ref, left_ref, x_ref, down_ref, right_ref, down_base, top_ref, below_ref, side_ref):
    top_ref[...] = x_ref[:, : TC * TILE]
    for k in range(TC):
        tile = (TR - 1) * TC + k
        keep = pattern_ref[0, tile].astype(F32)
        below_ref[:, k * TILE : (k + 1) * TILE] = keep * dot(
            x_ref[:, tile * TILE : (tile + 1) * TILE], down_ref[down_base + k]
        )
    is_left = left_ref[0] == 1
    for r in range(TR):
        last = r * TC + TC - 1
        keep = pattern_ref[1, last].astype(F32)
        product = keep * dot(x_ref[:, last * TILE : (last + 1) * TILE], right_ref[r, 0])
        first_tile = x_ref[:, r * TC * TILE : (r * TC + 1) * TILE].astype(F32)
        side_ref[:, r * TILE : (r + 1) * TILE] = jnp.where(is_left, product, first_tile)


def edges_kernel(
    pattern_ref, left_ref, x_ref, down_ref, right_ref, rows_ref, target_ref, weight_ref, count_ref,
    top_ref, below_ref, side_ref, table_ref,
):
    live = lax.broadcasted_iota(jnp.int32, (CAP, PEERS), 0) < count_ref[...]
    table_ref[0] = rows_ref[...].astype(F32)
    table_ref[1] = target_ref[...].astype(F32)
    table_ref[2] = jnp.where(live, weight_ref[...].astype(F32), 0.0)
    write_edges(pattern_ref, left_ref, x_ref, down_ref, right_ref, 0, top_ref, below_ref, side_ref)


EDGE_SHAPES = (
    jax.ShapeDtypeStruct((ROWS, TC * TILE), BF16),
    jax.ShapeDtypeStruct((ROWS, TC * TILE), F32),
    jax.ShapeDtypeStruct((ROWS, TR * TILE), F32),
)
SMEM = pl.BlockSpec(memory_space=pltpu.SMEM)
VMEM = pl.BlockSpec(memory_space=pltpu.VMEM)
DOWN_EDGE = pl.BlockSpec((TC, TILE, TILE), lambda i: (TR - 1, 0, 0))
RIGHT_EDGE = pl.BlockSpec((TR, 1, TILE, TILE), lambda i: (0, TC - 1, 0, 0))


def whole(shape):
    return pl.BlockSpec(shape, lambda i: (0,) * len(shape))


def edges(pattern, left_flag, x, down_hop, right_hop, link_rows, link_target, link_weight, link_count):
    links = (link_rows.T, link_target.T, link_weight.T, link_count.reshape(1, PEERS))
    shapes = EDGE_SHAPES + (jax.ShapeDtypeStruct((3, CAP, PEERS), F32),)
    return pl.pallas_call(
        edges_kernel,
        grid=(1,),
        in_specs=[SMEM, SMEM, whole((ROWS, SITES_DEV)), DOWN_EDGE, RIGHT_EDGE] + [whole(a.shape) for a in links],
        out_specs=tuple(whole(s.shape) for s in shapes),
        out_shape=shapes,
        compiler_params=params(),
        cost_estimate=COST,
        name="edges",
    )(pattern, left_flag, x, down_hop, right_hop.reshape(TR, TC, TILE, TILE), *links)


def kept(pattern_ref, which, tile, value):
    return jnp.where(pattern_ref[which, tile] == 1, value, jnp.zeros_like(value))


def local_tile(pattern_ref, x_ref, onsite_ref, down_ref, right_ref, tile):
    def block(other):
        return x_ref[:, other * TILE : (other + 1) * TILE]

    r, k = divmod(tile, TC)
    fields = [block(tile)]
    tiles = [onsite_ref[tile]]
    if r > 0:
        fields.append(kept(pattern_ref, 0, tile - TC, block(tile - TC)))
        tiles.append(down_ref[tile - TC])
    if k > 0:
        fields.append(kept(pattern_ref, 1, tile - 1, block(tile - 1)))
        tiles.append(right_ref[tile - 1])
    total = dot(jnp.concatenate(fields, axis=1), jnp.concatenate(tiles, axis=0))
    fields = []
    tiles = []
    if r < TR - 1:
        fields.append(kept(pattern_ref, 0, tile, block(tile + TC)))
        tiles.append(down_ref[tile])
    if k < TC - 1:
        fields.append(kept(pattern_ref, 1, tile, block(tile + 1)))
        tiles.append(right_ref[tile])
    if fields:
        total = total + dot(jnp.concatenate(fields, axis=1), jnp.concatenate(tiles, axis=1), NT)
    return total


def halo_tile(pattern_ref, is_left, down_edge, right_edge, above_ref, below_ref, side_ref, tile):
    r, k = divmod(tile, TC)
    total = None

    def plus(value):
        return value if total is None else total + value

    if r == 0:
        total = plus(above_ref[:, k * TILE : (k + 1) * TILE])
    if r == TR - 1:
        lower = below_ref[:, k * TILE : (k + 1) * TILE]
        total = plus(dot(kept(pattern_ref, 0, tile, lower), down_edge(k), NT))
    if k == 0:
        total = plus(jnp.where(is_left, 0.0, side_ref[:, r * TILE : (r + 1) * TILE]))
    if k == TC - 1:
        righter = jnp.where(is_left, side_ref[:, r * TILE : (r + 1) * TILE], 0.0).astype(BF16)
        total = plus(dot(kept(pattern_ref, 1, tile, righter), right_edge(r), NT))
    return total


def signed(value):
    return jnp.where(lax.broadcasted_iota(jnp.int32, value.shape, 0) < ROWS // 2, value, -value)


def swapped(value):
    return jnp.concatenate([value[ROWS // 2 :], value[: ROWS // 2]], axis=0)


def vector_mean(value):
    comps = value.reshape(4, 16, value.shape[-1])
    return jnp.sum(comps, axis=1) * (1.0 / 16.0)


def near_kernel(
    pattern_ref, left_ref, v0_ref, onsite_ref, down_ref, right_ref, above_ref, below_ref, side_ref,
    pairing_ref, hot_ref, high_ref, near_ref, out_ref,
):
    is_left = left_ref[0] == 1
    for tile in range(TR * TC):
        cols = slice(tile * TILE, (tile + 1) * TILE)
        hop = local_tile(pattern_ref, v0_ref, onsite_ref, down_ref, right_ref, tile)
        halo = halo_tile(
            pattern_ref, is_left, lambda k: down_ref[(TR - 1) * TC + k], lambda r: right_ref[r * TC + TC - 1],
            above_ref, below_ref, side_ref, tile,
        )
        hop = hop if halo is None else hop + halo
        near_ref[:, cols] = signed(hop) + pairing_ref[:, cols] * swapped(v0_ref[:, cols].astype(F32))
    pairs = [split(near_ref[:, h * SPAN : (h + 1) * SPAN]) for h in range(HI)]
    terms = [[p[0] for p in pairs], [p[1] for p in pairs]]
    for start in range(0, SLOTS, CHUNK):
        out_ref[start : start + CHUNK, :] = gather_ends(terms, hot_ref, high_ref, start, CHUNK)


def near(pattern, left_flag, v0, onsite, down_hop, right_hop, halo, pairing, hot, high):
    return pl.pallas_call(
        near_kernel,
        in_specs=[SMEM, SMEM] + [VMEM] * 10,
        out_shape=(
            jax.ShapeDtypeStruct((ROWS, SITES_DEV), F32),
            jax.ShapeDtypeStruct((SLOTS, 2 * ROWS), F32),
        ),
        compiler_params=params(),
        cost_estimate=COST,
        name="near",
    )(pattern, left_flag, v0, onsite, down_hop, right_hop, *halo, pairing, hot, high)


SCATTER_SCRATCH = [pltpu.VMEM((HI * ROWS, 2 * SLOTS), BF16), pltpu.VMEM((HI * ROWS, SPAN), F32)]


def scatter_into(landed, hot_ref, high_ref, mask_ref, total_ref):
    turned = landed.astype(F32).T.astype(BF16)
    high_send = high_ref[0:SLOTS, :].T.astype(BF16)[:ROWS]
    high_recv = high_ref[SLOTS : 2 * SLOTS, :].T.astype(BF16)[:ROWS]
    zero = jnp.zeros((ROWS, SLOTS), BF16)
    for h in range(HI):
        rows = slice(h * ROWS, (h + 1) * ROWS)
        mask_ref[rows, 0:SLOTS] = jnp.where(high_send == BF16(h), turned[ROWS:], zero)
        mask_ref[rows, SLOTS : 2 * SLOTS] = jnp.where(high_recv == BF16(h), turned[:ROWS], zero)
    group = 4
    for start in range(0, HI, group):
        total_ref[start * ROWS : (start + group) * ROWS, :] = dot(
            mask_ref[start * ROWS : (start + group) * ROWS, :], hot_ref[0 : 2 * SLOTS, :]
        )


def relay_kernel(landed_ref, hot_ref, high_ref, weight_ref, near_ref, out_ref, mask_ref, total_ref):
    scatter_into(landed_ref[...], hot_ref, high_ref, mask_ref, total_ref)
    pairs = [split(signed(total_ref[h * ROWS : (h + 1) * ROWS, :])) for h in range(HI)]
    terms = [[p[0] for p in pairs], [p[1] for p in pairs]]
    for start in range(0, SLOTS, CHUNK):
        rows = slice(start, start + CHUNK)
        ends = gather_ends(terms, hot_ref, high_ref, start, CHUNK) + near_ref[rows, :]
        out_ref[rows, :] = as_payload(ends, weight_ref[rows, :])


def relay(landed, hot, high, weight, near_ends):
    return pl.pallas_call(
        relay_kernel,
        out_shape=jax.ShapeDtypeStruct((SLOTS, 2 * ROWS), BF16),
        scratch_shapes=SCATTER_SCRATCH,
        compiler_params=params(),
        cost_estimate=COST,
        name="relay",
    )(landed, hot, high, weight, near_ends)


def first_kernel(
    pattern_ref, left_ref, v0_ref, landed_ref, hot_ref, high_ref, near_ref, down_ref, right_ref,
    one_ref, x_ref, mom_ref, top_ref, below_ref, side_ref, mask_ref, total_ref,
):
    scatter_into(landed_ref[...], hot_ref, high_ref, mask_ref, total_ref)
    for h in range(HI):
        cols = slice(h * SPAN, (h + 1) * SPAN)
        v0 = v0_ref[:, cols].astype(F32)
        one = near_ref[:, cols] + signed(total_ref[h * ROWS : (h + 1) * ROWS, :])
        one_ref[:, cols] = one
        x_ref[:, cols] = one.astype(BF16)
        mom_ref[0, :, cols] = vector_mean(v0 * v0)
        mom_ref[1, :, cols] = vector_mean(v0 * one)
    write_edges(pattern_ref, left_ref, x_ref, down_ref, right_ref, 0, top_ref, below_ref, side_ref)


def first(pattern, left_flag, v0, landed, hot, high, near_part, down_hop, right_hop):
    shapes = (
        jax.ShapeDtypeStruct((ROWS, SITES_DEV), F32),
        jax.ShapeDtypeStruct((ROWS, SITES_DEV), BF16),
        jax.ShapeDtypeStruct((2, 4, SITES_DEV), F32),
    ) + EDGE_SHAPES
    return pl.pallas_call(
        first_kernel,
        grid=(1,),
        in_specs=[SMEM, SMEM]
        + [whole(a.shape) for a in (v0, landed, hot, high, near_part)]
        + [DOWN_EDGE, RIGHT_EDGE],
        out_specs=tuple(whole(s.shape) for s in shapes),
        out_shape=shapes,
        scratch_shapes=SCATTER_SCRATCH,
        compiler_params=params(),
        cost_estimate=COST,
        name="first",
    )(pattern, left_flag, v0, landed, hot, high, near_part, down_hop, right_hop.reshape(TR, TC, TILE, TILE))


def local_kernel(pattern_ref, x_ref, onsite_ref, down_ref, right_ref, out_ref):
    for tile in range(TR * TC):
        out_ref[:, tile * TILE : (tile + 1) * TILE] = local_tile(
            pattern_ref, x_ref, onsite_ref, down_ref, right_ref, tile
        )


def local(pattern, x, onsite, down_hop, right_hop):
    return pl.pallas_call(
        local_kernel,
        in_specs=[SMEM] + [VMEM] * 4,
        out_shape=jax.ShapeDtypeStruct((ROWS, SITES_DEV), F32),
        compiler_params=params(),
        cost_estimate=COST,
        name="local",
    )(pattern, x, onsite, down_hop, right_hop)


def second_kernel(
    pattern_ref, left_ref, v0_ref, one_ref, landed_ref, hot_ref, high_ref, local_ref, pairing_ref, mom_in_ref,
    above_ref, below_ref, side_ref, down_ref, right_ref, two_ref, mom_ref, mask_ref, total_ref,
):
    scatter_into(landed_ref[...], hot_ref, high_ref, mask_ref, total_ref)
    is_left = left_ref[0] == 1
    mom_ref[0:2] = mom_in_ref[...]
    for tile in range(TR * TC):
        cols = slice(tile * TILE, (tile + 1) * TILE)
        h, part = divmod(tile, SPAN // TILE)
        hop = local_ref[:, cols] + total_ref[h * ROWS : (h + 1) * ROWS, part * TILE : (part + 1) * TILE]
        halo = halo_tile(
            pattern_ref, is_left, lambda k: down_ref[k], lambda r: right_ref[r, 0],
            above_ref, below_ref, side_ref, tile,
        )
        hop = hop if halo is None else hop + halo
        v0 = v0_ref[:, cols].astype(F32)
        two = 2.0 * (signed(hop) + pairing_ref[:, cols] * swapped(one_ref[:, cols])) - v0
        two_ref[:, cols] = two
        mom_ref[2, :, cols] = vector_mean(v0 * two)


def second(pattern, left_flag, v0, one, landed, hot, high, local_part, pairing, mom, halo, down_hop, right_hop):
    shapes = (
        jax.ShapeDtypeStruct((ROWS, SITES_DEV), F32),
        jax.ShapeDtypeStruct((3, 4, SITES_DEV), F32),
    )
    arrays = (v0, one, landed, hot, high, local_part, pairing, mom) + tuple(halo)
    return pl.pallas_call(
        second_kernel,
        grid=(1,),
        in_specs=[SMEM, SMEM] + [whole(a.shape) for a in arrays] + [DOWN_EDGE, RIGHT_EDGE],
        out_specs=tuple(whole(s.shape) for s in shapes),
        out_shape=shapes,
        scratch_shapes=SCATTER_SCRATCH,
        compiler_params=params(),
        cost_estimate=COST,
        name="second",
    )(pattern, left_flag, *arrays, down_hop, right_hop.reshape(TR, TC, TILE, TILE))


def passed_along(value, axis, by):
    length = lax.axis_size(axis)
    pairs = [(i, i + by) for i in range(length) if 0 <= i + by < length]
    return lax.ppermute(value, axis, pairs)


def partner_2(value, axis, bit):
    return lax.ppermute(value, axis, [(i, i ^ 1 << bit) for i in range(lax.axis_size(axis))])


def spread_out(payload):
    return lax.all_to_all(
        payload.reshape(PEERS, CAP, 2 * ROWS), "tile", split_axis=0, concat_axis=0, tiled=True
    ).reshape(SLOTS, 2 * ROWS)


def other_layer(value):
    return partner_2(value, "layer", 1)


def shards(
    rand_vectors,
    onsite,
    down_hop,
    right_hop,
    pattern,
    pairing,
    link_rows,
    link_target,
    link_weight,
    link_count,
):
    v0 = rand_vectors.reshape(ROWS, SITES_DEV)
    pairing = pairing.reshape(1, SITES_DEV)
    pattern = pattern.T
    left_flag = (1 - lax.axis_index("layer") % 2).astype(jnp.int32).reshape(1)

    def halo_of(top, below_part, side_part):
        return (
            passed_along(below_part, "tile", 1),
            passed_along(top, "tile", -1),
            partner_2(side_part, "layer", 0),
        )

    *edge_parts, table = edges(
        pattern, left_flag, v0, down_hop, right_hop, link_rows, link_target, link_weight, link_count
    )
    halo = halo_of(*edge_parts)
    tables_other = tables_of(other_layer(table))
    hot, high, weight, payload = prepare(v0, table)
    landed_other = spread_out(payload)
    hot, tables_other = lax.optimization_barrier((hot, tables_other))
    near_part, near_ends = near(
        pattern, left_flag, v0, onsite, down_hop, right_hop, halo, pairing, hot, high
    )
    near_ends = other_layer(near_ends)
    landed_other, near_part = lax.optimization_barrier((landed_other, near_part))
    landed = other_layer(landed_other)
    payload = relay(landed_other, *tables_other, near_ends)
    landed_two = spread_out(payload)
    one, x, mom, *edge_parts = first(
        pattern, left_flag, v0, landed, hot, high, near_part, down_hop, right_hop
    )
    halo = halo_of(*edge_parts)
    local_part = local(pattern, x, onsite, down_hop, right_hop)
    landed_two, local_part, halo = lax.optimization_barrier((landed_two, local_part, halo))
    two, mom = second(
        pattern, left_flag, v0, one, landed_two, hot, high, local_part, pairing, mom, halo, down_hop, right_hop
    )
    shape = rand_vectors.shape
    return one.reshape(shape), two.reshape(shape), mom


def solution(mesh):
    both = ("tile", "layer")
    in_specs = (
        P(None, None, both),
        P(both, None, None),
        P(both, None, None),
        P(both, None, None),
        P(both, None),
        P(both),
        P(both, None),
        P(both, None),
        P(both, None),
        P(both),
    )
    out_specs = (P(None, None, both), P(None, None, both), P(None, None, both))
    return jax.shard_map(shards, mesh=mesh, in_specs=in_specs, out_specs=out_specs, check_vma=False)
```

```python
import jax
import jax.numpy as jnp
from jax import lax
from jax.experimental import pallas as pl
from jax.experimental.pallas import tpu as pltpu
from jax.sharding import PartitionSpec as P

TILE = 128
TR = 4
TC = 6
ROWS = 64
SITES_DEV = TR * TC * TILE
PEERS = 128
CAP = 8
SLOTS = PEERS * CAP
SPAN = 256
HI = SITES_DEV // SPAN
F32 = jnp.float32
BF16 = jnp.bfloat16
NT = (((1,), (1,)), ((), ()))
NN = (((1,), (0,)), ((), ()))
VMEM_LIMIT = 56 * 1024 * 1024


def dot(a, b, dims=NN):
    return lax.dot_general(a, b, dims, preferred_element_type=F32)


COST = pl.CostEstimate(flops=1000000, bytes_accessed=100000, transcendentals=0)


def params():
    return pltpu.CompilerParams(vmem_limit_bytes=VMEM_LIMIT)


def per_slot(table):
    spread = jnp.broadcast_to(table[None], (PEERS, CAP, PEERS)).reshape(SLOTS, PEERS)
    own = lax.broadcasted_iota(jnp.int32, (SLOTS, PEERS), 0) // CAP == lax.broadcasted_iota(
        jnp.int32, (SLOTS, PEERS), 1
    )
    return dot(jnp.where(own, spread, 0.0).astype(BF16), jnp.ones((PEERS, TILE), BF16))


def build_tables(rows, target, weight, hot_ref, high_ref, weight_ref):
    lane = lax.broadcasted_iota(jnp.int32, (SLOTS, SPAN), 1).astype(F32)
    spread_weight = per_slot(weight)
    weight_ref[...] = spread_weight
    wide_weight = jnp.concatenate([spread_weight, spread_weight], axis=1)
    for end, table in ((0, rows), (1, target)):
        coarse = jnp.floor(table * (1.0 / SPAN))
        low = per_slot(table - coarse * SPAN)
        high_ref[end * SLOTS : (end + 1) * SLOTS, :] = per_slot(coarse)
        same = lane == jnp.concatenate([low, low], axis=1)
        hot_ref[2 * end * SLOTS : (2 * end + 1) * SLOTS, :] = jnp.where(same, 1.0, 0.0).astype(BF16)
        if end == 1:
            hot_ref[SLOTS : 2 * SLOTS, :] = jnp.where(same, wide_weight, 0.0).astype(BF16)


def gather_ends(parts, hot_ref, high_ref, start, chunk):
    lane = lax.broadcasted_iota(jnp.int32, (chunk, TILE), 1)
    half = (lane >= ROWS).astype(F32)
    ends = []
    for end in range(2):
        hot = hot_ref[2 * end * SLOTS + start : 2 * end * SLOTS + start + chunk, :]
        high = high_ref[end * SLOTS + start : end * SLOTS + start + chunk, :] - half
        total = jnp.zeros((chunk, TILE), F32)
        for q in range(HI // 2):
            found = dot(hot, jnp.concatenate([parts[2 * q], parts[2 * q + 1]], axis=0), NT)
            total = jnp.where(high == 2.0 * q, found, total)
        ends.append(total + pltpu.roll(total, ROWS, 1))
    return jnp.where(lane < ROWS, ends[0], ends[1])


def as_payload(ends, weight):
    field = ends.astype(BF16)
    lane = lax.broadcasted_iota(jnp.int32, ends.shape, 1)
    return jnp.where(lane < ROWS, field.astype(F32), field.astype(F32) * weight).astype(BF16)


CHUNK = 256


def gather_payload(x_ref, hot_ref, high_ref, weight_ref, out_ref):
    parts = [x_ref[:, h * SPAN : (h + 1) * SPAN] for h in range(HI)]
    for start in range(0, SLOTS, CHUNK):
        ends = gather_ends(parts, hot_ref, high_ref, start, CHUNK)
        out_ref[start : start + CHUNK, :] = as_payload(ends, weight_ref[start : start + CHUNK, :])


def prepare_kernel(
    x_ref, rows_ref, target_ref, weight_ref, count_ref, hot_ref, high_ref, spread_ref, out_ref
):
    live = lax.broadcasted_iota(jnp.int32, (CAP, PEERS), 0) < count_ref[...]
    weight = jnp.where(live, weight_ref[...].astype(F32), 0.0)
    build_tables(
        rows_ref[...].astype(F32), target_ref[...].astype(F32), weight, hot_ref, high_ref, spread_ref
    )
    gather_payload(x_ref, hot_ref, high_ref, spread_ref, out_ref)


TABLE_SHAPES = (
    jax.ShapeDtypeStruct((3 * SLOTS, SPAN), BF16),
    jax.ShapeDtypeStruct((2 * SLOTS, TILE), F32),
    jax.ShapeDtypeStruct((SLOTS, TILE), F32),
)


def prepare(x, link_rows, link_target, link_weight, link_count):
    return pl.pallas_call(
        prepare_kernel,
        out_shape=TABLE_SHAPES + (jax.ShapeDtypeStruct((SLOTS, 2 * ROWS), BF16),),
        compiler_params=params(),
        cost_estimate=COST,
        name="prepare",
    )(x, link_rows.T, link_target.T, link_weight.T, link_count.reshape(1, PEERS))


def write_edges(pattern_ref, left_ref, x_ref, down_ref, right_ref, down_base, top_ref, below_ref, side_ref):
    top_ref[...] = x_ref[:, : TC * TILE]
    for k in range(TC):
        tile = (TR - 1) * TC + k
        keep = pattern_ref[0, tile].astype(F32)
        below_ref[:, k * TILE : (k + 1) * TILE] = keep * dot(
            x_ref[:, tile * TILE : (tile + 1) * TILE], down_ref[down_base + k]
        )
    is_left = left_ref[0] == 1
    for r in range(TR):
        last = r * TC + TC - 1
        keep = pattern_ref[1, last].astype(F32)
        product = keep * dot(x_ref[:, last * TILE : (last + 1) * TILE], right_ref[r, 0])
        first_tile = x_ref[:, r * TC * TILE : (r * TC + 1) * TILE].astype(F32)
        side_ref[:, r * TILE : (r + 1) * TILE] = jnp.where(is_left, product, first_tile)


def edges_kernel(pattern_ref, left_ref, x_ref, down_ref, right_ref, top_ref, below_ref, side_ref):
    write_edges(pattern_ref, left_ref, x_ref, down_ref, right_ref, 0, top_ref, below_ref, side_ref)


EDGE_SHAPES = (
    jax.ShapeDtypeStruct((ROWS, TC * TILE), BF16),
    jax.ShapeDtypeStruct((ROWS, TC * TILE), F32),
    jax.ShapeDtypeStruct((ROWS, TR * TILE), F32),
)
SMEM = pl.BlockSpec(memory_space=pltpu.SMEM)
VMEM = pl.BlockSpec(memory_space=pltpu.VMEM)
DOWN_EDGE = pl.BlockSpec((TC, TILE, TILE), lambda i: (TR - 1, 0, 0))
RIGHT_EDGE = pl.BlockSpec((TR, 1, TILE, TILE), lambda i: (0, TC - 1, 0, 0))


def whole(shape):
    return pl.BlockSpec(shape, lambda i: (0,) * len(shape))


def edges(pattern, left_flag, x, down_hop, right_hop):
    return pl.pallas_call(
        edges_kernel,
        grid=(1,),
        in_specs=[SMEM, SMEM, whole((ROWS, SITES_DEV)), DOWN_EDGE, RIGHT_EDGE],
        out_specs=tuple(whole(s.shape) for s in EDGE_SHAPES),
        out_shape=EDGE_SHAPES,
        compiler_params=params(),
        cost_estimate=COST,
        name="edges",
    )(pattern, left_flag, x, down_hop, right_hop.reshape(TR, TC, TILE, TILE))


def kept(pattern_ref, which, tile, value):
    return jnp.where(pattern_ref[which, tile] == 1, value, jnp.zeros_like(value))


def local_tile(pattern_ref, x_ref, onsite_ref, down_ref, right_ref, tile):
    def block(other):
        return x_ref[:, other * TILE : (other + 1) * TILE]

    r, k = divmod(tile, TC)
    fields = [block(tile)]
    tiles = [onsite_ref[tile]]
    if r > 0:
        fields.append(kept(pattern_ref, 0, tile - TC, block(tile - TC)))
        tiles.append(down_ref[tile - TC])
    if k > 0:
        fields.append(kept(pattern_ref, 1, tile - 1, block(tile - 1)))
        tiles.append(right_ref[tile - 1])
    total = dot(jnp.concatenate(fields, axis=1), jnp.concatenate(tiles, axis=0))
    fields = []
    tiles = []
    if r < TR - 1:
        fields.append(kept(pattern_ref, 0, tile, block(tile + TC)))
        tiles.append(down_ref[tile])
    if k < TC - 1:
        fields.append(kept(pattern_ref, 1, tile, block(tile + 1)))
        tiles.append(right_ref[tile])
    if fields:
        total = total + dot(jnp.concatenate(fields, axis=1), jnp.concatenate(tiles, axis=1), NT)
    return total


def halo_tile(pattern_ref, is_left, down_edge, right_edge, above_ref, below_ref, side_ref, tile):
    r, k = divmod(tile, TC)
    total = None

    def plus(value):
        return value if total is None else total + value

    if r == 0:
        total = plus(above_ref[:, k * TILE : (k + 1) * TILE])
    if r == TR - 1:
        lower = below_ref[:, k * TILE : (k + 1) * TILE]
        total = plus(dot(kept(pattern_ref, 0, tile, lower), down_edge(k), NT))
    if k == 0:
        total = plus(jnp.where(is_left, 0.0, side_ref[:, r * TILE : (r + 1) * TILE]))
    if k == TC - 1:
        righter = jnp.where(is_left, side_ref[:, r * TILE : (r + 1) * TILE], 0.0).astype(BF16)
        total = plus(dot(kept(pattern_ref, 1, tile, righter), right_edge(r), NT))
    return total


def signed(value):
    return jnp.where(lax.broadcasted_iota(jnp.int32, value.shape, 0) < ROWS // 2, value, -value)


def swapped(value):
    return jnp.concatenate([value[ROWS // 2 :], value[: ROWS // 2]], axis=0)


def vector_mean(value):
    comps = value.reshape(4, 16, value.shape[-1])
    return jnp.sum(comps, axis=1) * (1.0 / 16.0)


def near_kernel(
    pattern_ref, left_ref, v0_ref, onsite_ref, down_ref, right_ref, above_ref, below_ref, side_ref,
    pairing_ref, near_ref,
):
    is_left = left_ref[0] == 1
    for tile in range(TR * TC):
        cols = slice(tile * TILE, (tile + 1) * TILE)
        hop = local_tile(pattern_ref, v0_ref, onsite_ref, down_ref, right_ref, tile)
        halo = halo_tile(
            pattern_ref, is_left, lambda k: down_ref[(TR - 1) * TC + k], lambda r: right_ref[r * TC + TC - 1],
            above_ref, below_ref, side_ref, tile,
        )
        hop = hop if halo is None else hop + halo
        near_ref[:, cols] = signed(hop) + pairing_ref[:, cols] * swapped(v0_ref[:, cols].astype(F32))


def near(pattern, left_flag, v0, onsite, down_hop, right_hop, halo, pairing):
    return pl.pallas_call(
        near_kernel,
        in_specs=[SMEM, SMEM] + [VMEM] * 8,
        out_shape=jax.ShapeDtypeStruct((ROWS, SITES_DEV), F32),
        compiler_params=params(),
        cost_estimate=COST,
        name="near",
    )(pattern, left_flag, v0, onsite, down_hop, right_hop, *halo, pairing)


SCATTER_SCRATCH = [pltpu.VMEM((HI * ROWS, 2 * SLOTS), BF16), pltpu.VMEM((HI * ROWS, SPAN), F32)]


def scatter_into(landed, hot_ref, high_ref, mask_ref, total_ref):
    turned = landed.astype(F32).T.astype(BF16)
    high_send = high_ref[0:SLOTS, :].T.astype(BF16)[:ROWS]
    high_recv = high_ref[SLOTS : 2 * SLOTS, :].T.astype(BF16)[:ROWS]
    zero = jnp.zeros((ROWS, SLOTS), BF16)
    for h in range(HI):
        rows = slice(h * ROWS, (h + 1) * ROWS)
        mask_ref[rows, 0:SLOTS] = jnp.where(high_send == BF16(h), turned[ROWS:], zero)
        mask_ref[rows, SLOTS : 2 * SLOTS] = jnp.where(high_recv == BF16(h), turned[:ROWS], zero)
    group = 4
    for start in range(0, HI, group):
        total_ref[start * ROWS : (start + group) * ROWS, :] = dot(
            mask_ref[start * ROWS : (start + group) * ROWS, :], hot_ref[0 : 2 * SLOTS, :]
        )


def first_kernel(
    pattern_ref, left_ref, v0_ref, landed_ref, hot_ref, high_ref, weight_ref, near_ref, down_ref, right_ref,
    one_ref, x_ref, mom_ref, top_ref, below_ref, side_ref, out_ref, mask_ref, total_ref,
):
    scatter_into(landed_ref[...], hot_ref, high_ref, mask_ref, total_ref)
    for h in range(HI):
        cols = slice(h * SPAN, (h + 1) * SPAN)
        v0 = v0_ref[:, cols].astype(F32)
        one = near_ref[:, cols] + signed(total_ref[h * ROWS : (h + 1) * ROWS, :])
        one_ref[:, cols] = one
        x_ref[:, cols] = one.astype(BF16)
        mom_ref[0, :, cols] = vector_mean(v0 * v0)
        mom_ref[1, :, cols] = vector_mean(v0 * one)
    gather_payload(x_ref, hot_ref, high_ref, weight_ref, out_ref)
    write_edges(pattern_ref, left_ref, x_ref, down_ref, right_ref, 0, top_ref, below_ref, side_ref)


def first(pattern, left_flag, v0, landed, hot, high, weight, near_part, down_hop, right_hop):
    shapes = (
        jax.ShapeDtypeStruct((ROWS, SITES_DEV), F32),
        jax.ShapeDtypeStruct((ROWS, SITES_DEV), BF16),
        jax.ShapeDtypeStruct((2, 4, SITES_DEV), F32),
    ) + EDGE_SHAPES + (jax.ShapeDtypeStruct((SLOTS, 2 * ROWS), BF16),)
    return pl.pallas_call(
        first_kernel,
        grid=(1,),
        in_specs=[SMEM, SMEM]
        + [whole(a.shape) for a in (v0, landed, hot, high, weight, near_part)]
        + [DOWN_EDGE, RIGHT_EDGE],
        out_specs=tuple(whole(s.shape) for s in shapes),
        out_shape=shapes,
        scratch_shapes=SCATTER_SCRATCH,
        compiler_params=params(),
        cost_estimate=COST,
        name="first",
    )(pattern, left_flag, v0, landed, hot, high, weight, near_part, down_hop, right_hop.reshape(TR, TC, TILE, TILE))


def local_kernel(pattern_ref, x_ref, onsite_ref, down_ref, right_ref, out_ref):
    for tile in range(TR * TC):
        out_ref[:, tile * TILE : (tile + 1) * TILE] = local_tile(
            pattern_ref, x_ref, onsite_ref, down_ref, right_ref, tile
        )


def local(pattern, x, onsite, down_hop, right_hop):
    return pl.pallas_call(
        local_kernel,
        in_specs=[SMEM] + [VMEM] * 4,
        out_shape=jax.ShapeDtypeStruct((ROWS, SITES_DEV), F32),
        compiler_params=params(),
        cost_estimate=COST,
        name="local",
    )(pattern, x, onsite, down_hop, right_hop)


def second_kernel(
    pattern_ref, left_ref, v0_ref, one_ref, landed_ref, hot_ref, high_ref, local_ref, pairing_ref, mom_in_ref,
    above_ref, below_ref, side_ref, down_ref, right_ref, two_ref, mom_ref, mask_ref, total_ref,
):
    scatter_into(landed_ref[...], hot_ref, high_ref, mask_ref, total_ref)
    is_left = left_ref[0] == 1
    mom_ref[0:2] = mom_in_ref[...]
    for tile in range(TR * TC):
        cols = slice(tile * TILE, (tile + 1) * TILE)
        h, part = divmod(tile, SPAN // TILE)
        hop = local_ref[:, cols] + total_ref[h * ROWS : (h + 1) * ROWS, part * TILE : (part + 1) * TILE]
        halo = halo_tile(
            pattern_ref, is_left, lambda k: down_ref[k], lambda r: right_ref[r, 0],
            above_ref, below_ref, side_ref, tile,
        )
        hop = hop if halo is None else hop + halo
        v0 = v0_ref[:, cols].astype(F32)
        two = 2.0 * (signed(hop) + pairing_ref[:, cols] * swapped(one_ref[:, cols])) - v0
        two_ref[:, cols] = two
        mom_ref[2, :, cols] = vector_mean(v0 * two)


def second(pattern, left_flag, v0, one, landed, hot, high, local_part, pairing, mom, halo, down_hop, right_hop):
    shapes = (
        jax.ShapeDtypeStruct((ROWS, SITES_DEV), F32),
        jax.ShapeDtypeStruct((3, 4, SITES_DEV), F32),
    )
    arrays = (v0, one, landed, hot, high, local_part, pairing, mom) + tuple(halo)
    return pl.pallas_call(
        second_kernel,
        grid=(1,),
        in_specs=[SMEM, SMEM] + [whole(a.shape) for a in arrays] + [DOWN_EDGE, RIGHT_EDGE],
        out_specs=tuple(whole(s.shape) for s in shapes),
        out_shape=shapes,
        scratch_shapes=SCATTER_SCRATCH,
        compiler_params=params(),
        cost_estimate=COST,
        name="second",
    )(pattern, left_flag, *arrays, down_hop, right_hop.reshape(TR, TC, TILE, TILE))


def passed_along(value, axis, by):
    length = lax.axis_size(axis)
    pairs = [(i, i + by) for i in range(length) if 0 <= i + by < length]
    return lax.ppermute(value, axis, pairs)


def partner_2(value, axis, bit):
    return lax.ppermute(value, axis, [(i, i ^ 1 << bit) for i in range(lax.axis_size(axis))])


def spread_out(payload):
    return lax.all_to_all(
        payload.reshape(PEERS, CAP, 2 * ROWS), "tile", split_axis=0, concat_axis=0, tiled=True
    ).reshape(SLOTS, 2 * ROWS)


def other_layer(value):
    return partner_2(value, "layer", 1)


def shards(
    rand_vectors,
    onsite,
    down_hop,
    right_hop,
    pattern,
    pairing,
    link_rows,
    link_target,
    link_weight,
    link_count,
):
    v0 = rand_vectors.reshape(ROWS, SITES_DEV)
    pairing = pairing.reshape(1, SITES_DEV)
    pattern = pattern.T
    left_flag = (1 - lax.axis_index("layer") % 2).astype(jnp.int32).reshape(1)

    def halo_of(top, below_part, side_part):
        return (
            passed_along(below_part, "tile", 1),
            passed_along(top, "tile", -1),
            partner_2(side_part, "layer", 0),
        )

    hot, high, weight, payload = prepare(v0, link_rows, link_target, link_weight, link_count)
    spread = spread_out(payload)
    halo = halo_of(*edges(pattern, left_flag, v0, down_hop, right_hop))
    near_part = near(pattern, left_flag, v0, onsite, down_hop, right_hop, halo, pairing)
    spread, near_part = lax.optimization_barrier((spread, near_part))
    landed = other_layer(spread)
    one, x, mom, *edge_parts, payload = first(
        pattern, left_flag, v0, landed, hot, high, weight, near_part, down_hop, right_hop
    )
    spread = spread_out(payload)
    halo = halo_of(*edge_parts)
    local_part = local(pattern, x, onsite, down_hop, right_hop)
    spread, local_part, halo = lax.optimization_barrier((spread, local_part, halo))
    landed = other_layer(spread)
    two, mom = second(
        pattern, left_flag, v0, one, landed, hot, high, local_part, pairing, mom, halo, down_hop, right_hop
    )
    shape = rand_vectors.shape
    return one.reshape(shape), two.reshape(shape), mom


def solution(mesh):
    both = ("tile", "layer")
    in_specs = (
        P(None, None, both),
        P(both, None, None),
        P(both, None, None),
        P(both, None, None),
        P(both, None),
        P(both),
        P(both, None),
        P(both, None),
        P(both, None),
        P(both),
    )
    out_specs = (P(None, None, both), P(None, None, both), P(None, None, both))
    return jax.shard_map(shards, mesh=mesh, in_specs=in_specs, out_specs=out_specs, check_vma=False)
```

```python
import jax
import jax.numpy as jnp
from jax import lax
from jax.experimental import pallas as pl
from jax.experimental.pallas import tpu as pltpu
from jax.sharding import Mesh
from jax.sharding import PartitionSpec as P

TILE = 128
TR = 4
TC = 6
ROWS = 64
SITES_DEV = TR * TC * TILE
PEERS = 128
CAP = 8
SLOTS = PEERS * CAP
SPAN = 256
HI = SITES_DEV // SPAN
F32 = jnp.float32
BF16 = jnp.bfloat16
NT = (((1,), (1,)), ((), ()))
NN = (((1,), (0,)), ((), ()))
VMEM_LIMIT = 56 * 1024 * 1024


def dot(a, b, dims=NN):
    return lax.dot_general(a, b, dims, preferred_element_type=F32)


COST = pl.CostEstimate(flops=1000000, bytes_accessed=100000, transcendentals=0)


def params():
    return pltpu.CompilerParams(vmem_limit_bytes=VMEM_LIMIT)


def per_slot(table):
    spread = jnp.broadcast_to(table[None], (PEERS, CAP, PEERS)).reshape(SLOTS, PEERS)
    own = lax.broadcasted_iota(jnp.int32, (SLOTS, PEERS), 0) // CAP == lax.broadcasted_iota(
        jnp.int32, (SLOTS, PEERS), 1
    )
    return dot(jnp.where(own, spread, 0.0).astype(BF16), jnp.ones((PEERS, TILE), BF16))


def build_tables(rows, target, weight, hot_ref, high_ref, weight_ref):
    lane = lax.broadcasted_iota(jnp.int32, (SLOTS, SPAN), 1).astype(F32)
    spread_weight = per_slot(weight)
    weight_ref[...] = spread_weight
    wide_weight = jnp.concatenate([spread_weight, spread_weight], axis=1)
    for end, table in ((0, rows), (1, target)):
        coarse = jnp.floor(table * (1.0 / SPAN))
        low = per_slot(table - coarse * SPAN)
        high_ref[end * SLOTS : (end + 1) * SLOTS, :] = per_slot(coarse)
        same = lane == jnp.concatenate([low, low], axis=1)
        hot_ref[2 * end * SLOTS : (2 * end + 1) * SLOTS, :] = jnp.where(same, 1.0, 0.0).astype(BF16)
        if end == 1:
            hot_ref[SLOTS : 2 * SLOTS, :] = jnp.where(same, wide_weight, 0.0).astype(BF16)


def gather_ends(parts, hot_ref, high_ref, start, chunk):
    lane = lax.broadcasted_iota(jnp.int32, (chunk, TILE), 1)
    half = (lane >= ROWS).astype(F32)
    ends = []
    for end in range(2):
        hot = hot_ref[2 * end * SLOTS + start : 2 * end * SLOTS + start + chunk, :]
        high = high_ref[end * SLOTS + start : end * SLOTS + start + chunk, :] - half
        total = jnp.zeros((chunk, TILE), F32)
        for q in range(HI // 2):
            found = dot(hot, jnp.concatenate([parts[2 * q], parts[2 * q + 1]], axis=0), NT)
            total = jnp.where(high == 2.0 * q, found, total)
        ends.append(total + pltpu.roll(total, ROWS, 1))
    return jnp.where(lane < ROWS, ends[0], ends[1])


def as_payload(ends, weight):
    field = ends.astype(BF16)
    lane = lax.broadcasted_iota(jnp.int32, ends.shape, 1)
    return jnp.where(lane < ROWS, field.astype(F32), field.astype(F32) * weight).astype(BF16)


CHUNK = 256


def gather_payload(x_ref, hot_ref, high_ref, weight_ref, out_ref):
    parts = [x_ref[:, h * SPAN : (h + 1) * SPAN] for h in range(HI)]
    for start in range(0, SLOTS, CHUNK):
        ends = gather_ends(parts, hot_ref, high_ref, start, CHUNK)
        payload = as_payload(ends, weight_ref[start : start + CHUNK, :])
        out_ref[0, start : start + CHUNK, :] = payload
        out_ref[1, start : start + CHUNK, :] = payload


def prepare_kernel(
    x_ref, rows_ref, target_ref, weight_ref, count_ref, hot_ref, high_ref, spread_ref, out_ref
):
    live = lax.broadcasted_iota(jnp.int32, (CAP, PEERS), 0) < count_ref[...]
    weight = jnp.where(live, weight_ref[...].astype(F32), 0.0)
    build_tables(
        rows_ref[...].astype(F32), target_ref[...].astype(F32), weight, hot_ref, high_ref, spread_ref
    )
    gather_payload(x_ref, hot_ref, high_ref, spread_ref, out_ref)


TABLE_SHAPES = (
    jax.ShapeDtypeStruct((3 * SLOTS, SPAN), BF16),
    jax.ShapeDtypeStruct((2 * SLOTS, TILE), F32),
    jax.ShapeDtypeStruct((SLOTS, TILE), F32),
)


def prepare(x, link_rows, link_target, link_weight, link_count):
    return pl.pallas_call(
        prepare_kernel,
        out_shape=TABLE_SHAPES + (jax.ShapeDtypeStruct((2, SLOTS, 2 * ROWS), BF16),),
        compiler_params=params(),
        cost_estimate=COST,
        name="prepare",
    )(x, link_rows.T, link_target.T, link_weight.T, link_count.reshape(1, PEERS))


def write_edges(pattern_ref, left_ref, x_ref, down_ref, right_ref, down_base, top_ref, below_ref, side_ref):
    top_ref[...] = x_ref[:, : TC * TILE]
    for k in range(TC):
        tile = (TR - 1) * TC + k
        keep = pattern_ref[0, tile].astype(F32)
        below_ref[:, k * TILE : (k + 1) * TILE] = keep * dot(
            x_ref[:, tile * TILE : (tile + 1) * TILE], down_ref[down_base + k]
        )
    is_left = left_ref[0] == 1
    for r in range(TR):
        last = r * TC + TC - 1
        keep = pattern_ref[1, last].astype(F32)
        product = keep * dot(x_ref[:, last * TILE : (last + 1) * TILE], right_ref[r, 0])
        first_tile = x_ref[:, r * TC * TILE : (r * TC + 1) * TILE].astype(F32)
        side_ref[:, r * TILE : (r + 1) * TILE] = jnp.where(is_left, product, first_tile)


def edges_kernel(pattern_ref, left_ref, x_ref, down_ref, right_ref, top_ref, below_ref, side_ref):
    write_edges(pattern_ref, left_ref, x_ref, down_ref, right_ref, 0, top_ref, below_ref, side_ref)


EDGE_SHAPES = (
    jax.ShapeDtypeStruct((ROWS, TC * TILE), BF16),
    jax.ShapeDtypeStruct((ROWS, TC * TILE), F32),
    jax.ShapeDtypeStruct((ROWS, TR * TILE), F32),
)
SMEM = pl.BlockSpec(memory_space=pltpu.SMEM)
VMEM = pl.BlockSpec(memory_space=pltpu.VMEM)
DOWN_EDGE = pl.BlockSpec((TC, TILE, TILE), lambda i: (TR - 1, 0, 0))
RIGHT_EDGE = pl.BlockSpec((TR, 1, TILE, TILE), lambda i: (0, TC - 1, 0, 0))


def whole(shape):
    return pl.BlockSpec(shape, lambda i: (0,) * len(shape))


def edges(pattern, left_flag, x, down_hop, right_hop):
    return pl.pallas_call(
        edges_kernel,
        grid=(1,),
        in_specs=[SMEM, SMEM, whole((ROWS, SITES_DEV)), DOWN_EDGE, RIGHT_EDGE],
        out_specs=tuple(whole(s.shape) for s in EDGE_SHAPES),
        out_shape=EDGE_SHAPES,
        compiler_params=params(),
        cost_estimate=COST,
        name="edges",
    )(pattern, left_flag, x, down_hop, right_hop.reshape(TR, TC, TILE, TILE))


def kept(pattern_ref, which, tile, value):
    return jnp.where(pattern_ref[which, tile] == 1, value, jnp.zeros_like(value))


def local_tile(pattern_ref, x_ref, onsite_ref, down_ref, right_ref, tile):
    def block(other):
        return x_ref[:, other * TILE : (other + 1) * TILE]

    r, k = divmod(tile, TC)
    fields = [block(tile)]
    tiles = [onsite_ref[tile]]
    if r > 0:
        fields.append(kept(pattern_ref, 0, tile - TC, block(tile - TC)))
        tiles.append(down_ref[tile - TC])
    if k > 0:
        fields.append(kept(pattern_ref, 1, tile - 1, block(tile - 1)))
        tiles.append(right_ref[tile - 1])
    total = dot(jnp.concatenate(fields, axis=1), jnp.concatenate(tiles, axis=0))
    fields = []
    tiles = []
    if r < TR - 1:
        fields.append(kept(pattern_ref, 0, tile, block(tile + TC)))
        tiles.append(down_ref[tile])
    if k < TC - 1:
        fields.append(kept(pattern_ref, 1, tile, block(tile + 1)))
        tiles.append(right_ref[tile])
    if fields:
        total = total + dot(jnp.concatenate(fields, axis=1), jnp.concatenate(tiles, axis=1), NT)
    return total


def halo_tile(pattern_ref, is_left, down_edge, right_edge, above_ref, below_ref, side_ref, tile):
    r, k = divmod(tile, TC)
    total = None

    def plus(value):
        return value if total is None else total + value

    if r == 0:
        total = plus(above_ref[:, k * TILE : (k + 1) * TILE])
    if r == TR - 1:
        lower = below_ref[:, k * TILE : (k + 1) * TILE]
        total = plus(dot(kept(pattern_ref, 0, tile, lower), down_edge(k), NT))
    if k == 0:
        total = plus(jnp.where(is_left, 0.0, side_ref[:, r * TILE : (r + 1) * TILE]))
    if k == TC - 1:
        righter = jnp.where(is_left, side_ref[:, r * TILE : (r + 1) * TILE], 0.0).astype(BF16)
        total = plus(dot(kept(pattern_ref, 1, tile, righter), right_edge(r), NT))
    return total


def signed(value):
    return jnp.where(lax.broadcasted_iota(jnp.int32, value.shape, 0) < ROWS // 2, value, -value)


def swapped(value):
    return jnp.concatenate([value[ROWS // 2 :], value[: ROWS // 2]], axis=0)


def vector_mean(value):
    comps = value.reshape(4, 16, value.shape[-1])
    return jnp.sum(comps, axis=1) * (1.0 / 16.0)


def near_kernel(
    pattern_ref, left_ref, v0_ref, onsite_ref, down_ref, right_ref, above_ref, below_ref, side_ref,
    pairing_ref, near_ref,
):
    is_left = left_ref[0] == 1
    for tile in range(TR * TC):
        cols = slice(tile * TILE, (tile + 1) * TILE)
        hop = local_tile(pattern_ref, v0_ref, onsite_ref, down_ref, right_ref, tile)
        halo = halo_tile(
            pattern_ref, is_left, lambda k: down_ref[(TR - 1) * TC + k], lambda r: right_ref[r * TC + TC - 1],
            above_ref, below_ref, side_ref, tile,
        )
        hop = hop if halo is None else hop + halo
        near_ref[:, cols] = signed(hop) + pairing_ref[:, cols] * swapped(v0_ref[:, cols].astype(F32))


def near(pattern, left_flag, v0, onsite, down_hop, right_hop, halo, pairing):
    return pl.pallas_call(
        near_kernel,
        in_specs=[SMEM, SMEM] + [VMEM] * 8,
        out_shape=jax.ShapeDtypeStruct((ROWS, SITES_DEV), F32),
        compiler_params=params(),
        cost_estimate=COST,
        name="near",
    )(pattern, left_flag, v0, onsite, down_hop, right_hop, *halo, pairing)


SCATTER_SCRATCH = [pltpu.VMEM((HI * ROWS, 2 * SLOTS), BF16), pltpu.VMEM((HI * ROWS, SPAN), F32)]


def scatter_into(landed, hot_ref, high_ref, mask_ref, total_ref):
    turned = landed.astype(F32).T.astype(BF16)
    high_send = high_ref[0:SLOTS, :].T.astype(BF16)[:ROWS]
    high_recv = high_ref[SLOTS : 2 * SLOTS, :].T.astype(BF16)[:ROWS]
    zero = jnp.zeros((ROWS, SLOTS), BF16)
    for h in range(HI):
        rows = slice(h * ROWS, (h + 1) * ROWS)
        mask_ref[rows, 0:SLOTS] = jnp.where(high_send == BF16(h), turned[ROWS:], zero)
        mask_ref[rows, SLOTS : 2 * SLOTS] = jnp.where(high_recv == BF16(h), turned[:ROWS], zero)
    group = 4
    for start in range(0, HI, group):
        total_ref[start * ROWS : (start + group) * ROWS, :] = dot(
            mask_ref[start * ROWS : (start + group) * ROWS, :], hot_ref[0 : 2 * SLOTS, :]
        )


def first_kernel(
    pattern_ref, left_ref, v0_ref, landed_ref, hot_ref, high_ref, weight_ref, near_ref, down_ref, right_ref,
    one_ref, x_ref, mom_ref, top_ref, below_ref, side_ref, out_ref, mask_ref, total_ref,
):
    scatter_into(landed_ref[left_ref[1]], hot_ref, high_ref, mask_ref, total_ref)
    for h in range(HI):
        cols = slice(h * SPAN, (h + 1) * SPAN)
        v0 = v0_ref[:, cols].astype(F32)
        one = near_ref[:, cols] + signed(total_ref[h * ROWS : (h + 1) * ROWS, :])
        one_ref[:, cols] = one
        x_ref[:, cols] = one.astype(BF16)
        mom_ref[0, :, cols] = vector_mean(v0 * v0)
        mom_ref[1, :, cols] = vector_mean(v0 * one)
    gather_payload(x_ref, hot_ref, high_ref, weight_ref, out_ref)
    write_edges(pattern_ref, left_ref, x_ref, down_ref, right_ref, 0, top_ref, below_ref, side_ref)


def first(pattern, left_flag, v0, landed, hot, high, weight, near_part, down_hop, right_hop):
    shapes = (
        jax.ShapeDtypeStruct((ROWS, SITES_DEV), F32),
        jax.ShapeDtypeStruct((ROWS, SITES_DEV), BF16),
        jax.ShapeDtypeStruct((2, 4, SITES_DEV), F32),
    ) + EDGE_SHAPES + (jax.ShapeDtypeStruct((2, SLOTS, 2 * ROWS), BF16),)
    return pl.pallas_call(
        first_kernel,
        grid=(1,),
        in_specs=[SMEM, SMEM]
        + [whole(a.shape) for a in (v0, landed, hot, high, weight, near_part)]
        + [DOWN_EDGE, RIGHT_EDGE],
        out_specs=tuple(whole(s.shape) for s in shapes),
        out_shape=shapes,
        scratch_shapes=SCATTER_SCRATCH,
        compiler_params=params(),
        cost_estimate=COST,
        name="first",
    )(pattern, left_flag, v0, landed, hot, high, weight, near_part, down_hop, right_hop.reshape(TR, TC, TILE, TILE))


def local_kernel(pattern_ref, x_ref, onsite_ref, down_ref, right_ref, out_ref):
    for tile in range(TR * TC):
        out_ref[:, tile * TILE : (tile + 1) * TILE] = local_tile(
            pattern_ref, x_ref, onsite_ref, down_ref, right_ref, tile
        )


def local(pattern, x, onsite, down_hop, right_hop):
    return pl.pallas_call(
        local_kernel,
        in_specs=[SMEM] + [VMEM] * 4,
        out_shape=jax.ShapeDtypeStruct((ROWS, SITES_DEV), F32),
        compiler_params=params(),
        cost_estimate=COST,
        name="local",
    )(pattern, x, onsite, down_hop, right_hop)


def second_kernel(
    pattern_ref, left_ref, v0_ref, one_ref, landed_ref, hot_ref, high_ref, local_ref, pairing_ref, mom_in_ref,
    above_ref, below_ref, side_ref, down_ref, right_ref, two_ref, mom_ref, mask_ref, total_ref,
):
    scatter_into(landed_ref[left_ref[1]], hot_ref, high_ref, mask_ref, total_ref)
    is_left = left_ref[0] == 1
    mom_ref[0:2] = mom_in_ref[...]
    for tile in range(TR * TC):
        cols = slice(tile * TILE, (tile + 1) * TILE)
        h, part = divmod(tile, SPAN // TILE)
        hop = local_ref[:, cols] + total_ref[h * ROWS : (h + 1) * ROWS, part * TILE : (part + 1) * TILE]
        halo = halo_tile(
            pattern_ref, is_left, lambda k: down_ref[k], lambda r: right_ref[r, 0],
            above_ref, below_ref, side_ref, tile,
        )
        hop = hop if halo is None else hop + halo
        v0 = v0_ref[:, cols].astype(F32)
        two = 2.0 * (signed(hop) + pairing_ref[:, cols] * swapped(one_ref[:, cols])) - v0
        two_ref[:, cols] = two
        mom_ref[2, :, cols] = vector_mean(v0 * two)


def second(pattern, left_flag, v0, one, landed, hot, high, local_part, pairing, mom, halo, down_hop, right_hop):
    shapes = (
        jax.ShapeDtypeStruct((ROWS, SITES_DEV), F32),
        jax.ShapeDtypeStruct((3, 4, SITES_DEV), F32),
    )
    arrays = (v0, one, landed, hot, high, local_part, pairing, mom) + tuple(halo)
    return pl.pallas_call(
        second_kernel,
        grid=(1,),
        in_specs=[SMEM, SMEM] + [whole(a.shape) for a in arrays] + [DOWN_EDGE, RIGHT_EDGE],
        out_specs=tuple(whole(s.shape) for s in shapes),
        out_shape=shapes,
        scratch_shapes=SCATTER_SCRATCH,
        compiler_params=params(),
        cost_estimate=COST,
        name="second",
    )(pattern, left_flag, *arrays, down_hop, right_hop.reshape(TR, TC, TILE, TILE))


TILE_AXES = ("z_low", "y", "x", "core")


def passed_along(value, by):
    length = PEERS
    pairs = [(i, i + by) for i in range(length) if 0 <= i + by < length]
    return lax.ppermute(value, TILE_AXES, pairs)


def spread_out(payload):
    spread = lax.all_to_all(
        payload.reshape(2 * PEERS, CAP, 2 * ROWS), ("sheet",) + TILE_AXES, split_axis=0, concat_axis=0, tiled=True
    )
    return spread.reshape(2, SLOTS, 2 * ROWS)


def shards(
    rand_vectors,
    onsite,
    down_hop,
    right_hop,
    pattern,
    pairing,
    link_rows,
    link_target,
    link_weight,
    link_count,
):
    v0 = rand_vectors.reshape(ROWS, SITES_DEV)
    pairing = pairing.reshape(1, SITES_DEV)
    pattern = pattern.T
    left_flag = jnp.stack([1 - lax.axis_index("side"), 1 - lax.axis_index("sheet")]).astype(jnp.int32)

    def halo_of(top, below_part, side_part):
        return (
            passed_along(below_part, 1),
            passed_along(top, -1),
            lax.ppermute(side_part, "side", [(0, 1), (1, 0)]),
        )

    hot, high, weight, payload = prepare(v0, link_rows, link_target, link_weight, link_count)
    spread = spread_out(payload)
    halo = halo_of(*edges(pattern, left_flag, v0, down_hop, right_hop))
    near_part = near(pattern, left_flag, v0, onsite, down_hop, right_hop, halo, pairing)
    landed, near_part = lax.optimization_barrier((spread, near_part))
    one, x, mom, *edge_parts, payload = first(
        pattern, left_flag, v0, landed, hot, high, weight, near_part, down_hop, right_hop
    )
    spread = spread_out(payload)
    halo = halo_of(*edge_parts)
    local_part = local(pattern, x, onsite, down_hop, right_hop)
    landed, local_part, halo = lax.optimization_barrier((spread, local_part, halo))
    two, mom = second(
        pattern, left_flag, v0, one, landed, hot, high, local_part, pairing, mom, halo, down_hop, right_hop
    )
    shape = rand_vectors.shape
    return one.reshape(shape), two.reshape(shape), mom


def solution(mesh):
    both = TILE_AXES + ("sheet", "side")
    mesh = Mesh(mesh.devices.reshape(2, 8, 4, 2, 2, 2), both)
    in_specs = (
        P(None, None, both),
        P(both, None, None),
        P(both, None, None),
        P(both, None, None),
        P(both, None),
        P(both),
        P(both, None),
        P(both, None),
        P(both, None),
        P(both),
    )
    out_specs = (P(None, None, both), P(None, None, both), P(None, None, both))
    return jax.shard_map(shards, mesh=mesh, in_specs=in_specs, out_specs=out_specs, check_vma=False)
```

```python
import jax
import jax.numpy as jnp
from jax import lax
from jax.experimental import pallas as pl
from jax.experimental.pallas import tpu as pltpu
from jax.sharding import Mesh
from jax.sharding import PartitionSpec as P

TILE = 128
TR = 4
TC = 6
ROWS = 64
SITES_DEV = TR * TC * TILE
PEERS = 128
CAP = 8
SLOTS = PEERS * CAP
SPAN = 256
HI = SITES_DEV // SPAN
F32 = jnp.float32
BF16 = jnp.bfloat16
NT = (((1,), (1,)), ((), ()))
NN = (((1,), (0,)), ((), ()))
VMEM_LIMIT = 56 * 1024 * 1024


def dot(a, b, dims=NN):
    return lax.dot_general(a, b, dims, preferred_element_type=F32)


COST = pl.CostEstimate(flops=1000000, bytes_accessed=100000, transcendentals=0)


def params():
    return pltpu.CompilerParams(vmem_limit_bytes=VMEM_LIMIT)


def per_slot(table):
    spread = jnp.broadcast_to(table[None], (PEERS, CAP, PEERS)).reshape(SLOTS, PEERS)
    own = lax.broadcasted_iota(jnp.int32, (SLOTS, PEERS), 0) // CAP == lax.broadcasted_iota(
        jnp.int32, (SLOTS, PEERS), 1
    )
    return dot(jnp.where(own, spread, 0.0).astype(BF16), jnp.ones((PEERS, TILE), BF16))


def build_tables(rows, target, weight, hot_ref, high_ref, weight_ref):
    lane = lax.broadcasted_iota(jnp.int32, (SLOTS, SPAN), 1).astype(F32)
    spread_weight = per_slot(weight)
    weight_ref[...] = spread_weight
    wide_weight = jnp.concatenate([spread_weight, spread_weight], axis=1)
    for end, table in ((0, rows), (1, target)):
        coarse = jnp.floor(table * (1.0 / SPAN))
        low = per_slot(table - coarse * SPAN)
        high_ref[end * SLOTS : (end + 1) * SLOTS, :] = per_slot(coarse)
        same = lane == jnp.concatenate([low, low], axis=1)
        hot_ref[2 * end * SLOTS : (2 * end + 1) * SLOTS, :] = jnp.where(same, 1.0, 0.0).astype(BF16)
        if end == 1:
            hot_ref[SLOTS : 2 * SLOTS, :] = jnp.where(same, wide_weight, 0.0).astype(BF16)


def gather_ends(parts, hot_ref, high_ref, start, chunk):
    lane = lax.broadcasted_iota(jnp.int32, (chunk, TILE), 1)
    half = (lane >= ROWS).astype(F32)
    ends = []
    for end in range(2):
        hot = hot_ref[2 * end * SLOTS + start : 2 * end * SLOTS + start + chunk, :]
        high = high_ref[end * SLOTS + start : end * SLOTS + start + chunk, :] - half
        total = jnp.zeros((chunk, TILE), F32)
        for q in range(HI // 2):
            found = dot(hot, jnp.concatenate([parts[2 * q], parts[2 * q + 1]], axis=0), NT)
            total = jnp.where(high == 2.0 * q, found, total)
        ends.append(total + pltpu.roll(total, ROWS, 1))
    return jnp.where(lane < ROWS, ends[0], ends[1])


def as_payload(ends, weight):
    field = ends.astype(BF16)
    lane = lax.broadcasted_iota(jnp.int32, ends.shape, 1)
    return jnp.where(lane < ROWS, field.astype(F32), field.astype(F32) * weight).astype(BF16)


CHUNK = 256


def gather_payload(x_ref, hot_ref, high_ref, weight_ref, out_ref):
    parts = [x_ref[:, h * SPAN : (h + 1) * SPAN] for h in range(HI)]
    for start in range(0, SLOTS, CHUNK):
        ends = gather_ends(parts, hot_ref, high_ref, start, CHUNK)
        payload = as_payload(ends, weight_ref[start : start + CHUNK, :])
        out_ref[0, start : start + CHUNK, :] = payload
        out_ref[1, start : start + CHUNK, :] = payload


def prepare_kernel(
    x_ref, rows_ref, target_ref, weight_ref, count_ref, hot_ref, high_ref, spread_ref, out_ref
):
    live = lax.broadcasted_iota(jnp.int32, (CAP, PEERS), 0) < count_ref[...]
    weight = jnp.where(live, weight_ref[...].astype(F32), 0.0)
    build_tables(
        rows_ref[...].astype(F32), target_ref[...].astype(F32), weight, hot_ref, high_ref, spread_ref
    )
    gather_payload(x_ref, hot_ref, high_ref, spread_ref, out_ref)


TABLE_SHAPES = (
    jax.ShapeDtypeStruct((3 * SLOTS, SPAN), BF16),
    jax.ShapeDtypeStruct((2 * SLOTS, TILE), F32),
    jax.ShapeDtypeStruct((SLOTS, TILE), F32),
)


def prepare(x, link_rows, link_target, link_weight, link_count):
    return pl.pallas_call(
        prepare_kernel,
        out_shape=TABLE_SHAPES + (jax.ShapeDtypeStruct((2, SLOTS, 2 * ROWS), BF16),),
        compiler_params=params(),
        cost_estimate=COST,
        name="prepare",
    )(x, link_rows.T, link_target.T, link_weight.T, link_count.reshape(1, PEERS))


def write_edges(pattern_ref, left_ref, x_ref, down_ref, right_ref, down_base, top_ref, below_ref, side_ref):
    top_ref[...] = x_ref[:, : TC * TILE]
    for k in range(TC):
        tile = (TR - 1) * TC + k
        keep = pattern_ref[0, tile].astype(F32)
        below_ref[:, k * TILE : (k + 1) * TILE] = keep * dot(
            x_ref[:, tile * TILE : (tile + 1) * TILE], down_ref[down_base + k]
        )
    is_left = left_ref[0] == 1
    for r in range(TR):
        last = r * TC + TC - 1
        keep = pattern_ref[1, last].astype(F32)
        product = keep * dot(x_ref[:, last * TILE : (last + 1) * TILE], right_ref[r, 0])
        first_tile = x_ref[:, r * TC * TILE : (r * TC + 1) * TILE].astype(F32)
        side_ref[:, r * TILE : (r + 1) * TILE] = jnp.where(is_left, product, first_tile)


def edges_kernel(pattern_ref, left_ref, x_ref, down_ref, right_ref, top_ref, below_ref, side_ref):
    write_edges(pattern_ref, left_ref, x_ref, down_ref, right_ref, 0, top_ref, below_ref, side_ref)


EDGE_SHAPES = (
    jax.ShapeDtypeStruct((ROWS, TC * TILE), BF16),
    jax.ShapeDtypeStruct((ROWS, TC * TILE), F32),
    jax.ShapeDtypeStruct((ROWS, TR * TILE), F32),
)
SMEM = pl.BlockSpec(memory_space=pltpu.SMEM)
VMEM = pl.BlockSpec(memory_space=pltpu.VMEM)
DOWN_EDGE = pl.BlockSpec((TC, TILE, TILE), lambda i: (TR - 1, 0, 0))
RIGHT_EDGE = pl.BlockSpec((TR, 1, TILE, TILE), lambda i: (0, TC - 1, 0, 0))


def whole(shape):
    return pl.BlockSpec(shape, lambda i: (0,) * len(shape))


def on_core(value):
    return pltpu.with_memory_space_constraint(value, pltpu.VMEM)


def edges(pattern, left_flag, x, down_hop, right_hop):
    return pl.pallas_call(
        edges_kernel,
        grid=(1,),
        in_specs=[SMEM, SMEM, whole((ROWS, SITES_DEV)), DOWN_EDGE, RIGHT_EDGE],
        out_specs=tuple(whole(s.shape) for s in EDGE_SHAPES),
        out_shape=EDGE_SHAPES,
        compiler_params=params(),
        cost_estimate=COST,
        name="edges",
    )(pattern, left_flag, x, down_hop, right_hop.reshape(TR, TC, TILE, TILE))


def kept(pattern_ref, which, tile, value):
    return jnp.where(pattern_ref[which, tile] == 1, value, jnp.zeros_like(value))


def local_tile(pattern_ref, x_ref, onsite_ref, down_ref, right_ref, tile):
    def block(other):
        return x_ref[:, other * TILE : (other + 1) * TILE]

    r, k = divmod(tile, TC)
    fields = [block(tile)]
    tiles = [onsite_ref[tile]]
    if r > 0:
        fields.append(kept(pattern_ref, 0, tile - TC, block(tile - TC)))
        tiles.append(down_ref[tile - TC])
    if k > 0:
        fields.append(kept(pattern_ref, 1, tile - 1, block(tile - 1)))
        tiles.append(right_ref[tile - 1])
    total = dot(jnp.concatenate(fields, axis=1), jnp.concatenate(tiles, axis=0))
    fields = []
    tiles = []
    if r < TR - 1:
        fields.append(kept(pattern_ref, 0, tile, block(tile + TC)))
        tiles.append(down_ref[tile])
    if k < TC - 1:
        fields.append(kept(pattern_ref, 1, tile, block(tile + 1)))
        tiles.append(right_ref[tile])
    if fields:
        total = total + dot(jnp.concatenate(fields, axis=1), jnp.concatenate(tiles, axis=1), NT)
    return total


def halo_tile(pattern_ref, is_left, down_edge, right_edge, above_ref, below_ref, side_ref, tile):
    r, k = divmod(tile, TC)
    total = None

    def plus(value):
        return value if total is None else total + value

    if r == 0:
        total = plus(above_ref[:, k * TILE : (k + 1) * TILE])
    if r == TR - 1:
        lower = below_ref[:, k * TILE : (k + 1) * TILE]
        total = plus(dot(kept(pattern_ref, 0, tile, lower), down_edge(k), NT))
    if k == 0:
        total = plus(jnp.where(is_left, 0.0, side_ref[:, r * TILE : (r + 1) * TILE]))
    if k == TC - 1:
        righter = jnp.where(is_left, side_ref[:, r * TILE : (r + 1) * TILE], 0.0).astype(BF16)
        total = plus(dot(kept(pattern_ref, 1, tile, righter), right_edge(r), NT))
    return total


def signed(value):
    return jnp.where(lax.broadcasted_iota(jnp.int32, value.shape, 0) < ROWS // 2, value, -value)


def swapped(value):
    return jnp.concatenate([value[ROWS // 2 :], value[: ROWS // 2]], axis=0)


def vector_mean(value):
    comps = value.reshape(4, 16, value.shape[-1])
    return jnp.sum(comps, axis=1) * (1.0 / 16.0)


SCATTER_SCRATCH = [pltpu.VMEM((HI * ROWS, 2 * SLOTS), BF16), pltpu.VMEM((HI * ROWS, SPAN), F32)]


def scatter_into(landed, hot_ref, high_ref, mask_ref, total_ref):
    turned = landed.astype(F32).T.astype(BF16)
    high_send = high_ref[0:SLOTS, :].T.astype(BF16)[:ROWS]
    high_recv = high_ref[SLOTS : 2 * SLOTS, :].T.astype(BF16)[:ROWS]
    zero = jnp.zeros((ROWS, SLOTS), BF16)
    for h in range(HI):
        rows = slice(h * ROWS, (h + 1) * ROWS)
        mask_ref[rows, 0:SLOTS] = jnp.where(high_send == BF16(h), turned[ROWS:], zero)
        mask_ref[rows, SLOTS : 2 * SLOTS] = jnp.where(high_recv == BF16(h), turned[:ROWS], zero)
    group = 4
    for start in range(0, HI, group):
        total_ref[start * ROWS : (start + group) * ROWS, :] = dot(
            mask_ref[start * ROWS : (start + group) * ROWS, :], hot_ref[0 : 2 * SLOTS, :]
        )


def whole_hop(pattern_ref, left_ref, local_ref, total_ref, above_ref, below_ref, side_ref, down_ref, right_ref, tile):
    h, part = divmod(tile, SPAN // TILE)
    hop = local_ref[:, tile * TILE : (tile + 1) * TILE]
    hop = hop + total_ref[h * ROWS : (h + 1) * ROWS, part * TILE : (part + 1) * TILE]
    halo = halo_tile(
        pattern_ref, left_ref[0] == 1, lambda k: down_ref[k], lambda r: right_ref[r, 0],
        above_ref, below_ref, side_ref, tile,
    )
    return hop if halo is None else hop + halo


def first_kernel(
    pattern_ref, left_ref, landed_ref, above_ref, below_ref, side_ref,
    v0_ref, hot_ref, high_ref, weight_ref, local_ref, pairing_ref, down_ref, right_ref,
    one_ref, x_ref, mom_ref, top_ref, lower_ref, beside_ref, out_ref, mask_ref, total_ref,
):
    scatter_into(landed_ref[left_ref[1]], hot_ref, high_ref, mask_ref, total_ref)
    for tile in range(TR * TC):
        cols = slice(tile * TILE, (tile + 1) * TILE)
        hop = whole_hop(
            pattern_ref, left_ref, local_ref, total_ref, above_ref, below_ref, side_ref, down_ref, right_ref, tile
        )
        v0 = v0_ref[:, cols].astype(F32)
        one = signed(hop) + pairing_ref[:, cols] * swapped(v0)
        one_ref[:, cols] = one
        x_ref[:, cols] = one.astype(BF16)
        mom_ref[0, :, cols] = vector_mean(v0 * v0)
        mom_ref[1, :, cols] = vector_mean(v0 * one)
    gather_payload(x_ref, hot_ref, high_ref, weight_ref, out_ref)
    write_edges(pattern_ref, left_ref, x_ref, down_ref, right_ref, 0, top_ref, lower_ref, beside_ref)


def first(pattern, left_flag, v0, landed, tables, local_part, pairing, halo, down_hop, right_hop):
    shapes = (
        jax.ShapeDtypeStruct((ROWS, SITES_DEV), F32),
        jax.ShapeDtypeStruct((ROWS, SITES_DEV), BF16),
        jax.ShapeDtypeStruct((2, 4, SITES_DEV), F32),
    ) + EDGE_SHAPES + (jax.ShapeDtypeStruct((2, SLOTS, 2 * ROWS), BF16),)
    resident = [on_core(a) for a in (landed, *halo)]
    arrays = (v0, *tables, local_part, pairing)
    return pl.pallas_call(
        first_kernel,
        grid=(1,),
        in_specs=[SMEM, SMEM] + [VMEM] * 4 + [whole(a.shape) for a in arrays] + [DOWN_EDGE, RIGHT_EDGE],
        out_specs=tuple(whole(s.shape) for s in shapes),
        out_shape=shapes,
        scratch_shapes=SCATTER_SCRATCH,
        compiler_params=params(),
        cost_estimate=COST,
        name="first",
    )(pattern, left_flag, *resident, *arrays, down_hop, right_hop.reshape(TR, TC, TILE, TILE))


def local_kernel(pattern_ref, x_ref, onsite_ref, down_ref, right_ref, out_ref):
    for tile in range(TR * TC):
        out_ref[:, tile * TILE : (tile + 1) * TILE] = local_tile(
            pattern_ref, x_ref, onsite_ref, down_ref, right_ref, tile
        )


def local(pattern, x, onsite, down_hop, right_hop):
    return pl.pallas_call(
        local_kernel,
        in_specs=[SMEM] + [VMEM] * 4,
        out_shape=jax.ShapeDtypeStruct((ROWS, SITES_DEV), F32),
        compiler_params=params(),
        cost_estimate=COST,
        name="local",
    )(pattern, x, onsite, down_hop, right_hop)


def second_kernel(
    pattern_ref, left_ref, landed_ref, above_ref, below_ref, side_ref,
    v0_ref, one_ref, hot_ref, high_ref, local_ref, pairing_ref, mom_in_ref, down_ref, right_ref,
    two_ref, mom_ref, mask_ref, total_ref,
):
    scatter_into(landed_ref[left_ref[1]], hot_ref, high_ref, mask_ref, total_ref)
    mom_ref[0:2] = mom_in_ref[...]
    for tile in range(TR * TC):
        cols = slice(tile * TILE, (tile + 1) * TILE)
        hop = whole_hop(
            pattern_ref, left_ref, local_ref, total_ref, above_ref, below_ref, side_ref, down_ref, right_ref, tile
        )
        v0 = v0_ref[:, cols].astype(F32)
        two = 2.0 * (signed(hop) + pairing_ref[:, cols] * swapped(one_ref[:, cols])) - v0
        two_ref[:, cols] = two
        mom_ref[2, :, cols] = vector_mean(v0 * two)


def second(pattern, left_flag, v0, one, landed, hot, high, local_part, pairing, mom, halo, down_hop, right_hop):
    shapes = (
        jax.ShapeDtypeStruct((ROWS, SITES_DEV), F32),
        jax.ShapeDtypeStruct((3, 4, SITES_DEV), F32),
    )
    resident = [on_core(a) for a in (landed, *halo)]
    arrays = (v0, one, hot, high, local_part, pairing, mom)
    return pl.pallas_call(
        second_kernel,
        grid=(1,),
        in_specs=[SMEM, SMEM] + [VMEM] * 4 + [whole(a.shape) for a in arrays] + [DOWN_EDGE, RIGHT_EDGE],
        out_specs=tuple(whole(s.shape) for s in shapes),
        out_shape=shapes,
        scratch_shapes=SCATTER_SCRATCH,
        compiler_params=params(),
        cost_estimate=COST,
        name="second",
    )(pattern, left_flag, *resident, *arrays, down_hop, right_hop.reshape(TR, TC, TILE, TILE))


TILE_AXES = ("z_low", "y", "x", "core")


def passed_along(value, by):
    length = PEERS
    pairs = [(i, i + by) for i in range(length) if 0 <= i + by < length]
    return lax.ppermute(value, TILE_AXES, pairs)


def spread_out(payload):
    spread = lax.all_to_all(
        payload.reshape(2 * PEERS, CAP, 2 * ROWS), ("sheet",) + TILE_AXES, split_axis=0, concat_axis=0, tiled=True
    )
    return spread.reshape(2, SLOTS, 2 * ROWS)


def shards(
    rand_vectors,
    onsite,
    down_hop,
    right_hop,
    pattern,
    pairing,
    link_rows,
    link_target,
    link_weight,
    link_count,
):
    v0 = rand_vectors.reshape(ROWS, SITES_DEV)
    pairing = pairing.reshape(1, SITES_DEV)
    pattern = pattern.T
    left_flag = jnp.stack([1 - lax.axis_index("side"), 1 - lax.axis_index("sheet")]).astype(jnp.int32)

    def halo_of(top, below_part, side_part):
        return (
            passed_along(below_part, 1),
            passed_along(top, -1),
            lax.ppermute(side_part, "side", [(0, 1), (1, 0)]),
        )

    *tables, payload = prepare(v0, link_rows, link_target, link_weight, link_count)
    hot, high, weight = tables
    spread = spread_out(payload)
    halo = halo_of(*edges(pattern, left_flag, v0, down_hop, right_hop))
    local_part = local(pattern, v0, onsite, down_hop, right_hop)
    landed, local_part, halo = lax.optimization_barrier((spread, local_part, halo))
    one, x, mom, *edge_parts, payload = first(
        pattern, left_flag, v0, landed, tables, local_part, pairing, halo, down_hop, right_hop
    )
    spread = spread_out(payload)
    halo = halo_of(*edge_parts)
    local_part = local(pattern, x, onsite, down_hop, right_hop)
    landed, local_part, halo = lax.optimization_barrier((spread, local_part, halo))
    two, mom = second(
        pattern, left_flag, v0, one, landed, hot, high, local_part, pairing, mom, halo, down_hop, right_hop
    )
    shape = rand_vectors.shape
    return one.reshape(shape), two.reshape(shape), mom


def solution(mesh):
    both = TILE_AXES + ("sheet", "side")
    mesh = Mesh(mesh.devices.reshape(2, 8, 4, 2, 2, 2), both)
    in_specs = (
        P(None, None, both),
        P(both, None, None),
        P(both, None, None),
        P(both, None, None),
        P(both, None),
        P(both),
        P(both, None),
        P(both, None),
        P(both, None),
        P(both),
    )
    out_specs = (P(None, None, both), P(None, None, both), P(None, None, both))
    return jax.shard_map(shards, mesh=mesh, in_specs=in_specs, out_specs=out_specs, check_vma=False)
```

```python
import jax
import jax.numpy as jnp
from jax import lax
from jax.experimental import pallas as pl
from jax.experimental.pallas import tpu as pltpu
from jax.sharding import Mesh
from jax.sharding import PartitionSpec as P

TILE = 128
TR = 4
TC = 6
ROWS = 64
SITES_DEV = TR * TC * TILE
PEERS = 128
CAP = 8
SLOTS = PEERS * CAP
SPAN = 256
HI = SITES_DEV // SPAN
F32 = jnp.float32
BF16 = jnp.bfloat16
NT = (((1,), (1,)), ((), ()))
NN = (((1,), (0,)), ((), ()))
VMEM_LIMIT = 56 * 1024 * 1024


def dot(a, b, dims=NN):
    return lax.dot_general(a, b, dims, preferred_element_type=F32)


COST = pl.CostEstimate(flops=1000000, bytes_accessed=100000, transcendentals=0)


def params():
    return pltpu.CompilerParams(vmem_limit_bytes=VMEM_LIMIT)


def per_slot(table):
    spread = jnp.broadcast_to(table[None], (PEERS, CAP, PEERS)).reshape(SLOTS, PEERS)
    own = lax.broadcasted_iota(jnp.int32, (SLOTS, PEERS), 0) // CAP == lax.broadcasted_iota(
        jnp.int32, (SLOTS, PEERS), 1
    )
    return dot(jnp.where(own, spread, 0.0).astype(BF16), jnp.ones((PEERS, TILE), BF16))


def build_tables(rows, target, weight, hot_ref, high_ref, weight_ref):
    lane = lax.broadcasted_iota(jnp.int32, (SLOTS, SPAN), 1).astype(F32)
    spread_weight = per_slot(weight)
    weight_ref[...] = spread_weight
    wide_weight = jnp.concatenate([spread_weight, spread_weight], axis=1)
    for end, table in ((0, rows), (1, target)):
        coarse = jnp.floor(table * (1.0 / SPAN))
        low = per_slot(table - coarse * SPAN)
        high_ref[end * SLOTS : (end + 1) * SLOTS, :] = per_slot(coarse)
        same = lane == jnp.concatenate([low, low], axis=1)
        hot_ref[2 * end * SLOTS : (2 * end + 1) * SLOTS, :] = jnp.where(same, 1.0, 0.0).astype(BF16)
        if end == 1:
            hot_ref[SLOTS : 2 * SLOTS, :] = jnp.where(same, wide_weight, 0.0).astype(BF16)


def gather_ends(parts, hot_ref, high_ref, start, chunk):
    lane = lax.broadcasted_iota(jnp.int32, (chunk, TILE), 1)
    half = (lane >= ROWS).astype(F32)
    ends = []
    for end in range(2):
        hot = hot_ref[2 * end * SLOTS + start : 2 * end * SLOTS + start + chunk, :]
        high = high_ref[end * SLOTS + start : end * SLOTS + start + chunk, :] - half
        total = jnp.zeros((chunk, TILE), F32)
        for q in range(HI // 2):
            found = dot(hot, jnp.concatenate([parts[2 * q], parts[2 * q + 1]], axis=0), NT)
            total = jnp.where(high == 2.0 * q, found, total)
        ends.append(total + pltpu.roll(total, ROWS, 1))
    return jnp.where(lane < ROWS, ends[0], ends[1])


def as_payload(ends, weight):
    field = ends.astype(BF16)
    lane = lax.broadcasted_iota(jnp.int32, ends.shape, 1)
    return jnp.where(lane < ROWS, field.astype(F32), field.astype(F32) * weight).astype(BF16)


CHUNK = 256


def gather_payload(x_ref, hot_ref, high_ref, weight_ref, out_ref):
    parts = [x_ref[:, h * SPAN : (h + 1) * SPAN] for h in range(HI)]
    for start in range(0, SLOTS, CHUNK):
        ends = gather_ends(parts, hot_ref, high_ref, start, CHUNK)
        payload = as_payload(ends, weight_ref[start : start + CHUNK, :])
        out_ref[0, start : start + CHUNK, :] = payload
        out_ref[1, start : start + CHUNK, :] = payload


def prepare_kernel(
    x_ref, rows_ref, target_ref, weight_ref, count_ref, hot_ref, high_ref, spread_ref, out_ref
):
    live = lax.broadcasted_iota(jnp.int32, (CAP, PEERS), 0) < count_ref[...]
    weight = jnp.where(live, weight_ref[...].astype(F32), 0.0)
    build_tables(
        rows_ref[...].astype(F32), target_ref[...].astype(F32), weight, hot_ref, high_ref, spread_ref
    )
    gather_payload(x_ref, hot_ref, high_ref, spread_ref, out_ref)


TABLE_SHAPES = (
    pltpu.VMEM((3 * SLOTS, SPAN), BF16),
    pltpu.VMEM((2 * SLOTS, TILE), F32),
    jax.ShapeDtypeStruct((SLOTS, TILE), F32),
)


def prepare(x, link_rows, link_target, link_weight, link_count):
    return pl.pallas_call(
        prepare_kernel,
        out_shape=TABLE_SHAPES + (jax.ShapeDtypeStruct((2, SLOTS, 2 * ROWS), BF16),),
        compiler_params=params(),
        cost_estimate=COST,
        name="prepare",
    )(x, link_rows.T, link_target.T, link_weight.T, link_count.reshape(1, PEERS))


def write_edges(pattern_ref, left_ref, x_ref, down_ref, right_ref, down_base, top_ref, below_ref, side_ref):
    top_ref[...] = x_ref[:, : TC * TILE]
    for k in range(TC):
        tile = (TR - 1) * TC + k
        keep = pattern_ref[0, tile].astype(F32)
        product = keep * dot(x_ref[:, tile * TILE : (tile + 1) * TILE], down_ref[down_base + k])
        below_ref[:, k * TILE : (k + 1) * TILE] = product.astype(BF16)
    is_left = left_ref[0] == 1
    for r in range(TR):
        last = r * TC + TC - 1
        keep = pattern_ref[1, last].astype(F32)
        product = keep * dot(x_ref[:, last * TILE : (last + 1) * TILE], right_ref[r, 0])
        first_tile = x_ref[:, r * TC * TILE : (r * TC + 1) * TILE]
        side_ref[:, r * TILE : (r + 1) * TILE] = jnp.where(is_left, product.astype(BF16), first_tile)


def edges_kernel(pattern_ref, left_ref, x_ref, down_ref, right_ref, top_ref, below_ref, side_ref):
    write_edges(pattern_ref, left_ref, x_ref, down_ref, right_ref, 0, top_ref, below_ref, side_ref)


EDGE_SHAPES = (
    jax.ShapeDtypeStruct((ROWS, TC * TILE), BF16),
    jax.ShapeDtypeStruct((ROWS, TC * TILE), BF16),
    jax.ShapeDtypeStruct((ROWS, TR * TILE), BF16),
)
SMEM = pl.BlockSpec(memory_space=pltpu.SMEM)
VMEM = pl.BlockSpec(memory_space=pltpu.VMEM)
DOWN_EDGE = pl.BlockSpec((TC, TILE, TILE), lambda i: (TR - 1, 0, 0))
RIGHT_EDGE = pl.BlockSpec((TR, 1, TILE, TILE), lambda i: (0, TC - 1, 0, 0))


def whole(shape):
    return pl.BlockSpec(shape, lambda i: (0,) * len(shape))


def on_core(value):
    return pltpu.with_memory_space_constraint(value, pltpu.VMEM)


def edges(pattern, left_flag, x, down_hop, right_hop):
    return pl.pallas_call(
        edges_kernel,
        grid=(1,),
        in_specs=[SMEM, SMEM, whole((ROWS, SITES_DEV)), DOWN_EDGE, RIGHT_EDGE],
        out_specs=tuple(whole(s.shape) for s in EDGE_SHAPES),
        out_shape=EDGE_SHAPES,
        compiler_params=params(),
        cost_estimate=COST,
        name="edges",
    )(pattern, left_flag, x, down_hop, right_hop.reshape(TR, TC, TILE, TILE))


def kept(pattern_ref, which, tile, value):
    return jnp.where(pattern_ref[which, tile] == 1, value, jnp.zeros_like(value))


def local_tile(pattern_ref, x_ref, onsite_ref, down_ref, right_ref, tile):
    def block(other):
        return x_ref[:, other * TILE : (other + 1) * TILE]

    r, k = divmod(tile, TC)
    fields = [block(tile)]
    tiles = [onsite_ref[tile]]
    if r > 0:
        fields.append(kept(pattern_ref, 0, tile - TC, block(tile - TC)))
        tiles.append(down_ref[tile - TC])
    if k > 0:
        fields.append(kept(pattern_ref, 1, tile - 1, block(tile - 1)))
        tiles.append(right_ref[tile - 1])
    total = dot(jnp.concatenate(fields, axis=1), jnp.concatenate(tiles, axis=0))
    fields = []
    tiles = []
    if r < TR - 1:
        fields.append(kept(pattern_ref, 0, tile, block(tile + TC)))
        tiles.append(down_ref[tile])
    if k < TC - 1:
        fields.append(kept(pattern_ref, 1, tile, block(tile + 1)))
        tiles.append(right_ref[tile])
    if fields:
        total = total + dot(jnp.concatenate(fields, axis=1), jnp.concatenate(tiles, axis=1), NT)
    return total


def halo_tile(pattern_ref, is_left, down_edge, right_edge, above_ref, below_ref, side_ref, tile):
    r, k = divmod(tile, TC)
    total = None

    def plus(value):
        return value if total is None else total + value

    if r == 0:
        total = plus(above_ref[:, k * TILE : (k + 1) * TILE].astype(F32))
    if r == TR - 1:
        lower = below_ref[:, k * TILE : (k + 1) * TILE]
        total = plus(dot(kept(pattern_ref, 0, tile, lower), down_edge(k), NT))
    if k == 0:
        total = plus(jnp.where(is_left, 0.0, side_ref[:, r * TILE : (r + 1) * TILE].astype(F32)))
    if k == TC - 1:
        righter = side_ref[:, r * TILE : (r + 1) * TILE]
        righter = jnp.where(is_left, righter, jnp.zeros_like(righter))
        total = plus(dot(kept(pattern_ref, 1, tile, righter), right_edge(r), NT))
    return total


def signed(value):
    return jnp.where(lax.broadcasted_iota(jnp.int32, value.shape, 0) < ROWS // 2, value, -value)


def swapped(value):
    return jnp.concatenate([value[ROWS // 2 :], value[: ROWS // 2]], axis=0)


def vector_mean(value):
    comps = value.reshape(4, 16, value.shape[-1])
    return jnp.sum(comps, axis=1) * (1.0 / 16.0)


SCATTER_SCRATCH = [pltpu.VMEM((HI * ROWS, 2 * SLOTS), BF16), pltpu.VMEM((HI * ROWS, SPAN), F32)]


def scatter_into(landed, hot_ref, high_ref, mask_ref, total_ref):
    turned = landed.astype(F32).T.astype(BF16)
    high_send = high_ref[0:SLOTS, :].T.astype(BF16)[:ROWS]
    high_recv = high_ref[SLOTS : 2 * SLOTS, :].T.astype(BF16)[:ROWS]
    zero = jnp.zeros((ROWS, SLOTS), BF16)
    for h in range(HI):
        rows = slice(h * ROWS, (h + 1) * ROWS)
        mask_ref[rows, 0:SLOTS] = jnp.where(high_send == BF16(h), turned[ROWS:], zero)
        mask_ref[rows, SLOTS : 2 * SLOTS] = jnp.where(high_recv == BF16(h), turned[:ROWS], zero)
    group = 4
    for start in range(0, HI, group):
        total_ref[start * ROWS : (start + group) * ROWS, :] = dot(
            mask_ref[start * ROWS : (start + group) * ROWS, :], hot_ref[0 : 2 * SLOTS, :]
        )


def whole_hop(pattern_ref, left_ref, local_ref, total_ref, above_ref, below_ref, side_ref, down_ref, right_ref, tile):
    h, part = divmod(tile, SPAN // TILE)
    hop = local_ref[:, tile * TILE : (tile + 1) * TILE]
    hop = hop + total_ref[h * ROWS : (h + 1) * ROWS, part * TILE : (part + 1) * TILE]
    halo = halo_tile(
        pattern_ref, left_ref[0] == 1, lambda k: down_ref[k], lambda r: right_ref[r, 0],
        above_ref, below_ref, side_ref, tile,
    )
    return hop if halo is None else hop + halo


def first_kernel(
    pattern_ref, left_ref, landed_ref, above_ref, below_ref, side_ref, hot_ref, high_ref,
    v0_ref, weight_ref, local_ref, pairing_ref, down_ref, right_ref,
    one_ref, x_ref, mom_ref, top_ref, lower_ref, beside_ref, out_ref, mask_ref, total_ref,
):
    scatter_into(landed_ref[left_ref[1]], hot_ref, high_ref, mask_ref, total_ref)
    for tile in range(TR * TC):
        cols = slice(tile * TILE, (tile + 1) * TILE)
        hop = whole_hop(
            pattern_ref, left_ref, local_ref, total_ref, above_ref, below_ref, side_ref, down_ref, right_ref, tile
        )
        v0 = v0_ref[:, cols].astype(F32)
        one = signed(hop) + pairing_ref[:, cols] * swapped(v0)
        one_ref[:, cols] = one
        x_ref[:, cols] = one.astype(BF16)
        mom_ref[0, :, cols] = vector_mean(v0 * v0)
        mom_ref[1, :, cols] = vector_mean(v0 * one)
    gather_payload(x_ref, hot_ref, high_ref, weight_ref, out_ref)
    write_edges(pattern_ref, left_ref, x_ref, down_ref, right_ref, 0, top_ref, lower_ref, beside_ref)


def first(pattern, left_flag, v0, landed, tables, local_part, pairing, halo, down_hop, right_hop):
    shapes = (
        jax.ShapeDtypeStruct((ROWS, SITES_DEV), F32),
        jax.ShapeDtypeStruct((ROWS, SITES_DEV), BF16),
        jax.ShapeDtypeStruct((2, 4, SITES_DEV), F32),
    ) + EDGE_SHAPES + (jax.ShapeDtypeStruct((2, SLOTS, 2 * ROWS), BF16),)
    hot, high, weight = tables
    resident = [on_core(a) for a in (landed, *halo, hot, high)]
    arrays = (v0, weight, local_part, pairing)
    return pl.pallas_call(
        first_kernel,
        grid=(1,),
        in_specs=[SMEM, SMEM] + [VMEM] * len(resident) + [whole(a.shape) for a in arrays] + [DOWN_EDGE, RIGHT_EDGE],
        out_specs=tuple(whole(s.shape) for s in shapes),
        out_shape=shapes,
        scratch_shapes=SCATTER_SCRATCH,
        compiler_params=params(),
        cost_estimate=COST,
        name="first",
    )(pattern, left_flag, *resident, *arrays, down_hop, right_hop.reshape(TR, TC, TILE, TILE))


def local_kernel(pattern_ref, x_ref, onsite_ref, down_ref, right_ref, out_ref):
    for tile in range(TR * TC):
        out_ref[:, tile * TILE : (tile + 1) * TILE] = local_tile(
            pattern_ref, x_ref, onsite_ref, down_ref, right_ref, tile
        )


def local(pattern, x, onsite, down_hop, right_hop):
    return pl.pallas_call(
        local_kernel,
        in_specs=[SMEM] + [VMEM] * 4,
        out_shape=jax.ShapeDtypeStruct((ROWS, SITES_DEV), F32),
        compiler_params=params(),
        cost_estimate=COST,
        name="local",
    )(pattern, x, onsite, down_hop, right_hop)


def second_kernel(
    pattern_ref, left_ref, landed_ref, above_ref, below_ref, side_ref, hot_ref, high_ref,
    v0_ref, one_ref, local_ref, pairing_ref, mom_in_ref, down_ref, right_ref,
    two_ref, mom_ref, mask_ref, total_ref,
):
    scatter_into(landed_ref[left_ref[1]], hot_ref, high_ref, mask_ref, total_ref)
    mom_ref[0:2] = mom_in_ref[...]
    for tile in range(TR * TC):
        cols = slice(tile * TILE, (tile + 1) * TILE)
        hop = whole_hop(
            pattern_ref, left_ref, local_ref, total_ref, above_ref, below_ref, side_ref, down_ref, right_ref, tile
        )
        v0 = v0_ref[:, cols].astype(F32)
        two = 2.0 * (signed(hop) + pairing_ref[:, cols] * swapped(one_ref[:, cols])) - v0
        two_ref[:, cols] = two
        mom_ref[2, :, cols] = vector_mean(v0 * two)


def second(pattern, left_flag, v0, one, landed, hot, high, local_part, pairing, mom, halo, down_hop, right_hop):
    shapes = (
        jax.ShapeDtypeStruct((ROWS, SITES_DEV), F32),
        jax.ShapeDtypeStruct((3, 4, SITES_DEV), F32),
    )
    resident = [on_core(a) for a in (landed, *halo, hot, high)]
    arrays = (v0, one, local_part, pairing, mom)
    return pl.pallas_call(
        second_kernel,
        grid=(1,),
        in_specs=[SMEM, SMEM] + [VMEM] * len(resident) + [whole(a.shape) for a in arrays] + [DOWN_EDGE, RIGHT_EDGE],
        out_specs=tuple(whole(s.shape) for s in shapes),
        out_shape=shapes,
        scratch_shapes=SCATTER_SCRATCH,
        compiler_params=params(),
        cost_estimate=COST,
        name="second",
    )(pattern, left_flag, *resident, *arrays, down_hop, right_hop.reshape(TR, TC, TILE, TILE))


TILE_AXES = ("z_low", "y", "x", "core")


def passed_along(value, by):
    length = PEERS
    pairs = [(i, i + by) for i in range(length) if 0 <= i + by < length]
    return lax.ppermute(value, TILE_AXES, pairs)


def spread_out(payload):
    spread = lax.all_to_all(
        payload.reshape(2 * PEERS, CAP, 2 * ROWS), ("sheet",) + TILE_AXES, split_axis=0, concat_axis=0, tiled=True
    )
    return spread.reshape(2, SLOTS, 2 * ROWS)


def shards(
    rand_vectors,
    onsite,
    down_hop,
    right_hop,
    pattern,
    pairing,
    link_rows,
    link_target,
    link_weight,
    link_count,
):
    v0 = rand_vectors.reshape(ROWS, SITES_DEV)
    pairing = pairing.reshape(1, SITES_DEV)
    pattern = pattern.T
    left_flag = jnp.stack([1 - lax.axis_index("side"), 1 - lax.axis_index("sheet")]).astype(jnp.int32)

    def halo_of(top, below_part, side_part):
        return (
            passed_along(below_part, 1),
            passed_along(top, -1),
            lax.ppermute(side_part, "side", [(0, 1), (1, 0)]),
        )

    *tables, payload = prepare(v0, link_rows, link_target, link_weight, link_count)
    hot, high, weight = tables
    spread = spread_out(payload)
    halo = halo_of(*edges(pattern, left_flag, v0, down_hop, right_hop))
    local_part = local(pattern, v0, onsite, down_hop, right_hop)
    landed, local_part, halo = lax.optimization_barrier((spread, local_part, halo))
    one, x, mom, *edge_parts, payload = first(
        pattern, left_flag, v0, landed, tables, local_part, pairing, halo, down_hop, right_hop
    )
    spread = spread_out(payload)
    halo = halo_of(*edge_parts)
    local_part = local(pattern, x, onsite, down_hop, right_hop)
    landed, local_part, halo = lax.optimization_barrier((spread, local_part, halo))
    two, mom = second(
        pattern, left_flag, v0, one, landed, hot, high, local_part, pairing, mom, halo, down_hop, right_hop
    )
    shape = rand_vectors.shape
    return one.reshape(shape), two.reshape(shape), mom


def solution(mesh):
    both = TILE_AXES + ("sheet", "side")
    mesh = Mesh(mesh.devices.reshape(2, 8, 4, 2, 2, 2), both)
    in_specs = (
        P(None, None, both),
        P(both, None, None),
        P(both, None, None),
        P(both, None, None),
        P(both, None),
        P(both),
        P(both, None),
        P(both, None),
        P(both, None),
        P(both),
    )
    out_specs = (P(None, None, both), P(None, None, both), P(None, None, both))
    return jax.shard_map(shards, mesh=mesh, in_specs=in_specs, out_specs=out_specs, check_vma=False)
```

```python
import jax
import jax.numpy as jnp
from jax import lax
from jax.experimental import pallas as pl
from jax.experimental.pallas import tpu as pltpu
from jax.sharding import Mesh
from jax.sharding import PartitionSpec as P

TILE = 128
TR = 4
TC = 6
ROWS = 64
SITES_DEV = TR * TC * TILE
PEERS = 128
CAP = 8
SLOTS = PEERS * CAP
SPAN = 256
HI = SITES_DEV // SPAN
F32 = jnp.float32
BF16 = jnp.bfloat16
NT = (((1,), (1,)), ((), ()))
NN = (((1,), (0,)), ((), ()))
VMEM_LIMIT = 56 * 1024 * 1024


def dot(a, b, dims=NN):
    return lax.dot_general(a, b, dims, preferred_element_type=F32)


COST = pl.CostEstimate(flops=1000000, bytes_accessed=100000, transcendentals=0)


def params():
    return pltpu.CompilerParams(vmem_limit_bytes=VMEM_LIMIT)


def picked(table):
    spread = jnp.broadcast_to(table[None], (PEERS, CAP, PEERS)).reshape(SLOTS, PEERS)
    own = lax.broadcasted_iota(jnp.int32, (SLOTS, PEERS), 0) // CAP == lax.broadcasted_iota(
        jnp.int32, (SLOTS, PEERS), 1
    )
    return jnp.where(own, spread, 0.0).astype(BF16)


def per_slot(table):
    return dot(picked(table), jnp.ones((PEERS, TILE), BF16))


def build_tables(rows, target, weight, hot_ref, high_ref, across_ref, weight_ref):
    lane = lax.broadcasted_iota(jnp.int32, (SLOTS, SPAN), 1).astype(F32)
    spread_weight = per_slot(weight)
    weight_ref[...] = spread_weight
    wide_weight = jnp.concatenate([spread_weight, spread_weight], axis=1)
    for end, table in ((0, rows), (1, target)):
        coarse = jnp.floor(table * (1.0 / SPAN))
        low = per_slot(table - coarse * SPAN)
        coarse = picked(coarse)
        high_ref[end * SLOTS : (end + 1) * SLOTS, :] = dot(coarse, jnp.ones((PEERS, TILE), BF16)).astype(BF16)
        across_ref[:, end * SLOTS : (end + 1) * SLOTS] = dot(jnp.ones((ROWS, PEERS), BF16), coarse, NT).astype(BF16)
        same = lane == jnp.concatenate([low, low], axis=1)
        hot_ref[2 * end * SLOTS : (2 * end + 1) * SLOTS, :] = jnp.where(same, 1.0, 0.0).astype(BF16)
        if end == 1:
            hot_ref[SLOTS : 2 * SLOTS, :] = jnp.where(same, wide_weight, 0.0).astype(BF16)


def gather_ends(parts, hot_ref, high_ref, start, chunk):
    lane = lax.broadcasted_iota(jnp.int32, (chunk, TILE), 1)
    half = (lane >= ROWS).astype(F32)
    ends = []
    for end in range(2):
        hot = hot_ref[2 * end * SLOTS + start : 2 * end * SLOTS + start + chunk, :]
        high = high_ref[end * SLOTS + start : end * SLOTS + start + chunk, :].astype(F32) - half
        total = jnp.zeros((chunk, TILE), F32)
        for q in range(HI // 2):
            found = dot(hot, jnp.concatenate([parts[2 * q], parts[2 * q + 1]], axis=0), NT)
            total = jnp.where(high == 2.0 * q, found, total)
        ends.append(total + pltpu.roll(total, ROWS, 1))
    return jnp.where(lane < ROWS, ends[0], ends[1])


def as_payload(ends, weight):
    field = ends.astype(BF16)
    lane = lax.broadcasted_iota(jnp.int32, ends.shape, 1)
    return jnp.where(lane < ROWS, field.astype(F32), field.astype(F32) * weight).astype(BF16)


CHUNK = 256


CHUNKS = SLOTS // CHUNK


def started(source, target, semaphore):
    copy = pltpu.make_async_copy(source, target, semaphore)
    copy.start()
    return copy


def gather_payload(x_ref, hot_ref, high_ref, weight_ref, out_ref, stage_ref, sems):
    parts = [x_ref[:, h * SPAN : (h + 1) * SPAN] for h in range(HI)]
    copies = []
    for i in range(CHUNKS):
        rows = pl.ds(i * CHUNK, CHUNK)
        ends = gather_ends(parts, hot_ref, high_ref, i * CHUNK, CHUNK)
        stage_ref[i * CHUNK : (i + 1) * CHUNK, :] = as_payload(ends, weight_ref[i * CHUNK : (i + 1) * CHUNK, :])
        for sheet in range(2):
            copies.append(started(stage_ref.at[rows, :], out_ref.at[sheet, rows, :], sems.at[sheet, i]))
    return copies


STAGE_SCRATCH = [pltpu.VMEM((SLOTS, 2 * ROWS), BF16), pltpu.SemaphoreType.DMA((2, CHUNKS))]
ANY = pl.BlockSpec(memory_space=pl.ANY)
SMEM = pl.BlockSpec(memory_space=pltpu.SMEM)
VMEM = pl.BlockSpec(memory_space=pltpu.VMEM)


def span(ref, h):
    return ref.at[:, pl.ds(h * SPAN, SPAN)]


def prepare_kernel(
    x_ref, rows_ref, target_ref, weight_ref, count_ref, hot_ref, high_ref, across_ref, spread_ref, out_ref,
    x_buf, x_sem, stage_ref, stage_sems,
):
    x_copy = started(x_ref, x_buf, x_sem)
    live = lax.broadcasted_iota(jnp.int32, (CAP, PEERS), 0) < count_ref[...]
    weight = jnp.where(live, weight_ref[...].astype(F32), 0.0)
    build_tables(
        rows_ref[...].astype(F32), target_ref[...].astype(F32), weight, hot_ref, high_ref, across_ref, spread_ref
    )
    x_copy.wait()
    for copy in gather_payload(x_buf, hot_ref, high_ref, spread_ref, out_ref, stage_ref, stage_sems):
        copy.wait()


TABLE_SHAPES = (
    pltpu.VMEM((3 * SLOTS, SPAN), BF16),
    pltpu.VMEM((2 * SLOTS, TILE), BF16),
    pltpu.VMEM((ROWS, 2 * SLOTS), BF16),
    jax.ShapeDtypeStruct((SLOTS, TILE), F32),
)


def prepare(x, link_rows, link_target, link_weight, link_count):
    return pl.pallas_call(
        prepare_kernel,
        in_specs=[ANY] + [VMEM] * 4,
        out_specs=(VMEM,) * len(TABLE_SHAPES) + (ANY,),
        out_shape=TABLE_SHAPES + (jax.ShapeDtypeStruct((2, SLOTS, 2 * ROWS), BF16),),
        scratch_shapes=[pltpu.VMEM((ROWS, SITES_DEV), BF16), pltpu.SemaphoreType.DMA(())] + STAGE_SCRATCH,
        compiler_params=params(),
        cost_estimate=COST,
        name="prepare",
    )(x, link_rows.T, link_target.T, link_weight.T, link_count.reshape(1, PEERS))


def write_edges(pattern_ref, left_ref, x_ref, down_ref, right_ref, down_base, top_ref, below_ref, side_ref):
    top_ref[...] = x_ref[:, : TC * TILE]
    for k in range(TC):
        tile = (TR - 1) * TC + k
        keep = pattern_ref[0, tile].astype(F32)
        product = keep * dot(x_ref[:, tile * TILE : (tile + 1) * TILE], down_ref[down_base + k])
        below_ref[:, k * TILE : (k + 1) * TILE] = product.astype(BF16)
    is_left = left_ref[0] == 1
    for r in range(TR):
        last = r * TC + TC - 1
        keep = pattern_ref[1, last].astype(F32)
        product = keep * dot(x_ref[:, last * TILE : (last + 1) * TILE], right_ref[r, 0])
        first_tile = x_ref[:, r * TC * TILE : (r * TC + 1) * TILE]
        side_ref[:, r * TILE : (r + 1) * TILE] = jnp.where(is_left, product.astype(BF16), first_tile)


def edges_kernel(pattern_ref, left_ref, x_ref, down_ref, right_ref, top_ref, below_ref, side_ref):
    write_edges(pattern_ref, left_ref, x_ref, down_ref, right_ref, 0, top_ref, below_ref, side_ref)


EDGE_SHAPES = (
    jax.ShapeDtypeStruct((ROWS, TC * TILE), BF16),
    jax.ShapeDtypeStruct((ROWS, TC * TILE), BF16),
    jax.ShapeDtypeStruct((ROWS, TR * TILE), BF16),
)
DOWN_EDGE = pl.BlockSpec((TC, TILE, TILE), lambda i: (TR - 1, 0, 0))
RIGHT_EDGE = pl.BlockSpec((TR, 1, TILE, TILE), lambda i: (0, TC - 1, 0, 0))


def whole(shape):
    return pl.BlockSpec(shape, lambda i: (0,) * len(shape))


def on_core(value):
    return pltpu.with_memory_space_constraint(value, pltpu.VMEM)


def edges(pattern, left_flag, x, down_hop, right_hop):
    return pl.pallas_call(
        edges_kernel,
        grid=(1,),
        in_specs=[SMEM, SMEM, whole((ROWS, SITES_DEV)), DOWN_EDGE, RIGHT_EDGE],
        out_specs=tuple(whole(s.shape) for s in EDGE_SHAPES),
        out_shape=EDGE_SHAPES,
        compiler_params=params(),
        cost_estimate=COST,
        name="edges",
    )(pattern, left_flag, x, down_hop, right_hop.reshape(TR, TC, TILE, TILE))


def kept(pattern_ref, which, tile, value):
    return jnp.where(pattern_ref[which, tile] == 1, value, jnp.zeros_like(value))


def local_tile(pattern_ref, x_ref, onsite_ref, down_ref, right_ref, tile):
    def block(other):
        return x_ref[:, other * TILE : (other + 1) * TILE]

    r, k = divmod(tile, TC)
    fields = [block(tile)]
    tiles = [onsite_ref[tile]]
    if r > 0:
        fields.append(kept(pattern_ref, 0, tile - TC, block(tile - TC)))
        tiles.append(down_ref[tile - TC])
    if k > 0:
        fields.append(kept(pattern_ref, 1, tile - 1, block(tile - 1)))
        tiles.append(right_ref[tile - 1])
    total = dot(jnp.concatenate(fields, axis=1), jnp.concatenate(tiles, axis=0))
    fields = []
    tiles = []
    if r < TR - 1:
        fields.append(kept(pattern_ref, 0, tile, block(tile + TC)))
        tiles.append(down_ref[tile])
    if k < TC - 1:
        fields.append(kept(pattern_ref, 1, tile, block(tile + 1)))
        tiles.append(right_ref[tile])
    if fields:
        total = total + dot(jnp.concatenate(fields, axis=1), jnp.concatenate(tiles, axis=1), NT)
    return total


def halo_tile(pattern_ref, is_left, down_edge, right_edge, above_ref, below_ref, side_ref, tile):
    r, k = divmod(tile, TC)
    total = None

    def plus(value):
        return value if total is None else total + value

    if r == 0:
        total = plus(above_ref[:, k * TILE : (k + 1) * TILE].astype(F32))
    if r == TR - 1:
        lower = below_ref[:, k * TILE : (k + 1) * TILE]
        total = plus(dot(kept(pattern_ref, 0, tile, lower), down_edge(k), NT))
    if k == 0:
        total = plus(jnp.where(is_left, 0.0, side_ref[:, r * TILE : (r + 1) * TILE].astype(F32)))
    if k == TC - 1:
        righter = side_ref[:, r * TILE : (r + 1) * TILE]
        righter = jnp.where(is_left, righter, jnp.zeros_like(righter))
        total = plus(dot(kept(pattern_ref, 1, tile, righter), right_edge(r), NT))
    return total


def signed(value):
    return jnp.where(lax.broadcasted_iota(jnp.int32, value.shape, 0) < ROWS // 2, value, -value)


def swapped(value):
    return jnp.concatenate([value[ROWS // 2 :], value[: ROWS // 2]], axis=0)


def vector_mean(value):
    comps = value.reshape(4, 16, value.shape[-1])
    return jnp.sum(comps, axis=1) * (1.0 / 16.0)


SCATTER_SCRATCH = [pltpu.VMEM((HI * ROWS, 2 * SLOTS), BF16), pltpu.VMEM((HI * ROWS, SPAN), F32)]


def scatter_into(landed, hot_ref, across_ref, mask_ref, total_ref):
    turned = landed.T
    ends = jnp.concatenate([turned[ROWS:], turned[:ROWS]], axis=1)
    zero = jnp.zeros_like(ends)
    for h in range(HI):
        mask_ref[h * ROWS : (h + 1) * ROWS, :] = jnp.where(across_ref[...] == BF16(h), ends, zero)
    group = 4
    for start in range(0, HI, group):
        total_ref[start * ROWS : (start + group) * ROWS, :] = dot(
            mask_ref[start * ROWS : (start + group) * ROWS, :], hot_ref[0 : 2 * SLOTS, :]
        )


def whole_hop(pattern_ref, left_ref, local_ref, total_ref, above_ref, below_ref, side_ref, down_ref, right_ref, tile):
    h, part = divmod(tile, SPAN // TILE)
    hop = local_ref[:, tile * TILE : (tile + 1) * TILE]
    hop = hop + total_ref[h * ROWS : (h + 1) * ROWS, part * TILE : (part + 1) * TILE]
    halo = halo_tile(
        pattern_ref, left_ref[0] == 1, lambda k: down_ref[k], lambda r: right_ref[r, 0],
        above_ref, below_ref, side_ref, tile,
    )
    return hop if halo is None else hop + halo


def first_kernel(
    pattern_ref, left_ref, landed_ref, above_ref, below_ref, side_ref, hot_ref, high_ref, across_ref,
    v0_hbm, local_hbm, weight_hbm, pairing_ref, down_ref, right_ref,
    one_hbm, x_hbm, mom_ref, top_ref, lower_ref, beside_ref, out_ref, mask_ref, total_ref,
    v0_ref, local_ref, weight_ref, one_ref, x_ref, in_sems, one_sems, x_sems, stage_ref, stage_sems,
):
    arriving = [
        started(source, target, in_sems.at[i])
        for i, (source, target) in enumerate(((v0_hbm, v0_ref), (local_hbm, local_ref), (weight_hbm, weight_ref)))
    ]
    scatter_into(landed_ref[left_ref[1]], hot_ref, across_ref, mask_ref, total_ref)
    for copy in arriving:
        copy.wait()
    leaving = []
    for tile in range(TR * TC):
        cols = slice(tile * TILE, (tile + 1) * TILE)
        hop = whole_hop(
            pattern_ref, left_ref, local_ref, total_ref, above_ref, below_ref, side_ref, down_ref, right_ref, tile
        )
        v0 = v0_ref[:, cols].astype(F32)
        one = signed(hop) + pairing_ref[:, cols] * swapped(v0)
        one_ref[:, cols] = one
        x_ref[:, cols] = one.astype(BF16)
        mom_ref[0, :, cols] = vector_mean(v0 * v0)
        mom_ref[1, :, cols] = vector_mean(v0 * one)
        h, part = divmod(tile, SPAN // TILE)
        if part == SPAN // TILE - 1:
            leaving.append(started(span(one_ref, h), span(one_hbm, h), one_sems.at[h]))
            leaving.append(started(span(x_ref, h), span(x_hbm, h), x_sems.at[h]))
    leaving += gather_payload(x_ref, hot_ref, high_ref, weight_ref, out_ref, stage_ref, stage_sems)
    write_edges(pattern_ref, left_ref, x_ref, down_ref, right_ref, 0, top_ref, lower_ref, beside_ref)
    for copy in leaving:
        copy.wait()


def first(pattern, left_flag, v0, landed, tables, local_part, pairing, halo, down_hop, right_hop):
    shapes = (
        jax.ShapeDtypeStruct((ROWS, SITES_DEV), F32),
        jax.ShapeDtypeStruct((ROWS, SITES_DEV), BF16),
        jax.ShapeDtypeStruct((2, 4, SITES_DEV), F32),
    ) + EDGE_SHAPES + (jax.ShapeDtypeStruct((2, SLOTS, 2 * ROWS), BF16),)
    hot, high, across, weight = tables
    resident = [on_core(a) for a in (landed, *halo, hot, high, across)]
    arrays = (v0, local_part, weight, pairing)
    return pl.pallas_call(
        first_kernel,
        grid=(1,),
        in_specs=[SMEM, SMEM] + [VMEM] * len(resident) + [ANY] * 3 + [whole(pairing.shape), DOWN_EDGE, RIGHT_EDGE],
        out_specs=(ANY, ANY) + tuple(whole(s.shape) for s in shapes[2:-1]) + (ANY,),
        out_shape=shapes,
        scratch_shapes=SCATTER_SCRATCH
        + [
            pltpu.VMEM((ROWS, SITES_DEV), BF16),
            pltpu.VMEM((ROWS, SITES_DEV), F32),
            pltpu.VMEM((SLOTS, TILE), F32),
            pltpu.VMEM((ROWS, SITES_DEV), F32),
            pltpu.VMEM((ROWS, SITES_DEV), BF16),
            pltpu.SemaphoreType.DMA((3,)),
            pltpu.SemaphoreType.DMA((HI,)),
            pltpu.SemaphoreType.DMA((HI,)),
        ]
        + STAGE_SCRATCH,
        compiler_params=params(),
        cost_estimate=COST,
        name="first",
    )(pattern, left_flag, *resident, *arrays, down_hop, right_hop.reshape(TR, TC, TILE, TILE))


def local_kernel(pattern_ref, x_ref, onsite_ref, down_ref, right_ref, out_ref):
    for tile in range(TR * TC):
        out_ref[:, tile * TILE : (tile + 1) * TILE] = local_tile(
            pattern_ref, x_ref, onsite_ref, down_ref, right_ref, tile
        )


def local(pattern, x, onsite, down_hop, right_hop):
    return pl.pallas_call(
        local_kernel,
        in_specs=[SMEM] + [VMEM] * 4,
        out_shape=jax.ShapeDtypeStruct((ROWS, SITES_DEV), F32),
        compiler_params=params(),
        cost_estimate=COST,
        name="local",
    )(pattern, x, onsite, down_hop, right_hop)


def second_kernel(
    pattern_ref, left_ref, landed_ref, above_ref, below_ref, side_ref, hot_ref, across_ref,
    v0_hbm, one_hbm, local_hbm, pairing_ref, mom_in_ref, down_ref, right_ref,
    two_hbm, mom_ref, mask_ref, total_ref, v0_ref, one_ref, local_ref, two_ref, in_sems, two_sems,
):
    arriving = [
        started(source, target, in_sems.at[i])
        for i, (source, target) in enumerate(((v0_hbm, v0_ref), (one_hbm, one_ref), (local_hbm, local_ref)))
    ]
    scatter_into(landed_ref[left_ref[1]], hot_ref, across_ref, mask_ref, total_ref)
    for copy in arriving:
        copy.wait()
    leaving = []
    mom_ref[0:2] = mom_in_ref[...]
    for tile in range(TR * TC):
        cols = slice(tile * TILE, (tile + 1) * TILE)
        hop = whole_hop(
            pattern_ref, left_ref, local_ref, total_ref, above_ref, below_ref, side_ref, down_ref, right_ref, tile
        )
        v0 = v0_ref[:, cols].astype(F32)
        two = 2.0 * (signed(hop) + pairing_ref[:, cols] * swapped(one_ref[:, cols])) - v0
        two_ref[:, cols] = two
        mom_ref[2, :, cols] = vector_mean(v0 * two)
        h, part = divmod(tile, SPAN // TILE)
        if part == SPAN // TILE - 1:
            leaving.append(started(span(two_ref, h), span(two_hbm, h), two_sems.at[h]))
    for copy in leaving:
        copy.wait()


def second(pattern, left_flag, v0, one, landed, hot, across, local_part, pairing, mom, halo, down_hop, right_hop):
    shapes = (
        jax.ShapeDtypeStruct((ROWS, SITES_DEV), F32),
        jax.ShapeDtypeStruct((3, 4, SITES_DEV), F32),
    )
    resident = [on_core(a) for a in (landed, *halo, hot, across)]
    arrays = (v0, one, local_part, pairing, mom)
    return pl.pallas_call(
        second_kernel,
        grid=(1,),
        in_specs=[SMEM, SMEM] + [VMEM] * len(resident) + [ANY] * 3 + [whole(pairing.shape), whole(mom.shape)] + [DOWN_EDGE, RIGHT_EDGE],
        out_specs=(ANY, whole(shapes[1].shape)),
        out_shape=shapes,
        scratch_shapes=SCATTER_SCRATCH
        + [
            pltpu.VMEM((ROWS, SITES_DEV), BF16),
            pltpu.VMEM((ROWS, SITES_DEV), F32),
            pltpu.VMEM((ROWS, SITES_DEV), F32),
            pltpu.VMEM((ROWS, SITES_DEV), F32),
            pltpu.SemaphoreType.DMA((3,)),
            pltpu.SemaphoreType.DMA((HI,)),
        ],
        compiler_params=params(),
        cost_estimate=COST,
        name="second",
    )(pattern, left_flag, *resident, *arrays, down_hop, right_hop.reshape(TR, TC, TILE, TILE))


TILE_AXES = ("z_low", "y", "x", "core")


def passed_along(value, by):
    length = PEERS
    pairs = [(i, i + by) for i in range(length) if 0 <= i + by < length]
    return lax.ppermute(value, TILE_AXES, pairs)


def spread_out(payload):
    spread = lax.all_to_all(
        payload.reshape(2 * PEERS, CAP, 2 * ROWS), ("sheet",) + TILE_AXES, split_axis=0, concat_axis=0, tiled=True
    )
    return spread.reshape(2, SLOTS, 2 * ROWS)


def shards(
    rand_vectors,
    onsite,
    down_hop,
    right_hop,
    pattern,
    pairing,
    link_rows,
    link_target,
    link_weight,
    link_count,
):
    v0 = rand_vectors.reshape(ROWS, SITES_DEV)
    pairing = pairing.reshape(1, SITES_DEV)
    pattern = pattern.T
    left_flag = jnp.stack([1 - lax.axis_index("side"), 1 - lax.axis_index("sheet")]).astype(jnp.int32)

    def halo_of(top, below_part, side_part):
        return (
            passed_along(below_part, 1),
            passed_along(top, -1),
            lax.ppermute(side_part, "side", [(0, 1), (1, 0)]),
        )

    *tables, payload = prepare(v0, link_rows, link_target, link_weight, link_count)
    hot, _, across, _ = tables
    spread = spread_out(payload)
    halo = halo_of(*edges(pattern, left_flag, v0, down_hop, right_hop))
    local_part = local(pattern, v0, onsite, down_hop, right_hop)
    landed, local_part, halo = lax.optimization_barrier((spread, local_part, halo))
    one, x, mom, *edge_parts, payload = first(
        pattern, left_flag, v0, landed, tables, local_part, pairing, halo, down_hop, right_hop
    )
    spread = spread_out(payload)
    halo = halo_of(*edge_parts)
    local_part = local(pattern, x, onsite, down_hop, right_hop)
    landed, local_part, halo = lax.optimization_barrier((spread, local_part, halo))
    two, mom = second(
        pattern, left_flag, v0, one, landed, hot, across, local_part, pairing, mom, halo, down_hop, right_hop
    )
    shape = rand_vectors.shape
    return one.reshape(shape), two.reshape(shape), mom


def solution(mesh):
    both = TILE_AXES + ("sheet", "side")
    mesh = Mesh(mesh.devices.reshape(2, 8, 4, 2, 2, 2), both)
    in_specs = (
        P(None, None, both),
        P(both, None, None),
        P(both, None, None),
        P(both, None, None),
        P(both, None),
        P(both),
        P(both, None),
        P(both, None),
        P(both, None),
        P(both),
    )
    out_specs = (P(None, None, both), P(None, None, both), P(None, None, both))
    return jax.shard_map(shards, mesh=mesh, in_specs=in_specs, out_specs=out_specs, check_vma=False)
```

```python
import jax
import jax.numpy as jnp
from jax import lax
from jax.experimental import pallas as pl
from jax.experimental.pallas import tpu as pltpu
from jax.sharding import Mesh
from jax.sharding import PartitionSpec as P

TILE = 128
TR = 4
TC = 6
ROWS = 64
SITES_DEV = TR * TC * TILE
PEERS = 128
CAP = 8
SLOTS = PEERS * CAP
SPAN = 256
HI = SITES_DEV // SPAN
F32 = jnp.float32
BF16 = jnp.bfloat16
NT = (((1,), (1,)), ((), ()))
NN = (((1,), (0,)), ((), ()))
VMEM_LIMIT = 56 * 1024 * 1024


def dot(a, b, dims=NN):
    return lax.dot_general(a, b, dims, preferred_element_type=F32)


COST = pl.CostEstimate(flops=1000000, bytes_accessed=100000, transcendentals=0)


def params():
    return pltpu.CompilerParams(vmem_limit_bytes=VMEM_LIMIT)


def picked(table):
    spread = jnp.broadcast_to(table[None], (PEERS, CAP, PEERS)).reshape(SLOTS, PEERS)
    own = lax.broadcasted_iota(jnp.int32, (SLOTS, PEERS), 0) // CAP == lax.broadcasted_iota(
        jnp.int32, (SLOTS, PEERS), 1
    )
    return jnp.where(own, spread, 0.0).astype(BF16)


def per_slot(table):
    return dot(picked(table), jnp.ones((PEERS, TILE), BF16))


def build_tables(rows, target, weight, hot_ref, high_ref, across_ref, weight_ref):
    lane = lax.broadcasted_iota(jnp.int32, (SLOTS, SPAN), 1).astype(F32)
    spread_weight = per_slot(weight)
    weight_ref[...] = spread_weight
    wide_weight = jnp.concatenate([spread_weight, spread_weight], axis=1)
    rows_half = lax.broadcasted_iota(jnp.int32, (2 * PEERS, 2 * TILE), 0) < PEERS
    both = (rows_half == (lax.broadcasted_iota(jnp.int32, (2 * PEERS, 2 * TILE), 1) < TILE)).astype(BF16)
    for end, table in ((0, rows), (1, target)):
        coarse = jnp.floor(table * (1.0 / SPAN))
        low = picked(table - coarse * SPAN)
        coarse = picked(coarse)
        wide = dot(jnp.concatenate([low, coarse], axis=1), both)
        low = wide[:, :TILE]
        high_ref[end * SLOTS : (end + 1) * SLOTS, :] = wide[:, TILE:].astype(BF16)
        across_ref[:, end * SLOTS : (end + 1) * SLOTS] = dot(jnp.ones((ROWS, PEERS), BF16), coarse, NT).astype(BF16)
        same = lane == jnp.concatenate([low, low], axis=1)
        hot_ref[2 * end * SLOTS : (2 * end + 1) * SLOTS, :] = jnp.where(same, 1.0, 0.0).astype(BF16)
        if end == 1:
            hot_ref[SLOTS : 2 * SLOTS, :] = jnp.where(same, wide_weight, 0.0).astype(BF16)


def gather_ends(parts, hot_ref, high_ref, start, chunk):
    lane = lax.broadcasted_iota(jnp.int32, (chunk, TILE), 1)
    half = (lane >= ROWS).astype(F32)
    ends = []
    for end in range(2):
        hot = hot_ref[2 * end * SLOTS + start : 2 * end * SLOTS + start + chunk, :]
        high = high_ref[end * SLOTS + start : end * SLOTS + start + chunk, :].astype(F32) - half
        total = jnp.zeros((chunk, TILE), F32)
        for q in range(HI // 4):
            found = dot(hot, jnp.concatenate(parts[4 * q : 4 * q + 4], axis=0), NT)
            total = jnp.where(high == 4.0 * q, found[:, :TILE], total)
            total = jnp.where(high == 4.0 * q + 2.0, found[:, TILE:], total)
        ends.append(total + pltpu.roll(total, ROWS, 1))
    return jnp.where(lane < ROWS, ends[0], ends[1])


def as_payload(ends, weight):
    field = ends.astype(BF16)
    lane = lax.broadcasted_iota(jnp.int32, ends.shape, 1)
    return jnp.where(lane < ROWS, field.astype(F32), field.astype(F32) * weight).astype(BF16)


CHUNK = 512


def gather_payload(x_ref, hot_ref, high_ref, weight_ref, out_ref):
    parts = [x_ref[:, h * SPAN : (h + 1) * SPAN] for h in range(HI)]
    for start in range(0, SLOTS, CHUNK):
        ends = gather_ends(parts, hot_ref, high_ref, start, CHUNK)
        payload = as_payload(ends, weight_ref[start : start + CHUNK, :])
        out_ref[0, start : start + CHUNK, :] = payload
        out_ref[1, start : start + CHUNK, :] = payload


def prepare_kernel(
    x_ref, rows_ref, target_ref, weight_ref, count_ref, hot_ref, high_ref, across_ref, spread_ref, out_ref
):
    live = lax.broadcasted_iota(jnp.int32, (CAP, PEERS), 0) < count_ref[...]
    weight = jnp.where(live, weight_ref[...].astype(F32), 0.0)
    build_tables(
        rows_ref[...].astype(F32), target_ref[...].astype(F32), weight, hot_ref, high_ref, across_ref, spread_ref
    )
    gather_payload(x_ref, hot_ref, high_ref, spread_ref, out_ref)


TABLE_SHAPES = (
    pltpu.VMEM((3 * SLOTS, SPAN), BF16),
    pltpu.VMEM((2 * SLOTS, TILE), BF16),
    pltpu.VMEM((ROWS, 2 * SLOTS), BF16),
    jax.ShapeDtypeStruct((SLOTS, TILE), F32),
)


def prepare(x, link_rows, link_target, link_weight, link_count):
    return pl.pallas_call(
        prepare_kernel,
        out_shape=TABLE_SHAPES + (jax.ShapeDtypeStruct((2, SLOTS, 2 * ROWS), BF16),),
        compiler_params=params(),
        cost_estimate=COST,
        name="prepare",
    )(x, link_rows.T, link_target.T, link_weight.T, link_count.reshape(1, PEERS))


def write_edges(pattern_ref, left_ref, x_ref, down_ref, right_ref, down_base, top_ref, below_ref, side_ref):
    top_ref[...] = x_ref[:, : TC * TILE]
    for k in range(TC):
        tile = (TR - 1) * TC + k
        keep = pattern_ref[0, tile].astype(F32)
        product = keep * dot(x_ref[:, tile * TILE : (tile + 1) * TILE], down_ref[down_base + k])
        below_ref[:, k * TILE : (k + 1) * TILE] = product.astype(BF16)
    is_left = left_ref[0] == 1
    for r in range(TR):
        last = r * TC + TC - 1
        keep = pattern_ref[1, last].astype(F32)
        product = keep * dot(x_ref[:, last * TILE : (last + 1) * TILE], right_ref[r, 0])
        first_tile = x_ref[:, r * TC * TILE : (r * TC + 1) * TILE]
        side_ref[:, r * TILE : (r + 1) * TILE] = jnp.where(is_left, product.astype(BF16), first_tile)


def edges_kernel(pattern_ref, left_ref, x_ref, down_ref, right_ref, top_ref, below_ref, side_ref):
    write_edges(pattern_ref, left_ref, x_ref, down_ref, right_ref, 0, top_ref, below_ref, side_ref)


EDGE_SHAPES = (
    jax.ShapeDtypeStruct((ROWS, TC * TILE), BF16),
    jax.ShapeDtypeStruct((ROWS, TC * TILE), BF16),
    jax.ShapeDtypeStruct((ROWS, TR * TILE), BF16),
)
SMEM = pl.BlockSpec(memory_space=pltpu.SMEM)
VMEM = pl.BlockSpec(memory_space=pltpu.VMEM)
DOWN_EDGE = pl.BlockSpec((TC, TILE, TILE), lambda i: (TR - 1, 0, 0))
RIGHT_EDGE = pl.BlockSpec((TR, 1, TILE, TILE), lambda i: (0, TC - 1, 0, 0))


def whole(shape):
    return pl.BlockSpec(shape, lambda i: (0,) * len(shape))


def on_core(value):
    return pltpu.with_memory_space_constraint(value, pltpu.VMEM)


def edges(pattern, left_flag, x, down_hop, right_hop):
    return pl.pallas_call(
        edges_kernel,
        grid=(1,),
        in_specs=[SMEM, SMEM, whole((ROWS, SITES_DEV)), DOWN_EDGE, RIGHT_EDGE],
        out_specs=tuple(whole(s.shape) for s in EDGE_SHAPES),
        out_shape=EDGE_SHAPES,
        compiler_params=params(),
        cost_estimate=COST,
        name="edges",
    )(pattern, left_flag, x, down_hop, right_hop.reshape(TR, TC, TILE, TILE))


def kept(pattern_ref, which, tile, value):
    return jnp.where(pattern_ref[which, tile] == 1, value, jnp.zeros_like(value))


def local_tile(pattern_ref, x_ref, onsite_ref, down_ref, right_ref, tile):
    def block(other):
        return x_ref[:, other * TILE : (other + 1) * TILE]

    r, k = divmod(tile, TC)
    fields = [block(tile)]
    tiles = [onsite_ref[tile]]
    if r > 0:
        fields.append(kept(pattern_ref, 0, tile - TC, block(tile - TC)))
        tiles.append(down_ref[tile - TC])
    if k > 0:
        fields.append(kept(pattern_ref, 1, tile - 1, block(tile - 1)))
        tiles.append(right_ref[tile - 1])
    total = dot(jnp.concatenate(fields, axis=1), jnp.concatenate(tiles, axis=0))
    fields = []
    tiles = []
    if r < TR - 1:
        fields.append(kept(pattern_ref, 0, tile, block(tile + TC)))
        tiles.append(down_ref[tile])
    if k < TC - 1:
        fields.append(kept(pattern_ref, 1, tile, block(tile + 1)))
        tiles.append(right_ref[tile])
    if fields:
        total = total + dot(jnp.concatenate(fields, axis=1), jnp.concatenate(tiles, axis=1), NT)
    return total


def halo_tile(pattern_ref, is_left, down_edge, right_edge, above_ref, below_ref, side_ref, tile):
    r, k = divmod(tile, TC)
    total = None

    def plus(value):
        return value if total is None else total + value

    if r == 0:
        total = plus(above_ref[:, k * TILE : (k + 1) * TILE].astype(F32))
    if r == TR - 1:
        lower = below_ref[:, k * TILE : (k + 1) * TILE]
        total = plus(dot(kept(pattern_ref, 0, tile, lower), down_edge(k), NT))
    if k == 0:
        total = plus(jnp.where(is_left, 0.0, side_ref[:, r * TILE : (r + 1) * TILE].astype(F32)))
    if k == TC - 1:
        righter = side_ref[:, r * TILE : (r + 1) * TILE]
        righter = jnp.where(is_left, righter, jnp.zeros_like(righter))
        total = plus(dot(kept(pattern_ref, 1, tile, righter), right_edge(r), NT))
    return total


def signed(value):
    return jnp.where(lax.broadcasted_iota(jnp.int32, value.shape, 0) < ROWS // 2, value, -value)


def swapped(value):
    return jnp.concatenate([value[ROWS // 2 :], value[: ROWS // 2]], axis=0)


def vector_mean(value):
    comps = value.reshape(4, 16, value.shape[-1])
    return jnp.sum(comps, axis=1) * (1.0 / 16.0)


SCATTER_SCRATCH = [pltpu.VMEM((HI * ROWS, 2 * SLOTS), BF16), pltpu.VMEM((HI * ROWS, SPAN), F32)]


def scatter_into(landed, hot_ref, across_ref, mask_ref, total_ref):
    turned = landed.T
    ends = jnp.concatenate([turned[ROWS:], turned[:ROWS]], axis=1)
    zero = jnp.zeros_like(ends)
    for h in range(HI):
        mask_ref[h * ROWS : (h + 1) * ROWS, :] = jnp.where(across_ref[...] == BF16(h), ends, zero)
    group = 2
    for start in range(0, HI, group):
        total_ref[start * ROWS : (start + group) * ROWS, :] = dot(
            mask_ref[start * ROWS : (start + group) * ROWS, :], hot_ref[0 : 2 * SLOTS, :]
        )


def whole_hop(pattern_ref, left_ref, local_ref, total_ref, above_ref, below_ref, side_ref, down_ref, right_ref, tile):
    h, part = divmod(tile, SPAN // TILE)
    hop = local_ref[:, tile * TILE : (tile + 1) * TILE]
    hop = hop + total_ref[h * ROWS : (h + 1) * ROWS, part * TILE : (part + 1) * TILE]
    halo = halo_tile(
        pattern_ref, left_ref[0] == 1, lambda k: down_ref[k], lambda r: right_ref[r, 0],
        above_ref, below_ref, side_ref, tile,
    )
    return hop if halo is None else hop + halo


def first_kernel(
    pattern_ref, left_ref, landed_ref, above_ref, below_ref, side_ref, hot_ref, high_ref, across_ref,
    v0_ref, local_ref, weight_ref, pairing_ref, down_ref, right_ref,
    one_ref, x_ref, mom_ref, top_ref, lower_ref, beside_ref, out_ref, mask_ref, total_ref,
):
    scatter_into(landed_ref[left_ref[1]], hot_ref, across_ref, mask_ref, total_ref)
    for tile in range(TR * TC):
        cols = slice(tile * TILE, (tile + 1) * TILE)
        hop = whole_hop(
            pattern_ref, left_ref, local_ref, total_ref, above_ref, below_ref, side_ref, down_ref, right_ref, tile
        )
        v0 = v0_ref[:, cols].astype(F32)
        one = signed(hop) + pairing_ref[:, cols] * swapped(v0)
        one_ref[:, cols] = one
        x_ref[:, cols] = one.astype(BF16)
        mom_ref[0, :, cols] = vector_mean(v0 * v0)
        mom_ref[1, :, cols] = vector_mean(v0 * one)
    gather_payload(x_ref, hot_ref, high_ref, weight_ref, out_ref)
    write_edges(pattern_ref, left_ref, x_ref, down_ref, right_ref, 0, top_ref, lower_ref, beside_ref)


def first(pattern, left_flag, v0, landed, tables, local_part, pairing, halo, down_hop, right_hop):
    shapes = (
        jax.ShapeDtypeStruct((ROWS, SITES_DEV), F32),
        jax.ShapeDtypeStruct((ROWS, SITES_DEV), BF16),
        jax.ShapeDtypeStruct((2, 4, SITES_DEV), F32),
    ) + EDGE_SHAPES + (jax.ShapeDtypeStruct((2, SLOTS, 2 * ROWS), BF16),)
    hot, high, across, weight = tables
    resident = [on_core(a) for a in (landed, *halo, hot, high, across)]
    arrays = (v0, local_part, weight, pairing)
    return pl.pallas_call(
        first_kernel,
        grid=(1,),
        in_specs=[SMEM, SMEM] + [VMEM] * len(resident) + [whole(a.shape) for a in arrays] + [DOWN_EDGE, RIGHT_EDGE],
        out_specs=tuple(whole(s.shape) for s in shapes),
        out_shape=shapes,
        scratch_shapes=SCATTER_SCRATCH,
        compiler_params=params(),
        cost_estimate=COST,
        name="first",
    )(pattern, left_flag, *resident, *arrays, down_hop, right_hop.reshape(TR, TC, TILE, TILE))


def local_kernel(pattern_ref, x_ref, onsite_ref, down_ref, right_ref, out_ref):
    for tile in range(TR * TC):
        out_ref[:, tile * TILE : (tile + 1) * TILE] = local_tile(
            pattern_ref, x_ref, onsite_ref, down_ref, right_ref, tile
        )


def local(pattern, x, onsite, down_hop, right_hop):
    return pl.pallas_call(
        local_kernel,
        in_specs=[SMEM] + [VMEM] * 4,
        out_shape=jax.ShapeDtypeStruct((ROWS, SITES_DEV), F32),
        compiler_params=params(),
        cost_estimate=COST,
        name="local",
    )(pattern, x, onsite, down_hop, right_hop)


def second_kernel(
    pattern_ref, left_ref, landed_ref, above_ref, below_ref, side_ref, hot_ref, across_ref,
    v0_ref, one_ref, local_ref, pairing_ref, mom_in_ref, down_ref, right_ref,
    two_ref, mom_ref, mask_ref, total_ref,
):
    scatter_into(landed_ref[left_ref[1]], hot_ref, across_ref, mask_ref, total_ref)
    mom_ref[0:2] = mom_in_ref[...]
    for tile in range(TR * TC):
        cols = slice(tile * TILE, (tile + 1) * TILE)
        hop = whole_hop(
            pattern_ref, left_ref, local_ref, total_ref, above_ref, below_ref, side_ref, down_ref, right_ref, tile
        )
        v0 = v0_ref[:, cols].astype(F32)
        two = 2.0 * (signed(hop) + pairing_ref[:, cols] * swapped(one_ref[:, cols])) - v0
        two_ref[:, cols] = two
        mom_ref[2, :, cols] = vector_mean(v0 * two)


def second(pattern, left_flag, v0, one, landed, hot, across, local_part, pairing, mom, halo, down_hop, right_hop):
    shapes = (
        jax.ShapeDtypeStruct((ROWS, SITES_DEV), F32),
        jax.ShapeDtypeStruct((3, 4, SITES_DEV), F32),
    )
    resident = [on_core(a) for a in (landed, *halo, hot, across)]
    arrays = (v0, one, local_part, pairing, mom)
    return pl.pallas_call(
        second_kernel,
        grid=(1,),
        in_specs=[SMEM, SMEM] + [VMEM] * len(resident) + [whole(a.shape) for a in arrays] + [DOWN_EDGE, RIGHT_EDGE],
        out_specs=tuple(whole(s.shape) for s in shapes),
        out_shape=shapes,
        scratch_shapes=SCATTER_SCRATCH,
        compiler_params=params(),
        cost_estimate=COST,
        name="second",
    )(pattern, left_flag, *resident, *arrays, down_hop, right_hop.reshape(TR, TC, TILE, TILE))


TILE_AXES = ("z_low", "y", "x", "core")


def passed_along(value, by):
    length = PEERS
    pairs = [(i, i + by) for i in range(length) if 0 <= i + by < length]
    return lax.ppermute(value, TILE_AXES, pairs)


def spread_out(payload):
    spread = lax.all_to_all(
        payload.reshape(2 * PEERS, CAP, 2 * ROWS), ("sheet",) + TILE_AXES, split_axis=0, concat_axis=0, tiled=True
    )
    return spread.reshape(2, SLOTS, 2 * ROWS)


def shards(
    rand_vectors,
    onsite,
    down_hop,
    right_hop,
    pattern,
    pairing,
    link_rows,
    link_target,
    link_weight,
    link_count,
):
    v0 = rand_vectors.reshape(ROWS, SITES_DEV)
    pairing = pairing.reshape(1, SITES_DEV)
    pattern = pattern.T
    left_flag = jnp.stack([1 - lax.axis_index("side"), 1 - lax.axis_index("sheet")]).astype(jnp.int32)

    def halo_of(top, below_part, side_part):
        return (
            passed_along(below_part, 1),
            passed_along(top, -1),
            lax.ppermute(side_part, "side", [(0, 1), (1, 0)]),
        )

    *tables, payload = prepare(v0, link_rows, link_target, link_weight, link_count)
    hot, _, across, _ = tables
    spread = spread_out(payload)
    halo = halo_of(*edges(pattern, left_flag, v0, down_hop, right_hop))
    local_part = local(pattern, v0, onsite, down_hop, right_hop)
    landed, local_part, halo = lax.optimization_barrier((spread, local_part, halo))
    one, x, mom, *edge_parts, payload = first(
        pattern, left_flag, v0, landed, tables, local_part, pairing, halo, down_hop, right_hop
    )
    spread = spread_out(payload)
    halo = halo_of(*edge_parts)
    local_part = local(pattern, x, onsite, down_hop, right_hop)
    landed, local_part, halo = lax.optimization_barrier((spread, local_part, halo))
    two, mom = second(
        pattern, left_flag, v0, one, landed, hot, across, local_part, pairing, mom, halo, down_hop, right_hop
    )
    shape = rand_vectors.shape
    return one.reshape(shape), two.reshape(shape), mom


def solution(mesh):
    both = TILE_AXES + ("sheet", "side")
    mesh = Mesh(mesh.devices.reshape(2, 8, 4, 2, 2, 2), both)
    in_specs = (
        P(None, None, both),
        P(both, None, None),
        P(both, None, None),
        P(both, None, None),
        P(both, None),
        P(both),
        P(both, None),
        P(both, None),
        P(both, None),
        P(both),
    )
    out_specs = (P(None, None, both), P(None, None, both), P(None, None, both))
    return jax.shard_map(shards, mesh=mesh, in_specs=in_specs, out_specs=out_specs, check_vma=False)
```

```python
import jax
import jax.numpy as jnp
from jax import lax
from jax.experimental import pallas as pl
from jax.experimental.pallas import tpu as pltpu
from jax.sharding import Mesh
from jax.sharding import PartitionSpec as P

TILE = 128
TR = 4
TC = 6
ROWS = 64
SITES_DEV = TR * TC * TILE
PEERS = 128
CAP = 8
SLOTS = PEERS * CAP
SPAN = 256
HI = SITES_DEV // SPAN
F32 = jnp.float32
BF16 = jnp.bfloat16
NT = (((1,), (1,)), ((), ()))
NN = (((1,), (0,)), ((), ()))
VMEM_LIMIT = 56 * 1024 * 1024


def dot(a, b, dims=NN):
    return lax.dot_general(a, b, dims, preferred_element_type=F32)


COST = pl.CostEstimate(flops=1000000, bytes_accessed=100000, transcendentals=0)


def params():
    return pltpu.CompilerParams(vmem_limit_bytes=VMEM_LIMIT)


def picked(table):
    spread = jnp.broadcast_to(table[None], (PEERS, CAP, PEERS)).reshape(SLOTS, PEERS)
    own = lax.broadcasted_iota(jnp.int32, (SLOTS, PEERS), 0) // CAP == lax.broadcasted_iota(
        jnp.int32, (SLOTS, PEERS), 1
    )
    return jnp.where(own, spread, 0.0).astype(BF16)


def per_slot(table):
    return dot(picked(table), jnp.ones((PEERS, TILE), BF16))


def build_tables(rows, target, weight, hot_ref, high_ref, across_ref, weight_ref):
    lane = lax.broadcasted_iota(jnp.int32, (SLOTS, SPAN), 1).astype(F32)
    spread_weight = per_slot(weight)
    weight_ref[...] = spread_weight
    wide_weight = jnp.concatenate([spread_weight, spread_weight], axis=1)
    rows_half = lax.broadcasted_iota(jnp.int32, (2 * PEERS, 2 * TILE), 0) < PEERS
    both = (rows_half == (lax.broadcasted_iota(jnp.int32, (2 * PEERS, 2 * TILE), 1) < TILE)).astype(BF16)
    for end, table in ((0, rows), (1, target)):
        coarse = jnp.floor(table * (1.0 / SPAN))
        low = picked(table - coarse * SPAN)
        coarse = picked(coarse)
        wide = dot(jnp.concatenate([low, coarse], axis=1), both)
        low = wide[:, :TILE]
        high_ref[end * SLOTS : (end + 1) * SLOTS, :] = wide[:, TILE:].astype(BF16)
        across_ref[:, end * SLOTS : (end + 1) * SLOTS] = dot(jnp.ones((ROWS, PEERS), BF16), coarse, NT).astype(BF16)
        same = lane == jnp.concatenate([low, low], axis=1)
        hot_ref[2 * end * SLOTS : (2 * end + 1) * SLOTS, :] = jnp.where(same, 1.0, 0.0).astype(BF16)
        if end == 1:
            hot_ref[SLOTS : 2 * SLOTS, :] = jnp.where(same, wide_weight, 0.0).astype(BF16)


def gather_ends(parts, hot_ref, high_ref, start, chunk):
    lane = lax.broadcasted_iota(jnp.int32, (chunk, TILE), 1)
    half = (lane >= ROWS).astype(F32)
    ends = []
    for end in range(2):
        hot = hot_ref[2 * end * SLOTS + start : 2 * end * SLOTS + start + chunk, :]
        high = high_ref[end * SLOTS + start : end * SLOTS + start + chunk, :].astype(F32) - half
        total = jnp.zeros((chunk, TILE), F32)
        for q in range(HI // 4):
            found = dot(hot, jnp.concatenate(parts[4 * q : 4 * q + 4], axis=0), NT)
            total = jnp.where(high == 4.0 * q, found[:, :TILE], total)
            total = jnp.where(high == 4.0 * q + 2.0, found[:, TILE:], total)
        ends.append(total + pltpu.roll(total, ROWS, 1))
    return jnp.where(lane < ROWS, ends[0], ends[1])


def as_payload(ends, weight):
    field = ends.astype(BF16)
    lane = lax.broadcasted_iota(jnp.int32, ends.shape, 1)
    return jnp.where(lane < ROWS, field.astype(F32), field.astype(F32) * weight).astype(BF16)


CHUNK = 512


def gather_payload(x_ref, hot_ref, high_ref, weight_ref, out_ref):
    parts = [x_ref[:, h * SPAN : (h + 1) * SPAN] for h in range(HI)]
    for start in range(0, SLOTS, CHUNK):
        ends = gather_ends(parts, hot_ref, high_ref, start, CHUNK)
        payload = as_payload(ends, weight_ref[start : start + CHUNK, :])
        out_ref[0, start : start + CHUNK, :] = payload
        out_ref[1, start : start + CHUNK, :] = payload


TABLE_SHAPES = (
    pltpu.VMEM((3 * SLOTS, SPAN), BF16),
    pltpu.VMEM((2 * SLOTS, TILE), BF16),
    pltpu.VMEM((ROWS, 2 * SLOTS), BF16),
    jax.ShapeDtypeStruct((SLOTS, TILE), F32),
)


def write_edges(pattern_ref, left_ref, x_ref, down_ref, right_ref, down_base, top_ref, below_ref, side_ref):
    top_ref[...] = x_ref[:, : TC * TILE]
    for k in range(TC):
        tile = (TR - 1) * TC + k
        keep = pattern_ref[0, tile].astype(F32)
        product = keep * dot(x_ref[:, tile * TILE : (tile + 1) * TILE], down_ref[down_base + k])
        below_ref[:, k * TILE : (k + 1) * TILE] = product.astype(BF16)
    is_left = (left_ref[0] & 1) == 1
    for r in range(TR):
        last = r * TC + TC - 1
        keep = pattern_ref[1, last].astype(F32)
        product = keep * dot(x_ref[:, last * TILE : (last + 1) * TILE], right_ref[r, 0])
        first_tile = x_ref[:, r * TC * TILE : (r * TC + 1) * TILE]
        side_ref[:, r * TILE : (r + 1) * TILE] = jnp.where(is_left, product.astype(BF16), first_tile)


EDGE_SHAPES = (
    jax.ShapeDtypeStruct((ROWS, TC * TILE), BF16),
    jax.ShapeDtypeStruct((ROWS, TC * TILE), BF16),
    jax.ShapeDtypeStruct((ROWS, TR * TILE), BF16),
)
SMEM = pl.BlockSpec(memory_space=pltpu.SMEM)
VMEM = pl.BlockSpec(memory_space=pltpu.VMEM)
DOWN_EDGE = pl.BlockSpec((TC, TILE, TILE), lambda i: (TR - 1, 0, 0))
RIGHT_EDGE = pl.BlockSpec((TR, 1, TILE, TILE), lambda i: (0, TC - 1, 0, 0))


def whole(shape):
    return pl.BlockSpec(shape, lambda i: (0,) * len(shape))


def on_core(value):
    return pltpu.with_memory_space_constraint(value, pltpu.VMEM)


def prepare_kernel(
    pattern_ref, left_ref, x_ref, rows_ref, target_ref, weight_ref, count_ref, down_ref, right_ref,
    hot_ref, high_ref, across_ref, spread_ref, top_ref, below_ref, side_ref, out_ref,
):
    live = lax.broadcasted_iota(jnp.int32, (CAP, PEERS), 0) < count_ref[...]
    weight = jnp.where(live, weight_ref[...].astype(F32), 0.0)
    build_tables(
        rows_ref[...].astype(F32), target_ref[...].astype(F32), weight, hot_ref, high_ref, across_ref, spread_ref
    )
    gather_payload(x_ref, hot_ref, high_ref, spread_ref, out_ref)
    write_edges(pattern_ref, left_ref, x_ref, down_ref, right_ref, 0, top_ref, below_ref, side_ref)


def prepare(pattern, left_flag, x, link_rows, link_target, link_weight, link_count, down_hop, right_hop):
    arrays = (x, link_rows.T, link_target.T, link_weight.T, link_count.reshape(1, PEERS))
    shapes = TABLE_SHAPES + EDGE_SHAPES + (jax.ShapeDtypeStruct((2, SLOTS, 2 * ROWS), BF16),)
    resident = len(TABLE_SHAPES) - 1
    return pl.pallas_call(
        prepare_kernel,
        grid=(1,),
        in_specs=[SMEM, SMEM] + [whole(a.shape) for a in arrays] + [DOWN_EDGE, RIGHT_EDGE],
        out_specs=(VMEM,) * resident + tuple(whole(s.shape) for s in shapes[resident:]),
        out_shape=shapes,
        compiler_params=params(),
        cost_estimate=COST,
        name="prepare",
    )(pattern, left_flag, *arrays, down_hop, right_hop.reshape(TR, TC, TILE, TILE))


def kept(pattern_ref, which, tile, value):
    return jnp.where(pattern_ref[which, tile] == 1, value, jnp.zeros_like(value))


def local_tile(pattern_ref, x_ref, onsite_ref, down_ref, right_ref, tile):
    def block(other):
        return x_ref[:, other * TILE : (other + 1) * TILE]

    r, k = divmod(tile, TC)
    fields = [block(tile)]
    tiles = [onsite_ref[tile]]
    if r > 0:
        fields.append(kept(pattern_ref, 0, tile - TC, block(tile - TC)))
        tiles.append(down_ref[tile - TC])
    if k > 0:
        fields.append(kept(pattern_ref, 1, tile - 1, block(tile - 1)))
        tiles.append(right_ref[tile - 1])
    total = dot(jnp.concatenate(fields, axis=1), jnp.concatenate(tiles, axis=0))
    fields = []
    tiles = []
    if r < TR - 1:
        fields.append(kept(pattern_ref, 0, tile, block(tile + TC)))
        tiles.append(down_ref[tile])
    if k < TC - 1:
        fields.append(kept(pattern_ref, 1, tile, block(tile + 1)))
        tiles.append(right_ref[tile])
    if fields:
        total = total + dot(jnp.concatenate(fields, axis=1), jnp.concatenate(tiles, axis=1), NT)
    return total


def halo_tile(pattern_ref, is_left, down_edge, right_edge, above_ref, below_ref, side_ref, tile):
    r, k = divmod(tile, TC)
    total = None

    def plus(value):
        return value if total is None else total + value

    if r == 0:
        total = plus(above_ref[:, k * TILE : (k + 1) * TILE].astype(F32))
    if r == TR - 1:
        lower = below_ref[:, k * TILE : (k + 1) * TILE]
        total = plus(dot(kept(pattern_ref, 0, tile, lower), down_edge(k), NT))
    if k == 0:
        total = plus(jnp.where(is_left, 0.0, side_ref[:, r * TILE : (r + 1) * TILE].astype(F32)))
    if k == TC - 1:
        righter = side_ref[:, r * TILE : (r + 1) * TILE]
        righter = jnp.where(is_left, righter, jnp.zeros_like(righter))
        total = plus(dot(kept(pattern_ref, 1, tile, righter), right_edge(r), NT))
    return total


def signed(value):
    return jnp.where(lax.broadcasted_iota(jnp.int32, value.shape, 0) < ROWS // 2, value, -value)


def swapped(value):
    return jnp.concatenate([value[ROWS // 2 :], value[: ROWS // 2]], axis=0)


def vector_mean(value):
    comps = value.reshape(4, 16, value.shape[-1])
    return jnp.sum(comps, axis=1) * (1.0 / 16.0)


SCATTER_SCRATCH = [pltpu.VMEM((HI * ROWS, 2 * SLOTS), BF16), pltpu.VMEM((HI * ROWS, SPAN), F32)]


def scatter_into(landed, hot_ref, across_ref, mask_ref, total_ref):
    turned = landed.T
    ends = jnp.concatenate([turned[ROWS:], turned[:ROWS]], axis=1)
    zero = jnp.zeros_like(ends)
    for h in range(HI):
        mask_ref[h * ROWS : (h + 1) * ROWS, :] = jnp.where(across_ref[...] == BF16(h), ends, zero)
    group = 2
    for start in range(0, HI, group):
        total_ref[start * ROWS : (start + group) * ROWS, :] = dot(
            mask_ref[start * ROWS : (start + group) * ROWS, :], hot_ref[0 : 2 * SLOTS, :]
        )


def whole_hop(pattern_ref, left_ref, local_ref, total_ref, above_ref, below_ref, side_ref, down_ref, right_ref, tile):
    h, part = divmod(tile, SPAN // TILE)
    hop = local_ref[:, tile * TILE : (tile + 1) * TILE]
    hop = hop + total_ref[h * ROWS : (h + 1) * ROWS, part * TILE : (part + 1) * TILE]
    halo = halo_tile(
        pattern_ref, (left_ref[0] & 1) == 1, lambda k: down_ref[k], lambda r: right_ref[r, 0],
        above_ref, below_ref, side_ref, tile,
    )
    return hop if halo is None else hop + halo


def first_kernel(
    pattern_ref, left_ref, landed_ref, above_ref, below_ref, side_ref, hot_ref, high_ref, across_ref,
    v0_ref, local_ref, weight_ref, pairing_ref, down_ref, right_ref,
    one_ref, x_ref, mom_ref, top_ref, lower_ref, beside_ref, out_ref, mask_ref, total_ref,
):
    scatter_into(landed_ref[left_ref[0] >> 1], hot_ref, across_ref, mask_ref, total_ref)
    for tile in range(TR * TC):
        cols = slice(tile * TILE, (tile + 1) * TILE)
        hop = whole_hop(
            pattern_ref, left_ref, local_ref, total_ref, above_ref, below_ref, side_ref, down_ref, right_ref, tile
        )
        v0 = v0_ref[:, cols].astype(F32)
        one = signed(hop) + pairing_ref[:, cols] * swapped(v0)
        one_ref[:, cols] = one
        x_ref[:, cols] = one.astype(BF16)
        mom_ref[0, :, cols] = vector_mean(v0 * v0)
        mom_ref[1, :, cols] = vector_mean(v0 * one)
    gather_payload(x_ref, hot_ref, high_ref, weight_ref, out_ref)
    write_edges(pattern_ref, left_ref, x_ref, down_ref, right_ref, 0, top_ref, lower_ref, beside_ref)


def first(pattern, left_flag, v0, landed, tables, local_part, pairing, halo, down_hop, right_hop):
    shapes = (
        jax.ShapeDtypeStruct((ROWS, SITES_DEV), F32),
        jax.ShapeDtypeStruct((ROWS, SITES_DEV), BF16),
        jax.ShapeDtypeStruct((2, 4, SITES_DEV), F32),
    ) + EDGE_SHAPES + (jax.ShapeDtypeStruct((2, SLOTS, 2 * ROWS), BF16),)
    hot, high, across, weight = tables
    resident = [on_core(a) for a in (landed, *halo, hot, high, across)]
    arrays = (v0, local_part, weight, pairing)
    return pl.pallas_call(
        first_kernel,
        grid=(1,),
        in_specs=[SMEM, SMEM] + [VMEM] * len(resident) + [whole(a.shape) for a in arrays] + [DOWN_EDGE, RIGHT_EDGE],
        out_specs=tuple(whole(s.shape) for s in shapes),
        out_shape=shapes,
        scratch_shapes=SCATTER_SCRATCH,
        compiler_params=params(),
        cost_estimate=COST,
        name="first",
    )(pattern, left_flag, *resident, *arrays, down_hop, right_hop.reshape(TR, TC, TILE, TILE))


def local_kernel(pattern_ref, x_ref, onsite_ref, down_ref, right_ref, out_ref):
    for tile in range(TR * TC):
        out_ref[:, tile * TILE : (tile + 1) * TILE] = local_tile(
            pattern_ref, x_ref, onsite_ref, down_ref, right_ref, tile
        )


def local(pattern, x, onsite, down_hop, right_hop):
    return pl.pallas_call(
        local_kernel,
        in_specs=[SMEM] + [VMEM] * 4,
        out_shape=jax.ShapeDtypeStruct((ROWS, SITES_DEV), F32),
        compiler_params=params(),
        cost_estimate=COST,
        name="local",
    )(pattern, x, onsite, down_hop, right_hop)


def second_kernel(
    pattern_ref, left_ref, landed_ref, above_ref, below_ref, side_ref, hot_ref, across_ref,
    v0_ref, one_ref, local_ref, pairing_ref, mom_in_ref, down_ref, right_ref,
    two_ref, mom_ref, mask_ref, total_ref,
):
    scatter_into(landed_ref[left_ref[0] >> 1], hot_ref, across_ref, mask_ref, total_ref)
    mom_ref[0:2] = mom_in_ref[...]
    for tile in range(TR * TC):
        cols = slice(tile * TILE, (tile + 1) * TILE)
        hop = whole_hop(
            pattern_ref, left_ref, local_ref, total_ref, above_ref, below_ref, side_ref, down_ref, right_ref, tile
        )
        v0 = v0_ref[:, cols].astype(F32)
        two = 2.0 * (signed(hop) + pairing_ref[:, cols] * swapped(one_ref[:, cols])) - v0
        two_ref[:, cols] = two
        mom_ref[2, :, cols] = vector_mean(v0 * two)


def second(pattern, left_flag, v0, one, landed, hot, across, local_part, pairing, mom, halo, down_hop, right_hop):
    shapes = (
        jax.ShapeDtypeStruct((ROWS, SITES_DEV), F32),
        jax.ShapeDtypeStruct((3, 4, SITES_DEV), F32),
    )
    resident = [on_core(a) for a in (landed, *halo, hot, across)]
    arrays = (v0, one, local_part, pairing, mom)
    return pl.pallas_call(
        second_kernel,
        grid=(1,),
        in_specs=[SMEM, SMEM] + [VMEM] * len(resident) + [whole(a.shape) for a in arrays] + [DOWN_EDGE, RIGHT_EDGE],
        out_specs=tuple(whole(s.shape) for s in shapes),
        out_shape=shapes,
        scratch_shapes=SCATTER_SCRATCH,
        compiler_params=params(),
        cost_estimate=COST,
        name="second",
    )(pattern, left_flag, *resident, *arrays, down_hop, right_hop.reshape(TR, TC, TILE, TILE))


TILE_AXES = ("z_low", "y", "x", "core")


def passed_along(value, by):
    length = PEERS
    pairs = [(i, i + by) for i in range(length) if 0 <= i + by < length]
    return lax.ppermute(value, TILE_AXES, pairs)


def spread_out(payload):
    spread = lax.all_to_all(
        payload.reshape(2 * PEERS, CAP, 2 * ROWS), ("sheet",) + TILE_AXES, split_axis=0, concat_axis=0, tiled=True
    )
    return spread.reshape(2, SLOTS, 2 * ROWS)


def shards(
    rand_vectors,
    onsite,
    down_hop,
    right_hop,
    pattern,
    pairing,
    link_rows,
    link_target,
    link_weight,
    link_count,
):
    v0 = rand_vectors.reshape(ROWS, SITES_DEV)
    pairing = pairing.reshape(1, SITES_DEV)
    pattern = pattern.T
    left_flag = (3 - lax.axis_index("side") - 2 * lax.axis_index("sheet")).astype(jnp.int32).reshape(1)

    def halo_of(top, below_part, side_part):
        return (
            passed_along(below_part, 1),
            passed_along(top, -1),
            lax.ppermute(side_part, "side", [(0, 1), (1, 0)]),
        )

    made = prepare(
        pattern, left_flag, v0, link_rows, link_target, link_weight, link_count, down_hop, right_hop
    )
    tables, edge_parts, payload = made[:4], made[4:7], made[7]
    hot, _, across, _ = tables
    spread = spread_out(payload)
    halo = halo_of(*edge_parts)
    local_part = local(pattern, v0, onsite, down_hop, right_hop)
    landed, local_part, halo = lax.optimization_barrier((spread, local_part, halo))
    one, x, mom, *edge_parts, payload = first(
        pattern, left_flag, v0, landed, tables, local_part, pairing, halo, down_hop, right_hop
    )
    spread = spread_out(payload)
    halo = halo_of(*edge_parts)
    local_part = local(pattern, x, onsite, down_hop, right_hop)
    landed, local_part, halo = lax.optimization_barrier((spread, local_part, halo))
    two, mom = second(
        pattern, left_flag, v0, one, landed, hot, across, local_part, pairing, mom, halo, down_hop, right_hop
    )
    shape = rand_vectors.shape
    return one.reshape(shape), two.reshape(shape), mom


def solution(mesh):
    both = TILE_AXES + ("sheet", "side")
    mesh = Mesh(mesh.devices.reshape(2, 8, 4, 2, 2, 2), both)
    in_specs = (
        P(None, None, both),
        P(both, None, None),
        P(both, None, None),
        P(both, None, None),
        P(both, None),
        P(both),
        P(both, None),
        P(both, None),
        P(both, None),
        P(both),
    )
    out_specs = (P(None, None, both), P(None, None, both), P(None, None, both))
    return jax.shard_map(shards, mesh=mesh, in_specs=in_specs, out_specs=out_specs, check_vma=False)
```

```python
import jax
import jax.numpy as jnp
from jax import lax
from jax.experimental import pallas as pl
from jax.experimental.pallas import tpu as pltpu
from jax.sharding import Mesh
from jax.sharding import PartitionSpec as P

TILE = 128
TR = 4
TC = 6
ROWS = 64
SITES_DEV = TR * TC * TILE
PEERS = 128
CAP = 8
SLOTS = PEERS * CAP
SPAN = 256
HI = SITES_DEV // SPAN
F32 = jnp.float32
BF16 = jnp.bfloat16
NT = (((1,), (1,)), ((), ()))
NN = (((1,), (0,)), ((), ()))
VMEM_LIMIT = 56 * 1024 * 1024


def dot(a, b, dims=NN):
    return lax.dot_general(a, b, dims, preferred_element_type=F32)


COST = pl.CostEstimate(flops=1000000, bytes_accessed=100000, transcendentals=0)


def params():
    return pltpu.CompilerParams(vmem_limit_bytes=VMEM_LIMIT)


def picked(table):
    spread = jnp.broadcast_to(table[None], (PEERS, CAP, PEERS)).reshape(SLOTS, PEERS)
    own = lax.broadcasted_iota(jnp.int32, (SLOTS, PEERS), 0) // CAP == lax.broadcasted_iota(
        jnp.int32, (SLOTS, PEERS), 1
    )
    return jnp.where(own, spread, 0.0).astype(BF16)


def per_slot(table):
    return dot(picked(table), jnp.ones((PEERS, TILE), BF16))


def build_tables(rows, target, weight, hot_ref, high_ref, across_ref, weight_ref):
    lane = lax.broadcasted_iota(jnp.int32, (SLOTS, SPAN), 1).astype(F32)
    spread_weight = per_slot(weight)
    weight_ref[...] = spread_weight
    wide_weight = jnp.concatenate([spread_weight, spread_weight], axis=1)
    rows_half = lax.broadcasted_iota(jnp.int32, (2 * PEERS, 2 * TILE), 0) < PEERS
    both = (rows_half == (lax.broadcasted_iota(jnp.int32, (2 * PEERS, 2 * TILE), 1) < TILE)).astype(BF16)
    for end, table in ((0, rows), (1, target)):
        coarse = jnp.floor(table * (1.0 / SPAN))
        low = picked(table - coarse * SPAN)
        coarse = picked(coarse)
        wide = dot(jnp.concatenate([low, coarse], axis=1), both)
        low = wide[:, :TILE]
        high_ref[end * SLOTS : (end + 1) * SLOTS, :] = wide[:, TILE:].astype(BF16)
        across_ref[:, end * SLOTS : (end + 1) * SLOTS] = dot(jnp.ones((ROWS, PEERS), BF16), coarse, NT).astype(BF16)
        same = lane == jnp.concatenate([low, low], axis=1)
        hot_ref[2 * end * SLOTS : (2 * end + 1) * SLOTS, :] = jnp.where(same, 1.0, 0.0).astype(BF16)
        if end == 1:
            hot_ref[SLOTS : 2 * SLOTS, :] = jnp.where(same, wide_weight, 0.0).astype(BF16)


def gather_ends(parts, hot_ref, high_ref, start, chunk):
    lane = lax.broadcasted_iota(jnp.int32, (chunk, TILE), 1)
    half = (lane >= ROWS).astype(F32)
    ends = []
    for end in range(2):
        hot = hot_ref[2 * end * SLOTS + start : 2 * end * SLOTS + start + chunk, :]
        high = high_ref[end * SLOTS + start : end * SLOTS + start + chunk, :].astype(F32) - half
        total = jnp.zeros((chunk, TILE), F32)
        for q in range(HI // 4):
            found = dot(hot, jnp.concatenate(parts[4 * q : 4 * q + 4], axis=0), NT)
            total = jnp.where(high == 4.0 * q, found[:, :TILE], total)
            total = jnp.where(high == 4.0 * q + 2.0, found[:, TILE:], total)
        ends.append(total + pltpu.roll(total, ROWS, 1))
    return jnp.where(lane < ROWS, ends[0], ends[1])


def as_payload(ends, weight):
    field = ends.astype(BF16)
    lane = lax.broadcasted_iota(jnp.int32, ends.shape, 1)
    return jnp.where(lane < ROWS, field.astype(F32), field.astype(F32) * weight).astype(BF16)


CHUNK = 512


def gather_payload(x_ref, hot_ref, high_ref, weight_ref, out_ref):
    parts = [x_ref[:, h * SPAN : (h + 1) * SPAN] for h in range(HI)]
    for start in range(0, SLOTS, CHUNK):
        ends = gather_ends(parts, hot_ref, high_ref, start, CHUNK)
        payload = as_payload(ends, weight_ref[start : start + CHUNK, :])
        out_ref[0, start : start + CHUNK, :] = payload
        out_ref[1, start : start + CHUNK, :] = payload


TABLE_SHAPES = (
    pltpu.VMEM((3 * SLOTS, SPAN), BF16),
    pltpu.VMEM((2 * SLOTS, TILE), BF16),
    pltpu.VMEM((ROWS, 2 * SLOTS), BF16),
    jax.ShapeDtypeStruct((SLOTS, TILE), F32),
)


def write_edges(pattern_ref, left_ref, x_ref, down_ref, right_ref, down_base, top_ref, below_ref, side_ref):
    top_ref[...] = x_ref[:, : TC * TILE]
    for k in range(TC):
        tile = (TR - 1) * TC + k
        keep = pattern_ref[0, tile].astype(F32)
        product = keep * dot(x_ref[:, tile * TILE : (tile + 1) * TILE], down_ref[down_base + k])
        below_ref[:, k * TILE : (k + 1) * TILE] = product.astype(BF16)
    is_left = (left_ref[0] & 1) == 1
    for r in range(TR):
        last = r * TC + TC - 1
        keep = pattern_ref[1, last].astype(F32)
        product = keep * dot(x_ref[:, last * TILE : (last + 1) * TILE], right_ref[r, 0])
        first_tile = x_ref[:, r * TC * TILE : (r * TC + 1) * TILE]
        side_ref[:, r * TILE : (r + 1) * TILE] = jnp.where(is_left, product.astype(BF16), first_tile)


EDGE_SHAPES = (
    jax.ShapeDtypeStruct((ROWS, TC * TILE), BF16),
    jax.ShapeDtypeStruct((ROWS, TC * TILE), BF16),
    jax.ShapeDtypeStruct((ROWS, TR * TILE), BF16),
)
SMEM = pl.BlockSpec(memory_space=pltpu.SMEM)
VMEM = pl.BlockSpec(memory_space=pltpu.VMEM)
DOWN_EDGE = pl.BlockSpec((TC, TILE, TILE), lambda i: (TR - 1, 0, 0))
RIGHT_EDGE = pl.BlockSpec((TR, 1, TILE, TILE), lambda i: (0, TC - 1, 0, 0))


def whole(shape):
    return pl.BlockSpec(shape, lambda i: (0,) * len(shape))


def on_core(value):
    return pltpu.with_memory_space_constraint(value, pltpu.VMEM)


def prepare_kernel(
    pattern_ref, left_ref, x_ref, rows_ref, target_ref, weight_ref, count_ref, down_ref, right_ref,
    hot_ref, high_ref, across_ref, spread_ref, top_ref, below_ref, side_ref, out_ref,
):
    live = lax.broadcasted_iota(jnp.int32, (CAP, PEERS), 0) < count_ref[...]
    weight = jnp.where(live, weight_ref[...].astype(F32), 0.0)
    build_tables(
        rows_ref[...].astype(F32), target_ref[...].astype(F32), weight, hot_ref, high_ref, across_ref, spread_ref
    )
    gather_payload(x_ref, hot_ref, high_ref, spread_ref, out_ref)
    write_edges(pattern_ref, left_ref, x_ref, down_ref, right_ref, 0, top_ref, below_ref, side_ref)


def prepare(pattern, left_flag, x, link_rows, link_target, link_weight, link_count, down_hop, right_hop):
    arrays = (x, link_rows.T, link_target.T, link_weight.T, link_count.reshape(1, PEERS))
    shapes = TABLE_SHAPES + EDGE_SHAPES + (jax.ShapeDtypeStruct((2, SLOTS, 2 * ROWS), BF16),)
    resident = len(TABLE_SHAPES) - 1
    return pl.pallas_call(
        prepare_kernel,
        grid=(1,),
        in_specs=[SMEM, SMEM] + [whole(a.shape) for a in arrays] + [DOWN_EDGE, RIGHT_EDGE],
        out_specs=(VMEM,) * resident + tuple(whole(s.shape) for s in shapes[resident:]),
        out_shape=shapes,
        compiler_params=params(),
        cost_estimate=COST,
        name="prepare",
    )(pattern, left_flag, *arrays, down_hop, right_hop.reshape(TR, TC, TILE, TILE))


def kept(pattern_ref, which, tile, value):
    return jnp.where(pattern_ref[which, tile] == 1, value, jnp.zeros_like(value))


def local_tile(pattern_ref, x_ref, onsite_ref, down_ref, right_ref, tile):
    def block(other):
        return x_ref[:, other * TILE : (other + 1) * TILE]

    r, k = divmod(tile, TC)
    fields = [block(tile)]
    tiles = [onsite_ref[tile]]
    if r > 0:
        fields.append(kept(pattern_ref, 0, tile - TC, block(tile - TC)))
        tiles.append(down_ref[tile - TC])
    if k > 0:
        fields.append(kept(pattern_ref, 1, tile - 1, block(tile - 1)))
        tiles.append(right_ref[tile - 1])
    total = dot(jnp.concatenate(fields, axis=1), jnp.concatenate(tiles, axis=0))
    fields = []
    tiles = []
    if r < TR - 1:
        fields.append(kept(pattern_ref, 0, tile, block(tile + TC)))
        tiles.append(down_ref[tile])
    if k < TC - 1:
        fields.append(kept(pattern_ref, 1, tile, block(tile + 1)))
        tiles.append(right_ref[tile])
    if fields:
        total = total + dot(jnp.concatenate(fields, axis=1), jnp.concatenate(tiles, axis=1), NT)
    return total


def halo_tile(pattern_ref, is_left, down_edge, right_edge, above_ref, below_ref, side_ref, tile):
    r, k = divmod(tile, TC)
    total = None

    def plus(value):
        return value if total is None else total + value

    if r == 0:
        total = plus(above_ref[:, k * TILE : (k + 1) * TILE].astype(F32))
    if r == TR - 1:
        lower = below_ref[:, k * TILE : (k + 1) * TILE]
        total = plus(dot(kept(pattern_ref, 0, tile, lower), down_edge(k), NT))
    if k == 0:
        total = plus(jnp.where(is_left, 0.0, side_ref[:, r * TILE : (r + 1) * TILE].astype(F32)))
    if k == TC - 1:
        righter = side_ref[:, r * TILE : (r + 1) * TILE]
        righter = jnp.where(is_left, righter, jnp.zeros_like(righter))
        total = plus(dot(kept(pattern_ref, 1, tile, righter), right_edge(r), NT))
    return total


def signed(value):
    return jnp.where(lax.broadcasted_iota(jnp.int32, value.shape, 0) < ROWS // 2, value, -value)


def swapped(value):
    return jnp.concatenate([value[ROWS // 2 :], value[: ROWS // 2]], axis=0)


def vector_mean(value):
    comps = value.reshape(4, 16, value.shape[-1])
    return jnp.sum(comps, axis=1) * (1.0 / 16.0)


SCATTER_SCRATCH = [pltpu.VMEM((HI * ROWS, 2 * SLOTS), BF16), pltpu.VMEM((HI * ROWS, SPAN), F32)]


def scatter_into(landed, hot_ref, across_ref, mask_ref, total_ref):
    turned = landed.T
    ends = jnp.concatenate([turned[ROWS:], turned[:ROWS]], axis=1)
    zero = jnp.zeros_like(ends)
    for h in range(HI):
        mask_ref[h * ROWS : (h + 1) * ROWS, :] = jnp.where(across_ref[...] == BF16(h), ends, zero)
    group = 1
    for start in range(0, HI, group):
        total_ref[start * ROWS : (start + group) * ROWS, :] = dot(
            mask_ref[start * ROWS : (start + group) * ROWS, :], hot_ref[0 : 2 * SLOTS, :]
        )


def whole_hop(pattern_ref, left_ref, local_ref, total_ref, above_ref, below_ref, side_ref, down_ref, right_ref, tile):
    h, part = divmod(tile, SPAN // TILE)
    hop = local_ref[:, tile * TILE : (tile + 1) * TILE]
    hop = hop + total_ref[h * ROWS : (h + 1) * ROWS, part * TILE : (part + 1) * TILE]
    halo = halo_tile(
        pattern_ref, (left_ref[0] & 1) == 1, lambda k: down_ref[k], lambda r: right_ref[r, 0],
        above_ref, below_ref, side_ref, tile,
    )
    return hop if halo is None else hop + halo


def first_kernel(
    pattern_ref, left_ref, landed_ref, above_ref, below_ref, side_ref, hot_ref, high_ref, across_ref,
    v0_ref, local_ref, weight_ref, pairing_ref, down_ref, right_ref,
    one_ref, x_ref, mom_ref, top_ref, lower_ref, beside_ref, out_ref, mask_ref, total_ref,
):
    scatter_into(landed_ref[left_ref[0] >> 1], hot_ref, across_ref, mask_ref, total_ref)
    for tile in range(TR * TC):
        cols = slice(tile * TILE, (tile + 1) * TILE)
        hop = whole_hop(
            pattern_ref, left_ref, local_ref, total_ref, above_ref, below_ref, side_ref, down_ref, right_ref, tile
        )
        v0 = v0_ref[:, cols].astype(F32)
        one = signed(hop) + pairing_ref[:, cols] * swapped(v0)
        one_ref[:, cols] = one
        x_ref[:, cols] = one.astype(BF16)
        mom_ref[0, :, cols] = vector_mean(v0 * v0)
        mom_ref[1, :, cols] = vector_mean(v0 * one)
    gather_payload(x_ref, hot_ref, high_ref, weight_ref, out_ref)
    write_edges(pattern_ref, left_ref, x_ref, down_ref, right_ref, 0, top_ref, lower_ref, beside_ref)


def first(pattern, left_flag, v0, landed, tables, local_part, pairing, halo, down_hop, right_hop):
    shapes = (
        jax.ShapeDtypeStruct((ROWS, SITES_DEV), F32),
        jax.ShapeDtypeStruct((ROWS, SITES_DEV), BF16),
        jax.ShapeDtypeStruct((2, 4, SITES_DEV), F32),
    ) + EDGE_SHAPES + (jax.ShapeDtypeStruct((2, SLOTS, 2 * ROWS), BF16),)
    hot, high, across, weight = tables
    resident = [on_core(a) for a in (landed, *halo, hot, high, across)]
    arrays = (v0, local_part, weight, pairing)
    return pl.pallas_call(
        first_kernel,
        grid=(1,),
        in_specs=[SMEM, SMEM] + [VMEM] * len(resident) + [whole(a.shape) for a in arrays] + [DOWN_EDGE, RIGHT_EDGE],
        out_specs=tuple(whole(s.shape) for s in shapes),
        out_shape=shapes,
        scratch_shapes=SCATTER_SCRATCH,
        compiler_params=params(),
        cost_estimate=COST,
        name="first",
    )(pattern, left_flag, *resident, *arrays, down_hop, right_hop.reshape(TR, TC, TILE, TILE))


def local_kernel(pattern_ref, x_ref, onsite_ref, down_ref, right_ref, out_ref):
    for tile in range(TR * TC):
        out_ref[:, tile * TILE : (tile + 1) * TILE] = local_tile(
            pattern_ref, x_ref, onsite_ref, down_ref, right_ref, tile
        )


def local(pattern, x, onsite, down_hop, right_hop):
    return pl.pallas_call(
        local_kernel,
        in_specs=[SMEM] + [VMEM] * 4,
        out_shape=jax.ShapeDtypeStruct((ROWS, SITES_DEV), F32),
        compiler_params=params(),
        cost_estimate=COST,
        name="local",
    )(pattern, x, onsite, down_hop, right_hop)


def second_kernel(
    pattern_ref, left_ref, landed_ref, above_ref, below_ref, side_ref, hot_ref, across_ref,
    v0_ref, one_ref, local_ref, pairing_ref, mom_in_ref, down_ref, right_ref,
    two_ref, mom_ref, mask_ref, total_ref,
):
    scatter_into(landed_ref[left_ref[0] >> 1], hot_ref, across_ref, mask_ref, total_ref)
    mom_ref[0:2] = mom_in_ref[...]
    for tile in range(TR * TC):
        cols = slice(tile * TILE, (tile + 1) * TILE)
        hop = whole_hop(
            pattern_ref, left_ref, local_ref, total_ref, above_ref, below_ref, side_ref, down_ref, right_ref, tile
        )
        v0 = v0_ref[:, cols].astype(F32)
        two = 2.0 * (signed(hop) + pairing_ref[:, cols] * swapped(one_ref[:, cols])) - v0
        two_ref[:, cols] = two
        mom_ref[2, :, cols] = vector_mean(v0 * two)


def second(pattern, left_flag, v0, one, landed, hot, across, local_part, pairing, mom, halo, down_hop, right_hop):
    shapes = (
        jax.ShapeDtypeStruct((ROWS, SITES_DEV), F32),
        jax.ShapeDtypeStruct((3, 4, SITES_DEV), F32),
    )
    resident = [on_core(a) for a in (landed, *halo, hot, across)]
    arrays = (v0, one, local_part, pairing, mom)
    return pl.pallas_call(
        second_kernel,
        grid=(1,),
        in_specs=[SMEM, SMEM] + [VMEM] * len(resident) + [whole(a.shape) for a in arrays] + [DOWN_EDGE, RIGHT_EDGE],
        out_specs=tuple(whole(s.shape) for s in shapes),
        out_shape=shapes,
        scratch_shapes=SCATTER_SCRATCH,
        compiler_params=params(),
        cost_estimate=COST,
        name="second",
    )(pattern, left_flag, *resident, *arrays, down_hop, right_hop.reshape(TR, TC, TILE, TILE))


TILE_AXES = ("z_low", "y", "x", "core")


def passed_along(value, by):
    length = PEERS
    pairs = [(i, i + by) for i in range(length) if 0 <= i + by < length]
    return lax.ppermute(value, TILE_AXES, pairs)


def spread_out(payload):
    spread = lax.all_to_all(
        payload.reshape(2 * PEERS, CAP, 2 * ROWS), ("sheet",) + TILE_AXES, split_axis=0, concat_axis=0, tiled=True
    )
    return spread.reshape(2, SLOTS, 2 * ROWS)


def shards(
    rand_vectors,
    onsite,
    down_hop,
    right_hop,
    pattern,
    pairing,
    link_rows,
    link_target,
    link_weight,
    link_count,
):
    v0 = rand_vectors.reshape(ROWS, SITES_DEV)
    pairing = pairing.reshape(1, SITES_DEV)
    pattern = pattern.T
    left_flag = (3 - lax.axis_index("side") - 2 * lax.axis_index("sheet")).astype(jnp.int32).reshape(1)

    def halo_of(top, below_part, side_part):
        return (
            passed_along(below_part, 1),
            passed_along(top, -1),
            lax.ppermute(side_part, "side", [(0, 1), (1, 0)]),
        )

    made = prepare(
        pattern, left_flag, v0, link_rows, link_target, link_weight, link_count, down_hop, right_hop
    )
    tables, edge_parts, payload = made[:4], made[4:7], made[7]
    hot, _, across, _ = tables
    spread = spread_out(payload)
    halo = halo_of(*edge_parts)
    local_part = local(pattern, v0, onsite, down_hop, right_hop)
    landed, local_part, halo = lax.optimization_barrier((spread, local_part, halo))
    one, x, mom, *edge_parts, payload = first(
        pattern, left_flag, v0, landed, tables, local_part, pairing, halo, down_hop, right_hop
    )
    spread = spread_out(payload)
    halo = halo_of(*edge_parts)
    local_part = local(pattern, x, onsite, down_hop, right_hop)
    landed, local_part, halo = lax.optimization_barrier((spread, local_part, halo))
    two, mom = second(
        pattern, left_flag, v0, one, landed, hot, across, local_part, pairing, mom, halo, down_hop, right_hop
    )
    shape = rand_vectors.shape
    return one.reshape(shape), two.reshape(shape), mom


def solution(mesh):
    both = TILE_AXES + ("sheet", "side")
    mesh = Mesh(mesh.devices.reshape(2, 8, 4, 2, 2, 2), both)
    in_specs = (
        P(None, None, both),
        P(both, None, None),
        P(both, None, None),
        P(both, None, None),
        P(both, None),
        P(both),
        P(both, None),
        P(both, None),
        P(both, None),
        P(both),
    )
    out_specs = (P(None, None, both), P(None, None, both), P(None, None, both))
    return jax.shard_map(shards, mesh=mesh, in_specs=in_specs, out_specs=out_specs, check_vma=False)
```
